32 devices in a mesh: dp: 8 (over z, core), fsdp: 4 (over y, x).
Axes of the slice: x: 2, y: 2, z: 4, core: 2. Of those that a mesh axis runs over, the one named last changes fastest.
Arguments:
- act: bfloat16 [8, 16, 512, 768], P('dp', None, 'fsdp'), may hold values from -6 to 6
- single: float32 [8, 512, 384], P('dp', 'fsdp'), may hold values from -6 to 6
- pair: bfloat16 [8, 512, 512, 128], P('dp', 'fsdp'), may hold values from -6 to 6
- segment: int32 [8, 512], P('dp', 'fsdp'), may hold values from 0 to 64, as said below
- padding: int32 [8, 512], P('dp', 'fsdp'), may hold values from 0 to 1, as said below
- cotangent: bfloat16 [8, 16, 512, 768], P('dp', None, 'fsdp'), may hold values from -6 to 6
- gain_s1: bfloat16 [384], P('fsdp'), may hold values from 0.099609375 to 1.8984375
- w_cond1: bfloat16 [384, 2304], P('fsdp'), may hold values from -0.3125 to 0.3125
- b_cond1: bfloat16 [2304], P('fsdp'), may hold values from -4 to 4
- query_key_value_gate_weight: bfloat16 [768, 3072], P('fsdp'), may hold values from -0.21875 to 0.21875
- b_q: bfloat16 [768], P('fsdp'), may hold values from -3 to 3
- gain_z: bfloat16 [128], P('fsdp'), may hold values from 0.099609375 to 1.8984375
- w_pair: bfloat16 [128, 16], P('fsdp'), may hold values from -0.5 to 0.5
- attention_output_weight: bfloat16 [768, 768], P('fsdp'), may hold values from -2.5 to 2.5
- gain_s2: bfloat16 [384], P('fsdp'), may hold values from 0.099609375 to 1.8984375
- w_cond2: bfloat16 [384, 2304], P('fsdp'), may hold values from -0.3125 to 0.3125
- b_cond2: bfloat16 [2304], P('fsdp'), may hold values from -4 to 4
- gate_up_weight: bfloat16 [768, 3072], P('fsdp'), may hold values from -0.21875 to 0.21875
- down_weight: bfloat16 [1536, 768], P('fsdp'), may hold values from -0.21875 to 0.21875
Outputs:
- block_out: bfloat16 [8, 16, 512, 768], P('dp', None, 'fsdp')
- act_grad: bfloat16 [8, 16, 512, 768], P('dp', None, 'fsdp')
- single_grad: float32 [8, 512, 384], P('dp', 'fsdp')
- pair_grad: bfloat16 [8, 512, 512, 128], P('dp', 'fsdp')
- grad_gain_s1: float32 [384], P('fsdp')
- grad_w_cond1: float32 [384, 2304], P('fsdp')
- grad_b_cond1: float32 [2304], P('fsdp')
- grad_w_qkvg: float32 [768, 3072], P('fsdp')
- grad_b_q: float32 [768], P('fsdp')
- grad_gain_z: float32 [128], P('fsdp')
- grad_w_pair: float32 [128, 16], P('fsdp')
- grad_w_o: float32 [768, 768], P('fsdp')
- grad_gain_s2: float32 [384], P('fsdp')
- grad_w_cond2: float32 [384, 2304], P('fsdp')
- grad_b_cond2: float32 [2304], P('fsdp')
- grad_w_ab: float32 [768, 3072], P('fsdp')
- grad_w_out: float32 [1536, 768], P('fsdp')
The draws below stay inside these ranges and needn't reach their ends.
Inputs may be any that keep to these rules, and one draw needn't show every extreme that they name: Numbers start at 0 in each crop, never fall, and rise by one where a new segment begins; new segments begin only among tokens 5 * 64 to 383 of a crop, so the first 320 tokens lie in segment 0; padded tokens carry the number of the crop's last unpadded token. `padding`: 1 on a tail of 1 to 128 tokens at the end of each crop, 0 elsewhere.
All inputs are finite; a program needn't handle non-finite values.
Results may differ from the reference program's by a relative error of at most 0.02.
The reference program's roundings to bfloat16 on the way count: a program that leaves them out, or rounds other values in their place, can miss the bound.
Values may be sent and summed in bfloat16 or wider, within the bound.
No kernel may reach another device: no remote copies, remote signals or barrier semaphores. Data moves between devices by JAX's collectives and lax.ppermute only.
A program may use at most 512 MiB of HBM per device.

```python
import jax
import jax.numpy as jnp
from jax import lax

D = 768
HEADS = 16
HEAD = 48
PAIR = 128
COND = 384
FF = 1536
SAMPLES = 16
LEN = 512
CROPS = 8


def crop_layout(key):
    drawn_tail = jax.random.randint(jax.random.fold_in(key, 11), (CROPS, 1), 1, LEN // 4 + 1)
    crop_ids = jnp.arange(CROPS, dtype=jnp.int32)[:, None]
    tail_len = jnp.where(crop_ids == 0, LEN // 4, drawn_tail).astype(jnp.int32)
    lottery = jax.random.randint(jax.random.fold_in(key, 12), (CROPS, LEN), 0, 16)
    places = jnp.arange(LEN, dtype=jnp.int32)[None, :]
    region = (places >= 5 * LEN // 8) & (places < 3 * LEN // 4)
    starts = region & ((lottery == 0) | (crop_ids == 0))
    numbers = jnp.cumsum(starts.astype(jnp.int32), axis=1).astype(jnp.int32)
    pad_flags = (places >= LEN - tail_len).astype(jnp.int32)
    return (numbers, pad_flags)


def draw_segment(key, part):
    return crop_layout(key)[0]


def draw_padding(key, part):
    return crop_layout(key)[1]


def steps_of(stream_key, dims, shards, least, top_value):
    gain = 1.0
    for dim, blocks in shards:
        steps = jax.random.uniform(jax.random.fold_in(jax.random.fold_in(stream_key, 6), dim), (blocks,), jnp.float32, least / len(shards), top_value / len(shards))
        gain = gain * jnp.repeat(jnp.exp(steps), dims[dim] // blocks).reshape((-1,) + (1,) * (len(dims) - 1 - dim))
    return gain


def noise(stream_key, extent, scale, bound, split=(), kind=jnp.bfloat16):
    array = jax.random.normal(stream_key, extent, jnp.float32) * scale
    if len(split) > 0:
        array = steps_of(stream_key, extent, split, -0.22, 0.18) * array
    return jnp.clip(array, min=-bound, max=bound).astype(kind)


def setup_inputs(seed: int = 0) -> dict:
    key_list = jax.random.split(jax.random.key(seed), 20)
    return {
        "act": noise(key_list[0], (CROPS, SAMPLES, LEN, D), 1.0, 6.0, ((0, 8), (2, 4))),
        "single": noise(key_list[1], (CROPS, LEN, COND), 1.0, 6.0, ((0, 8), (1, 4)), jnp.float32),
        "pair": noise(key_list[2], (CROPS, LEN, LEN, PAIR), 1.0, 6.0, ((0, 8), (1, 4))),
        "segment": draw_segment(jax.random.fold_in(key_list[19], 71), 0),
        "padding": draw_padding(jax.random.fold_in(key_list[19], 71), 0),
        "cotangent": noise(key_list[5], (CROPS, SAMPLES, LEN, D), 1.0, 6.0, ((0, 8), (2, 4))),
        "gain_s1": jnp.clip(1.0 + 0.18 * jax.random.normal(key_list[6], (COND,), jnp.float32), 0.099609375, 1.8984375).astype(jnp.bfloat16),
        "w_cond1": noise(key_list[7], (COND, 3 * D), COND ** -0.5, 0.3125, ((0, 4),)),
        "b_cond1": noise(key_list[8], (3 * D,), 1.0, 4.0, ((0, 4),)),
        "query_key_value_gate_weight": noise(key_list[9], (D, 4 * D), D ** -0.5, 0.21875, ((0, 4),)),
        "b_q": noise(key_list[10], (D,), 0.5, 3.0, ((0, 4),)),
        "gain_z": jnp.clip(1.0 + 0.18 * jax.random.normal(key_list[11], (PAIR,), jnp.float32), 0.099609375, 1.8984375).astype(jnp.bfloat16),
        "w_pair": noise(key_list[12], (PAIR, HEADS), PAIR ** -0.5, 0.5, ((0, 4),)),
        "attention_output_weight": noise(key_list[13], (D, D), (max(D // 128, 1)) ** -0.5, 2.5, ((0, 4),)),
        "gain_s2": jnp.clip(1.0 + 0.18 * jax.random.normal(key_list[14], (COND,), jnp.float32), 0.099609375, 1.8984375).astype(jnp.bfloat16),
        "w_cond2": noise(key_list[15], (COND, 3 * D), COND ** -0.5, 0.3125, ((0, 4),)),
        "b_cond2": noise(key_list[16], (3 * D,), 1.0, 4.0, ((0, 4),)),
        "gate_up_weight": noise(key_list[17], (D, 2 * FF), D ** -0.5, 0.21875, ((0, 4),)),
        "down_weight": noise(key_list[18], (FF, D), (FF // 2) ** -0.5, 0.21875, ((0, 4),)),
    }


EPS = 1e-05
EXACT_MATMUL = lax.Precision.HIGHEST

@jax.custom_vjp
def low(v):
    return lax.optimization_barrier(v.astype(jnp.bfloat16)).astype(jnp.float32)

@jax.custom_vjp
def reduced_backward(v):
    return v

def low_keep(v):
    return (low(v), None)

def low_pass(kept, grad):
    return (grad,)

def back_keep(v):
    return (v, None)

def back_low(kept, grad):
    return (low(grad),)
low.defvjp(low_keep, low_pass)
reduced_backward.defvjp(back_keep, back_low)

def norm_rows(values):
    average = lax.optimization_barrier(jnp.mean(values, axis=-1, keepdims=True))
    centred = values - average
    return centred * lax.rsqrt(lax.optimization_barrier(jnp.mean(centred * centred, axis=-1, keepdims=True)) + EPS)

def crop_forward(act_in, single_in, pair_in, params, seg_crop, tag_crop):
    gain_s1, w_cond1, b_cond1, query_key_value_gate_weight, b_q, gain_z, w_pair, attention_output_weight, gain_s2, w_cond2, b_cond2, gate_up_weight, down_weight = params
    single_n = norm_rows(single_in)
    single_first = low(single_n * gain_s1)
    cond_one = reduced_backward(jnp.dot(single_first, w_cond1, precision=EXACT_MATMUL)) + b_cond1
    input_first = low(jax.nn.sigmoid(cond_one[:, :D]) * norm_rows(act_in) + cond_one[:, D:2 * D])
    apply_projection = reduced_backward(jnp.einsum('itk,kh->ith', input_first, query_key_value_gate_weight, precision=EXACT_MATMUL))
    query_low = low(apply_projection[..., :D] + b_q).reshape(SAMPLES, LEN, HEADS, HEAD)
    keys_low = low(apply_projection[..., D:2 * D]).reshape(SAMPLES, LEN, HEADS, HEAD)
    values_low = low(apply_projection[..., 2 * D:3 * D]).reshape(SAMPLES, LEN, HEADS, HEAD)
    gate_attn = jax.nn.sigmoid(apply_projection[..., 3 * D:])
    pair_low = low(norm_rows(pair_in) * gain_z)
    pair_bias = reduced_backward(jnp.einsum('ijp,ph->hij', pair_low, w_pair, precision=EXACT_MATMUL))
    raw_scores = jnp.einsum('sihe,sjhe->shij', query_low, keys_low, precision=EXACT_MATMUL) * HEAD ** (-0.5) + pair_bias[None]
    allowed = seg_crop[:, None] == tag_crop[None, :]
    scores = reduced_backward(jnp.where(allowed[None, None], raw_scores, -1000000000.0))
    row_peak = lax.optimization_barrier(jnp.max(scores, axis=-1, keepdims=True))
    expo_vals = jnp.exp(scores - row_peak)
    attn_probs = expo_vals / lax.optimization_barrier(jnp.sum(expo_vals, axis=-1, keepdims=True))
    attn_mix = reduced_backward(jnp.einsum('shij,sjhe->sihe', low(attn_probs), values_low, precision=EXACT_MATMUL)).reshape(SAMPLES, LEN, D)
    branch_input = low(gate_attn * attn_mix)
    attention_result = reduced_backward(jnp.einsum('itk,kh->ith', branch_input, attention_output_weight, precision=EXACT_MATMUL))
    middle = act_in + jax.nn.sigmoid(cond_one[:, 2 * D:]) * attention_result
    single_second = low(single_n * gain_s2)
    cond_two = reduced_backward(jnp.dot(single_second, w_cond2, precision=EXACT_MATMUL)) + b_cond2
    input_second = low(jax.nn.sigmoid(cond_two[:, :D]) * norm_rows(middle) + cond_two[:, D:2 * D])
    gate_and_up = reduced_backward(jnp.einsum('itk,kh->ith', input_second, gate_up_weight, precision=EXACT_MATMUL))
    hidden_units = low(jax.nn.silu(gate_and_up[..., :FF]) * gate_and_up[..., FF:])
    feedforward_result = reduced_backward(jnp.einsum('hgn,nc->hgc', hidden_units, down_weight, precision=EXACT_MATMUL))
    return middle + jax.nn.sigmoid(cond_two[:, 2 * D:]) * feedforward_result

def reference(act, single, pair, segment, padding, cotangent, gain_s1, w_cond1, b_cond1, query_key_value_gate_weight, b_q, gain_z, w_pair, attention_output_weight, gain_s2, w_cond2, b_cond2, gate_up_weight, down_weight):
    params = tuple((weight.astype(jnp.float32) for weight in (gain_s1, w_cond1, b_cond1, query_key_value_gate_weight, b_q, gain_z, w_pair, attention_output_weight, gain_s2, w_cond2, b_cond2, gate_up_weight, down_weight)))
    key_tag = jnp.where(padding == 1, -1, segment).astype(jnp.int32)

    def one_crop(summed, crop_data):
        act_c, single_c, pair_c, seg_c, tag_c, cot_c = crop_data

        def forward(act_in, single_in, pair_in, weights):
            return crop_forward(act_in, single_in, pair_in, weights, seg_c, tag_c)
        result, pullback = jax.vjp(forward, act_c.astype(jnp.float32), single_c, pair_c.astype(jnp.float32), params)
        act_g, single_g, pair_g, weight_grads = pullback(cot_c.astype(jnp.float32))
        summed = tuple((before + update for before, update in zip(summed, weight_grads)))
        return (summed, (result.astype(jnp.bfloat16), act_g.astype(jnp.bfloat16), single_g, pair_g.astype(jnp.bfloat16)))
    starting = tuple((jnp.zeros(weight.shape, jnp.float32) for weight in params))
    totals, (block_out, act_grad, single_grad, pair_grad) = lax.scan(one_crop, starting, (act, single, pair, segment, key_tag, cotangent))
    return (block_out, act_grad, single_grad, pair_grad, totals[0], totals[1], totals[2], totals[3], totals[4], totals[5], totals[6], totals[7], totals[8], totals[9], totals[10], totals[11], totals[12])
```

```python
import functools

import jax
import jax.numpy as jnp
from jax import lax
from jax.experimental import pallas as pl
from jax.experimental.pallas import tpu as pltpu
from jax.sharding import PartitionSpec as P

HEADS = 16
HEAD = 48
FF = 1536
EPS = 1e-05
LOG2E = 1.4426950408889634
NEG = -1000000000.0
f32 = jnp.float32
bf16 = jnp.bfloat16
NT = (((1,), (1,)), ((), ()))
NN = (((1,), (0,)), ((), ()))
TN = (((0,), (0,)), ((), ()))


def norm_stats(values):
    average = jnp.mean(values, axis=-1, keepdims=True)
    centred = values - average
    inverse = lax.rsqrt(jnp.mean(centred * centred, axis=-1, keepdims=True) + EPS)
    return (centred * inverse, inverse)


def norm_back(normed, inverse, incoming):
    return inverse * (
        incoming
        - jnp.mean(incoming, axis=-1, keepdims=True)
        - normed * jnp.mean(incoming * normed, axis=-1, keepdims=True)
    )


def sig_slope(values):
    sigma_val = jax.nn.sigmoid(values)
    return sigma_val * (1.0 - sigma_val)


def dg(a, b, dims):
    return lax.dot_general(a, b, dims, preferred_element_type=f32)


def head_window(h, D):
    tile = jnp.minimum((h * HEAD) // 128, D // 128 - 2)
    return pl.multiple_of(tile * 128, 128), h * HEAD - tile * 128


def masked_bias(F, ids, seg_ref, tag_ref, parts, bm):
    for p in range(F):
        R = parts[p].shape[1]
        row = pl.multiple_of(ids[F + 2 + p] * R, 16)
        bm[pl.ds(row, R), :] = jnp.where(
            seg_ref[pl.ds(row, R), :] == tag_ref[...], parts[p][0].astype(f32) * LOG2E, -jnp.inf
        )


def head_scores(q, k, bm):
    s = dg(q, k, NT)
    return jnp.where(bm > -jnp.inf, s * (HEAD**-0.5 * LOG2E) + bm, NEG * LOG2E)


def attn_fwd_kernel(F, RB, ids, seg_ref, tag_ref, q_ref, k_ref, v_ref, *refs):
    parts = refs[:F]
    o_ref, lse_ref, bm = refs[F:]
    Sl, T, D = q_ref.shape
    h = pl.program_id(0)

    @pl.when(h == 0)
    def _():
        o_ref[...] = jnp.zeros_like(o_ref)
        lse_ref[...] = jnp.zeros_like(lse_ref)

    start, off = head_window(h, D)
    masked_bias(F, ids, seg_ref, tag_ref, parts, bm)
    lane = lax.broadcasted_iota(jnp.int32, (1, 256), 1)
    mine = (lane >= off) & (lane < off + HEAD)
    column = lax.broadcasted_iota(jnp.int32, (1, 128), 1) == h
    win = pl.ds(start, 256)

    def sample(s, _):
        kw = k_ref[s, :, win]
        vw = v_ref[s, :, win]
        vw = jnp.where(mine, vw, jnp.zeros_like(vw))
        for r in range(0, T, RB):
            rows = pl.ds(r, RB)
            qw = q_ref[s, rows, win]
            sc = head_scores(jnp.where(mine, qw, jnp.zeros_like(qw)), kw, bm[rows, :])
            m = jnp.max(sc, axis=-1, keepdims=True)
            p = jnp.exp2(sc - m)
            l = jnp.sum(p, axis=-1, keepdims=True)
            o_ref[s, rows, win] += dg(p.astype(bf16), vw, NN) * (1.0 / l)
            lse_ref[s, rows, :] = jnp.where(column, m + jnp.log2(l), lse_ref[s, rows, :])
        return 0

    lax.fori_loop(0, Sl, sample, 0)


def resident(a, single=True):
    return pl.BlockSpec(
        a.shape, lambda h, s: (0,) * len(a.shape), pipeline_mode=pl.Buffered(1) if single else None
    )


def attn_fwd(ids, seg, tag, q, k, v, parts):
    Sl, T, D = q.shape
    F = len(parts)
    H, R = parts[0].shape[:2]
    part = pl.BlockSpec((1, R, T), lambda h, s: (h, 0, 0))
    outs = [jax.ShapeDtypeStruct((Sl, T, D), f32), jax.ShapeDtypeStruct((Sl, T, 128), f32)]
    return pl.pallas_call(
        functools.partial(attn_fwd_kernel, F, min(T, 256)),
        grid_spec=pltpu.PrefetchScalarGridSpec(
            num_scalar_prefetch=1,
            grid=(H,),
            in_specs=[resident(x) for x in (seg, tag, q, k, v)] + [part] * F,
            out_specs=[resident(x) for x in outs],
            scratch_shapes=[pltpu.VMEM((T, T), f32)],
        ),
        out_shape=outs,
        compiler_params=pltpu.CompilerParams(
            dimension_semantics=("arbitrary",), vmem_limit_bytes=60 << 20
        ),
        cost_estimate=cost(Sl * H * T * T * 1024, Sl * T * D * 10 + H * T * T * 2, Sl * H * T * T),
        name="attn_fwd",
    )(ids, seg, tag, q, k, v, *parts)


def attn_bwd_kernel(F, RB, ids, seg_ref, tag_ref, q_ref, k_ref, v_ref, do_ref, lse_ref, *refs):
    parts = refs[:F]
    dq_ref, dk_ref, dv_ref = refs[F : F + 3]
    db_refs = refs[F + 3 : F + 3 + F]
    bm, dbacc, pb, dsb, qt, dot, dkt, dvt = refs[F + 3 + F :]
    Sl, T, D = q_ref.shape
    h = pl.program_id(0)

    @pl.when(h == 0)
    def _():
        dq_ref[...] = jnp.zeros_like(dq_ref)

        def turn(s, _):
            qt[s] = q_ref[s].T
            dot[s] = do_ref[s].T
            return 0

        lax.fori_loop(0, Sl, turn, 0)

    start, off = head_window(h, D)
    masked_bias(F, ids, seg_ref, tag_ref, parts, bm)
    lane = lax.broadcasted_iota(jnp.int32, (1, 256), 1)
    mine = (lane >= off) & (lane < off + HEAD)
    column = lax.broadcasted_iota(jnp.int32, (1, 128), 1) == h
    win = pl.ds(start, 256)
    here = pl.ds(pl.multiple_of(h * HEAD, 16), HEAD)
    root = HEAD**-0.5
    dbacc[...] = jnp.zeros_like(dbacc)

    def sample(s, _):
        kw = k_ref[s, :, win]
        vw = v_ref[s, :, win]
        km = jnp.where(mine, kw, jnp.zeros_like(kw))
        for r in range(0, T, RB):
            rows = pl.ds(r, RB)
            qw = q_ref[s, rows, win]
            gw = do_ref[s, rows, win]
            sc = head_scores(jnp.where(mine, qw, jnp.zeros_like(qw)), kw, bm[rows, :])
            lse = jnp.sum(
                jnp.where(column, lse_ref[s, rows, :], 0.0), axis=-1, keepdims=True
            )
            p = jnp.exp2(sc - lse)
            dp = dg(jnp.where(mine, gw, jnp.zeros_like(gw)), vw, NT)
            delta = jnp.sum(p * dp, axis=-1, keepdims=True)
            ds = (p * (dp - delta)).astype(bf16)
            pb[rows, :] = p.astype(bf16)
            dsb[rows, :] = ds
            dbacc[rows, :] += ds.astype(f32)
            dq_ref[s, rows, win] += dg(ds, km, NN) * root
        dvt[s, here, :] = dg(dot[s, here, :], pb[...], NN).astype(bf16)
        dkt[s, here, :] = (dg(qt[s, here, :], dsb[...], NN) * root).astype(bf16)
        return 0

    lax.fori_loop(0, Sl, sample, 0)
    for p in range(F):
        R = db_refs[p].shape[1]
        row = pl.multiple_of(ids[F + 2 + p] * R, 16)
        db_refs[p][0] = dbacc[pl.ds(row, R), :].astype(bf16)

    @pl.when(h == pl.num_programs(0) - 1)
    def _():
        def turn(s, _):
            dk_ref[s] = dkt[s].T
            dv_ref[s] = dvt[s].T
            return 0

        lax.fori_loop(0, Sl, turn, 0)


def attn_bwd(ids, seg, tag, q, k, v, do, lse, parts):
    Sl, T, D = q.shape
    F = len(parts)
    H, R = parts[0].shape[:2]
    part = pl.BlockSpec((1, R, T), lambda h, s: (h, 0, 0))
    outs = [
        jax.ShapeDtypeStruct((Sl, T, D), f32),
        jax.ShapeDtypeStruct((Sl, T, D), bf16),
        jax.ShapeDtypeStruct((Sl, T, D), bf16),
    ]
    res = pl.pallas_call(
        functools.partial(attn_bwd_kernel, F, min(T, 512)),
        grid_spec=pltpu.PrefetchScalarGridSpec(
            num_scalar_prefetch=1,
            grid=(H,),
            in_specs=[resident(x) for x in (seg, tag, q, k, v, do, lse)] + [part] * F,
            out_specs=[resident(x) for x in outs] + [part] * F,
            scratch_shapes=[
                pltpu.VMEM((T, T), f32),
                pltpu.VMEM((T, T), f32),
                pltpu.VMEM((T, T), bf16),
                pltpu.VMEM((T, T), bf16),
                pltpu.VMEM((Sl, D, T), bf16),
                pltpu.VMEM((Sl, D, T), bf16),
                pltpu.VMEM((Sl, D, T), bf16),
                pltpu.VMEM((Sl, D, T), bf16),
            ],
        ),
        out_shape=outs + [jax.ShapeDtypeStruct((H, R, T), bf16)] * F,
        compiler_params=pltpu.CompilerParams(
            dimension_semantics=("arbitrary",), vmem_limit_bytes=63 << 20
        ),
        cost_estimate=cost(Sl * H * T * T * 1536, Sl * T * D * 16 + H * T * T * 4, Sl * H * T * T),
        name="attn_bwd",
    )(ids, seg, tag, q, k, v, do, lse, *parts)
    return res[0], res[1], res[2], list(res[3:])


def pair_norm(x, ones):
    cen = x.astype(f32) - dg(x, ones, NN)
    inv = lax.rsqrt(dg((cen * cen).astype(bf16), ones, NN) + EPS)
    return cen * inv, inv


def pair_fwd_kernel(pair_ref, gain_ref, w_ref, out_ref, low):
    G, T, C = pair_ref.shape
    ones = jnp.full((C, C), 1.0 / C, bf16)

    def row(i, _):
        n, _ = pair_norm(pair_ref[i], ones)
        low[:, pl.ds(pl.multiple_of(i * C, 128), C)] = (n * gain_ref[...]).astype(bf16)
        return 0

    lax.fori_loop(0, G, row, 0)
    res = dg(w_ref[...], low[...], NT)
    out_ref[...] = res.reshape(res.shape[0] // G, G, T).astype(bf16)


def pair_fwd(pair, gain, w_rows):
    R, T, C = pair.shape
    G = 8
    H = w_rows.shape[0] // G
    return pl.pallas_call(
        pair_fwd_kernel,
        grid=(R // G,),
        in_specs=[
            pl.BlockSpec((G, T, C), lambda i: (i, 0, 0)),
            pl.BlockSpec((1, C), lambda i: (0, 0)),
            pl.BlockSpec((H * G, G * C), lambda i: (0, 0)),
        ],
        out_specs=pl.BlockSpec((H, G, T), lambda i: (0, i, 0)),
        out_shape=jax.ShapeDtypeStruct((H, R, T), bf16),
        scratch_shapes=[pltpu.VMEM((T, G * C), bf16)],
        compiler_params=pltpu.CompilerParams(
            dimension_semantics=("arbitrary",), vmem_limit_bytes=40 << 20
        ),
        cost_estimate=cost(R * T * C * 256, R * T * C * 3, R * T * C),
        name="pair_fwd",
    )(pair, gain, w_rows)


def pair_bwd_kernel(P, pair_ref, gain_ref, wc_ref, *refs):
    parts = refs[:P]
    out_ref, gw_ref, acc, turned = refs[P:]
    G, T, C = pair_ref.shape
    H = parts[0].shape[0]
    ones = jnp.full((C, C), 1.0 / C, bf16)

    @pl.when(pl.program_id(0) == 0)
    def _():
        acc[...] = jnp.zeros_like(acc)

    total = parts[0][...].astype(f32)
    for p in range(1, P):
        total = total + parts[p][...].astype(f32)
    flat = total.reshape(H * G, T)
    low8 = flat.astype(bf16)
    cols = low8.T
    turned[:, : H * G] = cols
    turned[:, H * G :] = cols

    def row(i, _):
        n, inv = pair_norm(pair_ref[i], ones)
        low = (n * gain_ref[...]).astype(bf16)
        acc[i] += dg(low8, low, NN)
        g = dg(turned[...], wc_ref[i], NN)
        mean = dg((g * n).astype(bf16), ones, NN)
        out_ref[i] = (inv * (g - n * mean)).astype(bf16)
        return 0

    lax.fori_loop(0, G, row, 0)

    @pl.when(pl.program_id(0) == pl.num_programs(0) - 1)
    def _():
        at = lax.broadcasted_iota(jnp.int32, (H * G, 1), 0) % G
        picked = jnp.zeros((H * G, C), f32)
        for i in range(G):
            picked = picked + jnp.where(at == i, acc[i], 0.0)
        gw_ref[...] = picked


def pair_bwd(pair, gain, wc, parts):
    R, T, C = pair.shape
    G = 8
    H = parts[0].shape[0]
    P = len(parts)
    return pl.pallas_call(
        functools.partial(pair_bwd_kernel, P),
        grid=(R // G,),
        in_specs=[
            pl.BlockSpec((G, T, C), lambda i: (i, 0, 0)),
            pl.BlockSpec((1, C), lambda i: (0, 0)),
            pl.BlockSpec((G, 2 * H * G, C), lambda i: (0, 0, 0)),
        ]
        + [pl.BlockSpec((H, G, T), lambda i: (0, i, 0))] * P,
        out_specs=[
            pl.BlockSpec((G, T, C), lambda i: (i, 0, 0)),
            pl.BlockSpec((H * G, C), lambda i: (0, 0)),
        ],
        out_shape=[
            jax.ShapeDtypeStruct((R, T, C), bf16),
            jax.ShapeDtypeStruct((H * G, C), f32),
        ],
        scratch_shapes=[
            pltpu.VMEM((G, H * G, C), f32),
            pltpu.VMEM((T, 2 * H * G), bf16),
        ],
        compiler_params=pltpu.CompilerParams(
            dimension_semantics=("arbitrary",), vmem_limit_bytes=40 << 20
        ),
        cost_estimate=cost(R * T * C * 512, R * T * C * 5, R * T * C),
        name="pair_bwd",
    )(pair, gain, wc, *parts)


def stats_of(x):
    mean = jnp.mean(x, axis=-1, keepdims=True)
    cen = x - mean
    inv = lax.rsqrt(jnp.mean(cen * cen, axis=-1, keepdims=True) + EPS)
    return cen * inv, inv


def sigmoid(x):
    return 1.0 / (1.0 + jnp.exp(-x))


def flat_rows(x):
    return x.reshape(x.shape[0] * x.shape[1], x.shape[2])


def over_samples(x, sb):
    R = x.shape[0] // sb
    total = x[:R]
    for i in range(1, sb):
        total = total + x[i * R : (i + 1) * R]
    return total


def tile_samples(x, sb):
    return x if sb == 1 else jnp.concatenate([x] * sb, axis=0)


def weight_copies(shapes, F, c, f, own, got, swapped, dst, sems):
    copies = []

    def add(src, to):
        copies.append(pltpu.make_async_copy(src, to, sems.at[len(copies)]))

    for i, (r, n) in enumerate(shapes):
        add(own[i], dst[i].at[pl.ds(pl.multiple_of(f * r, 16), r), :])
    for k in range(1, F):
        for packed, half in ((got[k - 1], c), (swapped[k - 1], 1 - c)):
            at = 0
            for i, (r, n) in enumerate(shapes):
                row = pl.multiple_of((f ^ k) * r, 16)
                for b in range(n // 2 // 384):
                    col = pl.multiple_of(half * (n // 2) + b * 384, 128)
                    add(
                        packed.at[pl.ds(at, r), :],
                        dst[i].at[pl.ds(row, r), pl.ds(col, 384)],
                    )
                    at += r
    return copies


def copies_in_group(shapes, F):
    return len(shapes) + (F - 1) * 2 * sum(n // 2 // 384 for _, n in shapes)


def pack_grads(shapes, F, c, accs, keep_ref, give_ref):
    for g in range(F):
        at = 0
        for (r, n), acc in zip(shapes, accs):
            for b in range(n // 2 // 384):
                for ref, half in ((keep_ref, c), (give_ref, 1 - c)):
                    col = pl.multiple_of(half * (n // 2) + b * 384, 128)
                    ref[g, at : at + r, :] = acc[g * r : (g + 1) * r, pl.ds(col, 384)].astype(bf16)
                at += r


def qkvg_kernel(F, shapes, ids, *refs):
    nin = 2 * (F - 1)
    act_ref, cond_ref, bq_ref, wq_hbm = refs[:4]
    got, swapped = refs[4 : 4 + F - 1], refs[4 + F - 1 : 4 + nin]
    q_ref, k_ref, v_ref, g_ref, w, sems = refs[4 + nin :]
    c, f = ids[F], ids[F + 1]

    @pl.when((pl.program_id(0) == 0) & (pl.program_id(1) == 0))
    def _():
        copies = weight_copies(shapes, F, c, f, (wq_hbm,), got, swapped, (w,), sems)
        for x in copies:
            x.start()
        for x in copies:
            x.wait()

    _, sb, R, D = act_ref.shape
    n, _ = stats_of(flat_rows(act_ref[0].astype(f32)))
    scale = tile_samples(sigmoid(cond_ref[:, :D]), sb)
    shift = tile_samples(cond_ref[:, D : 2 * D], sb)
    x = (scale * n + shift).astype(bf16)
    q_ref[...] = (dg(x, w[:, :D], NN) + bq_ref[...]).astype(bf16).reshape(sb, R, D)
    k_ref[...] = dg(x, w[:, D : 2 * D], NN).astype(bf16).reshape(sb, R, D)
    v_ref[...] = dg(x, w[:, 2 * D : 3 * D], NN).astype(bf16).reshape(sb, R, D)
    g_ref[0] = sigmoid(dg(x, w[:, 3 * D :], NN)).reshape(sb, R, D)


def sub_samples(sl, R):
    sb = max(1, min(sl, 256 // R))
    return sb, sl // sb


def cost(flops, nbytes, trans=0):
    return pl.CostEstimate(flops=int(flops), bytes_accessed=int(nbytes), transcendentals=int(trans))


ANY = pl.BlockSpec(memory_space=pl.ANY)


def qkvg_call(ids, act, cond, bq, wq, got, swapped):
    F, sl, R, D = act.shape
    T = F * R
    sb, nu = sub_samples(sl, R)
    shapes = [wq.shape]
    stacked = pl.BlockSpec((1, sb, R, D), lambda r, u, s: (r, u, 0, 0))
    natural = pl.BlockSpec((sb, R, D), lambda r, u, s: (u, s[r], 0))
    return pl.pallas_call(
        functools.partial(qkvg_kernel, F, shapes),
        grid_spec=pltpu.PrefetchScalarGridSpec(
            num_scalar_prefetch=1,
            grid=(F, nu),
            in_specs=[
                stacked,
                pl.BlockSpec((R, 2 * D), lambda r, u, s: (s[r], 0)),
                pl.BlockSpec((1, D), lambda r, u, s: (0, 0)),
            ]
            + [ANY] * (1 + 2 * (F - 1)),
            out_specs=[natural] * 3 + [stacked],
            scratch_shapes=[
                pltpu.VMEM((D, 4 * D), bf16),
                pltpu.SemaphoreType.DMA((copies_in_group(shapes, F),)),
            ],
        ),
        out_shape=[jax.ShapeDtypeStruct((sl, T, D), bf16)] * 3
        + [jax.ShapeDtypeStruct((F, sl, R, D), f32)],
        compiler_params=pltpu.CompilerParams(
            dimension_semantics=("arbitrary", "arbitrary"), vmem_limit_bytes=60 << 20
        ),
        cost_estimate=cost(8 * sl * T * D * D, 2 * sl * T * D * 6 + 8 * D * D, sl * T * D),
        name="qkvg",
    )(ids, act, cond, bq, wq, *got, *swapped)


def middle_kernel(F, shapes, ids, *refs):
    nin = 2 * (F - 1)
    mix_ref, gate_ref, act_ref, cot_ref, gone_ref, ctwo_ref = refs[:6]
    own = refs[6:9]
    got, swapped = refs[9 : 9 + F - 1], refs[9 + F - 1 : 9 + nin]
    (
        out_ref,
        da_ref,
        gpg_ref,
        mg_ref,
        ctg_ref,
        gog_ref,
        keep_ref,
        give_ref,
        wo,
        wab,
        wout,
        ao,
        aab,
        aout,
        sems,
    ) = refs[9 + nin :]
    c, f = ids[F], ids[F + 1]
    first = (pl.program_id(0) == 0) & (pl.program_id(1) == 0)
    last = (pl.program_id(0) == pl.num_programs(0) - 1) & (
        pl.program_id(1) == pl.num_programs(1) - 1
    )

    @pl.when(first)
    def _():
        copies = weight_copies(shapes, F, c, f, own, got, swapped, (wo, wab, wout), sems)
        for x in copies:
            x.start()
        ao[...] = jnp.zeros_like(ao)
        aab[...] = jnp.zeros_like(aab)
        aout[...] = jnp.zeros_like(aout)
        for x in copies:
            x.wait()

    _, sb, R, D = act_ref.shape
    H = wout.shape[0]
    gate = flat_rows(gate_ref[0])
    mix = flat_rows(mix_ref[...])
    branch = (gate * mix).astype(bf16)
    attn_out = dg(branch, wo[...], NN)
    sig_one = sigmoid(gone_ref[...])
    gate_one = tile_samples(sig_one, sb)
    middle = flat_rows(act_ref[0].astype(f32)) + gate_one * attn_out
    n, inv = stats_of(middle)
    sig_scale = sigmoid(ctwo_ref[:, :D])
    scale = tile_samples(sig_scale, sb)
    x2 = (scale * n + tile_samples(ctwo_ref[:, D : 2 * D], sb)).astype(bf16)
    up = dg(x2, wab[:, H:], NN)
    gp = dg(x2, wab[:, :H], NN)
    sg = sigmoid(gp)
    silu = gp * sg
    hidden = (silu * up).astype(bf16)
    ffn = dg(hidden, wout[...], NN)
    sig_two = sigmoid(ctwo_ref[:, 2 * D :])
    gate_two = tile_samples(sig_two, sb)
    out_ref[0] = (middle + gate_two * ffn).astype(bf16).reshape(sb, R, D)

    upstream = flat_rows(cot_ref[0].astype(f32))
    fg = (upstream * gate_two).astype(bf16)
    g_two = over_samples(upstream * ffn, sb) * (sig_two * (1.0 - sig_two))
    aout[...] += dg(hidden, fg, TN)
    hg = dg(fg, wout[...], NT)
    ga = (hg * up * sg * (1.0 + gp * (1.0 - sg))).astype(bf16)
    gb = (hg * silu).astype(bf16)
    aab[:, :H] += dg(x2, ga, TN)
    aab[:, H:] += dg(x2, gb, TN)
    xg = dg(ga, wab[:, :H], NT) + dg(gb, wab[:, H:], NT)
    g_scale = over_samples(xg * n, sb) * (sig_scale * (1.0 - sig_scale))
    g_shift = over_samples(xg, sb)
    inc = xg * scale
    mg = upstream + inv * (
        inc
        - jnp.mean(inc, axis=-1, keepdims=True)
        - n * jnp.mean(inc * n, axis=-1, keepdims=True)
    )
    mg_ref[0] = mg.reshape(sb, R, D)
    og = (mg * gate_one).astype(bf16)
    g_one = over_samples(mg * attn_out, sb) * (sig_one * (1.0 - sig_one))
    ao[...] += dg(branch, og, TN)
    bg = dg(og, wo[...], NT)
    da_ref[...] = (bg * gate).astype(bf16).reshape(sb, R, D)
    gpg_ref[0] = (bg * mix * (gate * (1.0 - gate))).astype(bf16).reshape(sb, R, D)

    @pl.when(pl.program_id(1) == 0)
    def _():
        ctg_ref[:, :D] = g_scale
        ctg_ref[:, D : 2 * D] = g_shift
        ctg_ref[:, 2 * D :] = g_two
        gog_ref[...] = g_one

    @pl.when(pl.program_id(1) > 0)
    def _():
        ctg_ref[:, :D] += g_scale
        ctg_ref[:, D : 2 * D] += g_shift
        ctg_ref[:, 2 * D :] += g_two
        gog_ref[...] += g_one

    @pl.when(last)
    def _():
        pack_grads(shapes, F, c, (ao, aab, aout), keep_ref, give_ref)


def middle_call(ids, mix, gate, act, cot, cond_one, cond_two, wo, wab, wout, got, swapped):
    F, sl, R, D = act.shape
    T = F * R
    H = wout.shape[0] * F
    sb, nu = sub_samples(sl, R)
    shapes = [wo.shape, wab.shape, wout.shape]
    rows = sum(r * (n // 2 // 384) for r, n in shapes)
    stacked = pl.BlockSpec((1, sb, R, D), lambda r, u, s: (r, u, 0, 0))
    natural = pl.BlockSpec((sb, R, D), lambda r, u, s: (u, s[r], 0))
    whole = pl.BlockSpec((F, rows, 384), lambda r, u, s: (0, 0, 0), pipeline_mode=pl.Buffered(1))
    flops = 3 * 2 * sl * T * D * (D + 3 * H)
    return pl.pallas_call(
        functools.partial(middle_kernel, F, shapes),
        grid_spec=pltpu.PrefetchScalarGridSpec(
            num_scalar_prefetch=1,
            grid=(F, nu),
            in_specs=[
                natural,
                stacked,
                stacked,
                stacked,
                pl.BlockSpec((R, D), lambda r, u, s: (s[r], 2)),
                pl.BlockSpec((R, 3 * D), lambda r, u, s: (s[r], 0)),
            ]
            + [ANY] * (3 + 2 * (F - 1)),
            out_specs=[
                stacked,
                natural,
                stacked,
                stacked,
                pl.BlockSpec((R, 3 * D), lambda r, u, s: (s[r], 0)),
                pl.BlockSpec((R, D), lambda r, u, s: (s[r], 0)),
                whole,
                whole,
            ],
            scratch_shapes=[
                pltpu.VMEM((D, D), bf16),
                pltpu.VMEM((D, 2 * H), bf16),
                pltpu.VMEM((H, D), bf16),
                pltpu.VMEM((D, D), f32),
                pltpu.VMEM((D, 2 * H), f32),
                pltpu.VMEM((H, D), f32),
                pltpu.SemaphoreType.DMA((copies_in_group(shapes, F),)),
            ],
        ),
        out_shape=[
            jax.ShapeDtypeStruct((F, sl, R, D), bf16),
            jax.ShapeDtypeStruct((sl, T, D), bf16),
            jax.ShapeDtypeStruct((F, sl, R, D), bf16),
            jax.ShapeDtypeStruct((F, sl, R, D), f32),
            jax.ShapeDtypeStruct((T, 3 * D), f32),
            jax.ShapeDtypeStruct((T, D), f32),
            jax.ShapeDtypeStruct((F, rows, 384), bf16),
            jax.ShapeDtypeStruct((F, rows, 384), bf16),
        ],
        compiler_params=pltpu.CompilerParams(
            dimension_semantics=("arbitrary", "arbitrary"), vmem_limit_bytes=63 << 20
        ),
        cost_estimate=cost(flops, sl * T * D * 24, sl * T * H),
        name="middle",
    )(ids, mix, gate, act, cot, cond_one, cond_two, wo, wab, wout, *got, *swapped)


def back_kernel(F, shapes, ids, *refs):
    nin = 2 * (F - 1)
    act_ref, cond_ref, dq_ref, dk_ref, dv_ref, gpg_ref, mg_ref, wq_hbm = refs[:8]
    got, swapped = refs[8 : 8 + F - 1], refs[8 + F - 1 : 8 + nin]
    ag_ref, cg_ref, bq_ref, keep_ref, give_ref, w, acc, sems = refs[8 + nin :]
    c, f = ids[F], ids[F + 1]
    first = (pl.program_id(0) == 0) & (pl.program_id(1) == 0)
    last = (pl.program_id(0) == pl.num_programs(0) - 1) & (
        pl.program_id(1) == pl.num_programs(1) - 1
    )

    @pl.when(first)
    def _():
        copies = weight_copies(shapes, F, c, f, (wq_hbm,), got, swapped, (w,), sems)
        for x in copies:
            x.start()
        acc[...] = jnp.zeros_like(acc)
        bq_ref[...] = jnp.zeros_like(bq_ref)
        for x in copies:
            x.wait()

    _, sb, R, D = act_ref.shape
    n, inv = stats_of(flat_rows(act_ref[0].astype(f32)))
    sig_scale = sigmoid(cond_ref[:, :D])
    scale = tile_samples(sig_scale, sb)
    x = (scale * n + tile_samples(cond_ref[:, D : 2 * D], sb)).astype(bf16)
    dq = flat_rows(dq_ref[...])
    bq_ref[...] += jnp.sum(dq, axis=0, keepdims=True)
    xg = None
    grads = (dq.astype(bf16), flat_rows(dk_ref[...]), flat_rows(dv_ref[...]), flat_rows(gpg_ref[0]))
    for i, g in enumerate(grads):
        acc[:, i * D : (i + 1) * D] += dg(x, g, TN)
        part = dg(g, w[:, i * D : (i + 1) * D], NT)
        xg = part if xg is None else xg + part
    g_scale = over_samples(xg * n, sb) * (sig_scale * (1.0 - sig_scale))
    g_shift = over_samples(xg, sb)
    inc = xg * scale
    ag = flat_rows(mg_ref[0]) + inv * (
        inc
        - jnp.mean(inc, axis=-1, keepdims=True)
        - n * jnp.mean(inc * n, axis=-1, keepdims=True)
    )
    ag_ref[0] = ag.astype(bf16).reshape(sb, R, D)

    @pl.when(pl.program_id(1) == 0)
    def _():
        cg_ref[:, :D] = g_scale
        cg_ref[:, D:] = g_shift

    @pl.when(pl.program_id(1) > 0)
    def _():
        cg_ref[:, :D] += g_scale
        cg_ref[:, D:] += g_shift

    @pl.when(last)
    def _():
        pack_grads(shapes, F, c, (acc,), keep_ref, give_ref)


def back_call(ids, act, cond, dq, dk, dv, gpg, mg, wq, got, swapped):
    F, sl, R, D = act.shape
    T = F * R
    sb, nu = sub_samples(sl, R)
    shapes = [wq.shape]
    rows = sum(r * (n // 2 // 384) for r, n in shapes)
    stacked = pl.BlockSpec((1, sb, R, D), lambda r, u, s: (r, u, 0, 0))
    natural = pl.BlockSpec((sb, R, D), lambda r, u, s: (u, s[r], 0))
    whole = pl.BlockSpec((F, rows, 384), lambda r, u, s: (0, 0, 0), pipeline_mode=pl.Buffered(1))
    return pl.pallas_call(
        functools.partial(back_kernel, F, shapes),
        grid_spec=pltpu.PrefetchScalarGridSpec(
            num_scalar_prefetch=1,
            grid=(F, nu),
            in_specs=[
                stacked,
                pl.BlockSpec((R, 2 * D), lambda r, u, s: (s[r], 0)),
                natural,
                natural,
                natural,
                stacked,
                stacked,
            ]
            + [ANY] * (1 + 2 * (F - 1)),
            out_specs=[
                stacked,
                pl.BlockSpec((R, 2 * D), lambda r, u, s: (s[r], 0)),
                pl.BlockSpec((1, D), lambda r, u, s: (0, 0)),
                whole,
                whole,
            ],
            scratch_shapes=[
                pltpu.VMEM((D, 4 * D), bf16),
                pltpu.VMEM((D, 4 * D), f32),
                pltpu.SemaphoreType.DMA((copies_in_group(shapes, F),)),
            ],
        ),
        out_shape=[
            jax.ShapeDtypeStruct((F, sl, R, D), bf16),
            jax.ShapeDtypeStruct((T, 2 * D), f32),
            jax.ShapeDtypeStruct((1, D), f32),
            jax.ShapeDtypeStruct((F, rows, 384), bf16),
            jax.ShapeDtypeStruct((F, rows, 384), bf16),
        ],
        compiler_params=pltpu.CompilerParams(
            dimension_semantics=("arbitrary", "arbitrary"), vmem_limit_bytes=60 << 20
        ),
        cost_estimate=cost(16 * sl * T * D * D, sl * T * D * 22 + 16 * D * D, sl * T),
        name="back",
    )(ids, act, cond, dq, dk, dv, gpg, mg, wq, *got, *swapped)


class Net:
    def __init__(self, dp, fsdp):
        self.Z, self.F, self.Fh = dp // 2, fsdp, fsdp // 2
        d = lax.axis_index("dp")
        self.z, self.c = d // 2, d % 2
        self.f = lax.axis_index("fsdp")
        self.fh, self.fl = self.f // self.Fh, self.f % self.Fh
        r = jnp.arange(self.F, dtype=jnp.int32)
        blocks = (self.c ^ (r % 2)) * self.Fh + (self.fl ^ (r // 2))
        rows = ((self.c + r // self.Fh) % 2) * self.Fh + (self.fl ^ (r % self.Fh))
        self.ids = jnp.concatenate(
            [blocks, jnp.stack([self.c, self.f]), rows]
        ).astype(jnp.int32)

    def send(self, x, fn):
        F = self.F
        pairs = []
        for z in range(self.Z):
            for c in range(2):
                for f in range(F):
                    z2, c2, f2 = fn(z, c, f)
                    pairs.append(((z * 2 + c) * F + f, (z2 * 2 + c2) * F + f2))
        return lax.ppermute(x, ("dp", "fsdp"), pairs)

    def core_swap(self, x):
        return self.send(x, lambda z, c, f: (z, 1 - c, f))

    def to_owner(self, x, a):
        Fh = self.Fh
        return self.send(x, lambda z, c, f: (z, f // Fh, c * Fh + ((f % Fh) ^ a)))

    def exchange_in(self, x):
        F, Fh = self.F, self.Fh
        sl = x.shape[0] // F
        parts = []
        for a in range(Fh):
            for b in range(2):
                g = (self.fl ^ a) * 2 + (self.fh ^ b)
                part = lax.dynamic_slice_in_dim(x, g * sl, sl, 0)
                parts.append(
                    self.send(part, lambda z, c, f: (z, (f // Fh) ^ b, c * Fh + ((f % Fh) ^ a)))
                )
        return parts

    def exchange_out(self, y):
        F, sl, R, D = y.shape
        Fh = self.Fh
        out = jnp.zeros((F * sl, R, D), y.dtype)
        for a in range(Fh):
            for b in range(2):
                part = self.send(
                    y[a * 2 + b], lambda z, c, f: (z, f // Fh, (c ^ b) * Fh + ((f % Fh) ^ a))
                )
                g = (self.fl ^ a) * 2 + (self.fh ^ b)
                out = lax.dynamic_update_slice_in_dim(out, part, g * sl, 0)
        return out

    def gather_rows(self, x):
        own = [self.to_owner(x, a) for a in range(self.Fh)]
        return own + [self.core_swap(p) for p in own]

    def natural(self, parts, axis):
        R = parts[0].shape[axis]
        shape = parts[0].shape
        out = jnp.zeros(shape[:axis] + (R * self.F,) + shape[axis + 1 :], parts[0].dtype)
        for p, part in enumerate(parts):
            out = lax.dynamic_update_slice_in_dim(out, part, self.ids[self.F + 2 + p] * R, axis)
        return out

    def reduce_rows(self, parts):
        Fh = self.Fh
        out = []
        for a in range(Fh):
            got = self.core_swap(parts[Fh + a])
            half = (parts[a].astype(f32) + got.astype(f32)).astype(got.dtype)
            out.append(self.to_owner(half, a))
        return out

    def core_half(self, x, half):
        n = x.shape[-1]
        x = lax.dynamic_slice_in_dim(x, half * (n // 2), n // 2, x.ndim - 1)
        return [x[..., b * 384 : (b + 1) * 384] for b in range(n // 2 // 384)]

    def pack(self, xs, half):
        blocks = [b for x in xs for b in self.core_half(x, half)]
        return jnp.concatenate(blocks, axis=-2)

    def gather_packed(self, packed):
        F = self.F
        got = [self.send(packed, lambda z, c, f: (z, c, f ^ k)) for k in range(1, F)]
        return got, [self.core_swap(g) for g in got]

    def gather_weight(self, w):
        return lax.all_gather(w, "fsdp", axis=0, tiled=True)

    def reduce_plane(self, keep, give):
        got = self.core_swap(give)
        total = None
        for k in range(self.F):
            mine = lax.dynamic_index_in_dim(keep, self.f ^ k, 0, keepdims=False)
            other = lax.dynamic_index_in_dim(got, self.f ^ k, 0, keepdims=False)
            part = mine.astype(f32) + other.astype(f32)
            if k:
                part = self.send(part.astype(bf16), lambda z, c, f: (z, c, f ^ k)).astype(f32)
            total = part if total is None else total + part
        return total.astype(bf16)

    def reduce_z(self, flat):
        Z = self.Z
        rows = flat.shape[0]
        pad = -rows % Z
        if pad:
            flat = jnp.pad(flat, ((0, pad), (0, 0)))
        bit = 1
        while bit < Z:
            h = flat.shape[0] // 2
            up = (self.z // bit) % 2
            keep = lax.dynamic_slice_in_dim(flat, up * h, h, 0)
            give = lax.dynamic_slice_in_dim(flat, (1 - up) * h, h, 0)
            got = self.send(give, lambda z, c, f: (z ^ bit, c, f))
            flat = (keep.astype(f32) + got.astype(f32)).astype(bf16)
            bit *= 2
        while bit > 1:
            bit //= 2
            up = (self.z // bit) % 2
            got = self.send(flat, lambda z, c, f: (z ^ bit, c, f))
            flat = jnp.concatenate(
                [jnp.where(up == 0, flat, got), jnp.where(up == 0, got, flat)], axis=0
            )
        other = self.core_swap(flat)
        return jnp.where(self.c == 0, flat, other), jnp.where(self.c == 0, other, flat)

    def unpack(self, halves, shapes):
        outs, at = [], 0
        for r, n in shapes:
            nb = n // 2 // 384
            cols = []
            for half in halves:
                for b in range(nb):
                    cols.append(half[at + b * r : at + (b + 1) * r])
            at += nb * r
            outs.append(jnp.concatenate(cols, axis=1).astype(f32))
        return outs


def body(
    dp,
    fsdp,
    act,
    single,
    pair,
    segment,
    padding,
    cotangent,
    gain_s1,
    w_cond1,
    b_cond1,
    w_qkvg,
    b_q,
    gain_z,
    w_pair,
    w_o,
    gain_s2,
    w_cond2,
    b_cond2,
    w_ab,
    w_out,
):
    net = Net(dp, fsdp)
    F, ids = net.F, net.ids
    act, single, pair, segment, padding, cotangent = (
        x[0] for x in (act, single, pair, segment, padding, cotangent)
    )
    S, R, D = act.shape
    T = R * F
    COND = single.shape[1]

    vecs = [gain_s1, b_cond1, b_q, gain_z, w_pair, gain_s2, b_cond2]
    sizes = [v.size for v in vecs]
    srows = -(-sum(sizes) // 768)
    flat = jnp.concatenate([v.reshape(-1) for v in vecs])
    flat = jnp.pad(flat, (0, srows * 768 - flat.shape[0])).reshape(srows, 768)
    smalls = jnp.zeros((F, srows, 768), bf16)
    for k in range(F):
        got = flat if k == 0 else net.send(flat, lambda z, c, f: (z, c, f ^ k))
        smalls = lax.dynamic_update_slice_in_dim(smalls, got[None], net.f ^ k, 0)
    smalls = smalls.reshape(F, srows * 768)
    full, at = [], 0
    for v, n in zip(vecs, sizes):
        full.append(smalls[:, at : at + n].reshape((F * v.shape[0],) + v.shape[1:]).astype(f32))
        at += n
    gs1, bc1, bq, gz, wp, gs2, bc2 = full

    wc1 = net.gather_weight(w_cond1)
    tag = jnp.where(padding == 1, -1, segment)
    cols = jnp.stack([segment.astype(f32), tag.astype(f32)], axis=1)
    cond_in = jnp.concatenate([single, jnp.pad(cols, ((0, 0), (0, 126)))], axis=1)
    cond_in = net.natural(net.gather_rows(cond_in), 0)
    single_all = cond_in[:, :COND]
    seg_col = cond_in[:, COND : COND + 1]
    tag_row = cond_in[:, COND + 1].reshape(1, T)

    act_l = jnp.stack(net.exchange_in(act))
    wq_got, wq_swapped = net.gather_packed(net.pack([w_qkvg], net.c))

    wt = wp.T
    eye = jnp.eye(8, dtype=f32)
    w_rows = (wt[:, None, None, :] * eye[None, :, :, None]).reshape(HEADS * 8, -1).astype(bf16)
    gz_row = gz.reshape(1, -1)
    bias = net.gather_rows(pair_fwd(pair, gz_row, w_rows))

    wc2 = net.gather_weight(w_cond2)
    single_n, _ = norm_stats(single_all)
    single_first = (single_n * gs1).astype(bf16)
    cond_one = dg(single_first, wc1, NN) + bc1
    q, k, v, gate = qkvg_call(
        ids, act_l, cond_one, bq.reshape(1, D), w_qkvg, wq_got, wq_swapped
    )

    mid_got, mid_swapped = net.gather_packed(net.pack([w_o, w_ab, w_out], net.c))
    cot_l = jnp.stack(net.exchange_in(cotangent))
    single_second = (single_n * gs2).astype(bf16)
    cond_two = dg(single_second, wc2, NN) + bc2

    mix, lse = attn_fwd(ids, seg_col, tag_row, q, k, v, bias)
    out, d_attn, gate_proj, mid_grad, cond_two_grad, gate_one_grad, keep, give = middle_call(
        ids, mix, gate, act_l, cot_l, cond_one, cond_two, w_o, w_ab, w_out, mid_got, mid_swapped
    )
    block_out = net.exchange_out(out)[None]

    cond_two_low = cond_two_grad.astype(bf16)
    grad_w_cond2 = dg(single_second, cond_two_low, TN)
    s_two_grad = dg(cond_two_low, wc2, NT)
    piece_mid = net.reduce_plane(keep, give)
    g4 = grad_w_cond2.astype(bf16).reshape(F, -1, 3 * D)
    piece_c2 = net.reduce_plane(net.pack([g4], net.c), net.pack([g4], 1 - net.c))
    early = [w_o.shape, w_ab.shape, w_out.shape, w_cond2.shape]
    total_wo, total_wab, total_wout, total_wc2 = net.unpack(
        net.reduce_z(jnp.concatenate([piece_mid, piece_c2], axis=0)), early
    )

    dq, dk, dv, db = attn_bwd(ids, seg_col, tag_row, q, k, v, d_attn, lse, bias)
    db = net.reduce_rows(db)
    ag, cond_one_part, bq_grad, keep, give = back_call(
        ids, act_l, cond_one, dq, dk, dv, gate_proj, mid_grad, w_qkvg, wq_got, wq_swapped
    )
    act_grad = net.exchange_out(ag)[None]
    cond_one_grad = jnp.concatenate([cond_one_part, gate_one_grad], axis=1)
    cond_one_low = cond_one_grad.astype(bf16)
    grad_w_cond1 = dg(single_first, cond_one_low, TN)
    s_one_grad = dg(cond_one_low, wc1, NT)
    s_grad = s_one_grad * gs1 + s_two_grad * gs2
    s_parts = [
        lax.dynamic_slice_in_dim(s_grad, ids[F + 2 + p] * R, R, 0) for p in range(F)
    ]
    s_grad = functools.reduce(jnp.add, net.reduce_rows(s_parts))
    local_n, local_inv = norm_stats(single)
    single_grad = norm_back(local_n, local_inv, s_grad)[None]

    wc = wt * gz_row
    wc = wc - jnp.mean(wc, axis=1, keepdims=True)
    wc = (wc[None, :, None, :] * eye[:, None, :, None]).reshape(8, HEADS * 8, -1)
    wc_hi = wc.astype(bf16)
    wc = jnp.concatenate([wc_hi, (wc - wc_hi.astype(f32)).astype(bf16)], axis=1)
    pair_grad, gw = pair_bwd(pair, gz_row, wc, db)
    grad_w_pair = jnp.sum(gw.reshape(HEADS, 8, -1), axis=1).T
    grad_gain_z = jnp.sum(wp * grad_w_pair, axis=1) / gz

    small_grads = [
        jnp.sum(s_one_grad * single_n, axis=0),
        jnp.sum(cond_one_grad, axis=0),
        bq_grad,
        grad_gain_z,
        grad_w_pair,
        jnp.sum(s_two_grad * single_n, axis=0),
        jnp.sum(cond_two_grad, axis=0),
    ]
    sg = jnp.concatenate([g.reshape(F, -1) for g in small_grads], axis=1)
    sg = jnp.pad(sg, ((0, 0), (0, srows * 768 - sg.shape[1]))).reshape(F, srows, 768)
    g4 = [grad_w_cond1.astype(bf16).reshape(F, -1, 3 * D), sg.astype(bf16)]
    piece_wq = net.reduce_plane(keep, give)
    piece_c1 = net.reduce_plane(net.pack(g4, net.c), net.pack(g4, 1 - net.c))
    late = [w_qkvg.shape, w_cond1.shape, (srows, 768)]
    total_wq, total_wc1, total_small = net.unpack(
        net.reduce_z(jnp.concatenate([piece_wq, piece_c1], axis=0)), late
    )
    total_small = total_small.reshape(-1)
    outs, at = [], 0
    for v_, n in zip(vecs, sizes):
        outs.append(total_small[at : at + n].reshape(v_.shape))
        at += n
    total_gs1, total_bc1, total_bq, total_gz, total_wp, total_gs2, total_bc2 = outs
    return (
        block_out,
        act_grad,
        single_grad,
        pair_grad[None],
        total_gs1,
        total_wc1,
        total_bc1,
        total_wq,
        total_bq,
        total_gz,
        total_wp,
        total_wo,
        total_gs2,
        total_wc2,
        total_bc2,
        total_wab,
        total_wout,
    )


def solution(mesh):
    return jax.shard_map(
        functools.partial(body, mesh.shape["dp"], mesh.shape["fsdp"]),
        mesh=mesh,
        in_specs=(
            P("dp", None, "fsdp", None),
            P("dp", "fsdp", None),
            P("dp", "fsdp", None, None),
            P("dp", "fsdp"),
            P("dp", "fsdp"),
            P("dp", None, "fsdp", None),
            P("fsdp"),
            P("fsdp", None),
            P("fsdp"),
            P("fsdp", None),
            P("fsdp"),
            P("fsdp"),
            P("fsdp", None),
            P("fsdp", None),
            P("fsdp"),
            P("fsdp", None),
            P("fsdp"),
            P("fsdp", None),
            P("fsdp", None),
        ),
        out_specs=(
            P("dp", None, "fsdp", None),
            P("dp", None, "fsdp", None),
            P("dp", "fsdp", None),
            P("dp", "fsdp", None, None),
            P("fsdp"),
            P("fsdp", None),
            P("fsdp"),
            P("fsdp", None),
            P("fsdp"),
            P("fsdp"),
            P("fsdp", None),
            P("fsdp", None),
            P("fsdp"),
            P("fsdp", None),
            P("fsdp"),
            P("fsdp", None),
            P("fsdp", None),
        ),
        check_vma=False,
    )
```

```python
import functools

import jax
import jax.numpy as jnp
from jax import lax
from jax.experimental import pallas as pl
from jax.experimental.pallas import tpu as pltpu
from jax.sharding import Mesh
from jax.sharding import PartitionSpec as P

HEADS = 16
HEAD = 48
FF = 1536
EPS = 1e-05
LOG2E = 1.4426950408889634
NEG = -1000000000.0
f32 = jnp.float32
bf16 = jnp.bfloat16
NT = (((1,), (1,)), ((), ()))
NN = (((1,), (0,)), ((), ()))
TN = (((0,), (0,)), ((), ()))


def norm_stats(values):
    average = jnp.mean(values, axis=-1, keepdims=True)
    centred = values - average
    inverse = lax.rsqrt(jnp.mean(centred * centred, axis=-1, keepdims=True) + EPS)
    return (centred * inverse, inverse)


def norm_back(normed, inverse, incoming):
    return inverse * (
        incoming
        - jnp.mean(incoming, axis=-1, keepdims=True)
        - normed * jnp.mean(incoming * normed, axis=-1, keepdims=True)
    )


def sig_slope(values):
    sigma_val = jax.nn.sigmoid(values)
    return sigma_val * (1.0 - sigma_val)


def dg(a, b, dims):
    return lax.dot_general(a, b, dims, preferred_element_type=f32)


def cost(flops, nbytes, trans=0):
    return pl.CostEstimate(flops=int(flops), bytes_accessed=int(nbytes), transcendentals=int(trans))


ANY = pl.BlockSpec(memory_space=pl.ANY)


def head_window(h, D):
    tile = jnp.minimum((h * HEAD) // 128, D // 128 - 2)
    return pl.multiple_of(tile * 128, 128), h * HEAD - tile * 128


def masked_bias(F, ids, seg_ref, tag_ref, parts, bm):
    for p in range(F):
        R = parts[p].shape[1]
        row = pl.multiple_of(ids[F + 2 + p] * R, 16)
        bm[pl.ds(row, R), :] = jnp.where(
            seg_ref[pl.ds(row, R), :] == tag_ref[...], parts[p][0].astype(f32) * LOG2E, -jnp.inf
        )


def head_scores(q, k, bm):
    s = dg(q, k, NT)
    return jnp.where(bm > -jnp.inf, s * (HEAD**-0.5 * LOG2E) + bm, NEG * LOG2E)


def attn_fwd_kernel(F, nd, RB, ids, seg_ref, tag_ref, q_ref, k_ref, v_ref, *refs):
    parts = refs[:F]
    o_ref, lse_ref, bm = refs[F + nd :]
    Sl, T, D = q_ref.shape
    h = pl.program_id(0)

    @pl.when(h == 0)
    def _():
        o_ref[...] = jnp.zeros_like(o_ref)
        lse_ref[...] = jnp.zeros_like(lse_ref)

    start, off = head_window(h, D)
    masked_bias(F, ids, seg_ref, tag_ref, parts, bm)
    lane = lax.broadcasted_iota(jnp.int32, (1, 256), 1)
    mine = (lane >= off) & (lane < off + HEAD)
    column = lax.broadcasted_iota(jnp.int32, (1, 128), 1) == h
    win = pl.ds(start, 256)

    def sample(s, _):
        kw = k_ref[s, :, win]
        vw = v_ref[s, :, win]
        vw = jnp.where(mine, vw, jnp.zeros_like(vw))
        for r in range(0, T, RB):
            rows = pl.ds(r, RB)
            qw = q_ref[s, rows, win]
            sc = head_scores(jnp.where(mine, qw, jnp.zeros_like(qw)), kw, bm[rows, :])
            m = jnp.max(sc, axis=-1, keepdims=True)
            p = jnp.exp2(sc - m)
            l = jnp.sum(p, axis=-1, keepdims=True)
            o_ref[s, rows, win] += dg(p.astype(bf16), vw, NN) * (1.0 / l)
            lse_ref[s, rows, :] = jnp.where(column, m + jnp.log2(l), lse_ref[s, rows, :])
        return 0

    lax.fori_loop(0, Sl, sample, 0, unroll=min(Sl, 4))


def resident(shape, last=0):
    at = (0,) * (len(shape) - 1) + (last,)
    return pl.BlockSpec(shape, lambda h, s: at, pipeline_mode=pl.Buffered(1))


def attn_fwd(ids, seg, tag, q, k, v, parts, group, deps=()):
    Sl, T, D = q.shape
    F = len(parts)
    H, R = parts[0].shape[:2]
    W = H * HEAD
    lanes = resident((Sl, T, W), group)
    part = pl.BlockSpec((1, R, T), lambda h, s: (h, 0, 0))
    outs = [jax.ShapeDtypeStruct((Sl, T, W), f32), jax.ShapeDtypeStruct((Sl, T, 128), f32)]
    return pl.pallas_call(
        functools.partial(attn_fwd_kernel, F, len(deps), min(T, 256)),
        grid_spec=pltpu.PrefetchScalarGridSpec(
            num_scalar_prefetch=1,
            grid=(H,),
            in_specs=[resident(seg.shape), resident(tag.shape), lanes, lanes, lanes]
            + [part] * F
            + [ANY] * len(deps),
            out_specs=[resident(x.shape) for x in outs],
            scratch_shapes=[pltpu.VMEM((T, T), f32)],
        ),
        out_shape=outs,
        compiler_params=pltpu.CompilerParams(
            dimension_semantics=("arbitrary",), vmem_limit_bytes=60 << 20
        ),
        cost_estimate=cost(Sl * H * T * T * 3700, Sl * T * W * 10 + H * T * T * 2, Sl * H * T * T),
        name="attn_fwd",
    )(ids, seg, tag, q, k, v, *parts, *deps)


def attn_bwd_kernel(F, nd, RB, ids, seg_ref, tag_ref, q_ref, k_ref, v_ref, do_ref, lse_ref, *refs):
    parts, refs = refs[:F], refs[nd:]
    dq_ref, dk_ref, dv_ref = refs[F : F + 3]
    db_refs = refs[F + 3 : F + 3 + F]
    bm, dbacc, pb, dsb, qt, dot, dkt, dvt = refs[F + 3 + F :]
    Sl, T, D = q_ref.shape
    h = pl.program_id(0)

    @pl.when(h == 0)
    def _():
        dq_ref[...] = jnp.zeros_like(dq_ref)

        def turn(s, _):
            qt[s] = q_ref[s].T
            dot[s] = do_ref[s].T
            return 0

        lax.fori_loop(0, Sl, turn, 0)

    start, off = head_window(h, D)
    masked_bias(F, ids, seg_ref, tag_ref, parts, bm)
    lane = lax.broadcasted_iota(jnp.int32, (1, 256), 1)
    mine = (lane >= off) & (lane < off + HEAD)
    column = lax.broadcasted_iota(jnp.int32, (1, 128), 1) == h
    win = pl.ds(start, 256)
    here = pl.ds(pl.multiple_of(h * HEAD, 16), HEAD)
    root = HEAD**-0.5
    dbacc[...] = jnp.zeros_like(dbacc)

    U = min(Sl, 2)

    def sample(s, u):
        kw = k_ref[s, :, win]
        vw = v_ref[s, :, win]
        km = jnp.where(mine, kw, jnp.zeros_like(kw))
        for r in range(0, T, RB):
            rows = pl.ds(r, RB)
            qw = q_ref[s, rows, win]
            gw = do_ref[s, rows, win]
            sc = head_scores(jnp.where(mine, qw, jnp.zeros_like(qw)), kw, bm[rows, :])
            lse = jnp.sum(
                jnp.where(column, lse_ref[s, rows, :], 0.0), axis=-1, keepdims=True
            )
            p = jnp.exp2(sc - lse)
            dp = dg(jnp.where(mine, gw, jnp.zeros_like(gw)), vw, NT)
            delta = jnp.sum(p * dp, axis=-1, keepdims=True)
            ds = (p * (dp - delta)).astype(bf16)
            pb[u, rows, :] = p.astype(bf16)
            dsb[u, rows, :] = ds
            dbacc[rows, :] += ds.astype(f32)
            dq_ref[s, rows, win] += dg(ds, km, NN) * root
        dvt[s, here, :] = dg(dot[s, here, :], pb[u], NN).astype(bf16)
        dkt[s, here, :] = (dg(qt[s, here, :], dsb[u], NN) * root).astype(bf16)

    def samples(i, _):
        for u in range(U):
            sample(i * U + u, u)
        return 0

    lax.fori_loop(0, Sl // U, samples, 0)
    for p in range(F):
        R = db_refs[p].shape[1]
        row = pl.multiple_of(ids[F + 2 + p] * R, 16)
        db_refs[p][0] = dbacc[pl.ds(row, R), :].astype(bf16)

    @pl.when(h == pl.num_programs(0) - 1)
    def _():
        def turn(s, _):
            dk_ref[s] = dkt[s].T
            dv_ref[s] = dvt[s].T
            return 0

        lax.fori_loop(0, Sl, turn, 0)


def attn_bwd(ids, seg, tag, q, k, v, do, lse, parts, group, deps=()):
    Sl, T, D = q.shape
    F = len(parts)
    H, R = parts[0].shape[:2]
    W = H * HEAD
    lanes = resident((Sl, T, W), group)
    part = pl.BlockSpec((1, R, T), lambda h, s: (h, 0, 0))
    outs = [
        jax.ShapeDtypeStruct((Sl, T, W), f32),
        jax.ShapeDtypeStruct((Sl, T, W), bf16),
        jax.ShapeDtypeStruct((Sl, T, W), bf16),
    ]
    res = pl.pallas_call(
        functools.partial(attn_bwd_kernel, F, len(deps), min(T, 512)),
        grid_spec=pltpu.PrefetchScalarGridSpec(
            num_scalar_prefetch=1,
            grid=(H,),
            in_specs=[resident(seg.shape), resident(tag.shape)]
            + [lanes] * 4
            + [resident(lse.shape)]
            + [part] * F
            + [ANY] * len(deps),
            out_specs=[resident(x.shape) for x in outs] + [part] * F,
            scratch_shapes=[
                pltpu.VMEM((T, T), f32),
                pltpu.VMEM((T, T), f32),
                pltpu.VMEM((2, T, T), bf16),
                pltpu.VMEM((2, T, T), bf16),
                pltpu.VMEM((Sl, W, T), bf16),
                pltpu.VMEM((Sl, W, T), bf16),
                pltpu.VMEM((Sl, W, T), bf16),
                pltpu.VMEM((Sl, W, T), bf16),
            ],
        ),
        out_shape=outs + [jax.ShapeDtypeStruct((H, R, T), bf16)] * F,
        compiler_params=pltpu.CompilerParams(
            dimension_semantics=("arbitrary",), vmem_limit_bytes=63 << 20
        ),
        cost_estimate=cost(Sl * H * T * T * 6200, Sl * T * W * 16 + H * T * T * 4, Sl * H * T * T),
        name="attn_bwd",
    )(ids, seg, tag, q, k, v, do, lse, *parts, *deps)
    return res[0], res[1], res[2], list(res[3:])


def pair_norm(x, ones):
    cen = x.astype(f32) - dg(x, ones, NN)
    inv = lax.rsqrt(dg((cen * cen).astype(bf16), ones, NN) + EPS)
    return cen * inv, inv


def pair_fwd_kernel(U, pair_ref, gain_ref, w_ref, *refs):
    first_ref, second_ref, low = refs[-3:]
    G, T, C = pair_ref.shape
    ones = jnp.full((C, C), 1.0 / C, bf16)

    def rows(i, _):
        x = pair_ref[pl.ds(i * U, U)].reshape(U * T, C)
        n, _ = pair_norm(x, ones)
        y = (n * gain_ref[...]).astype(bf16)
        for u in range(U):
            low[:, pl.ds(pl.multiple_of((i * U + u) * C, 128), C)] = y[u * T : (u + 1) * T]
        return 0

    if U == G:
        rows(0, 0)
    else:
        lax.fori_loop(0, G // U, rows, 0)
    res = dg(w_ref[...], low[...], NT)
    res = res.reshape(res.shape[0] // G, G, T).astype(bf16)
    H = res.shape[0] // 2
    first_ref[...] = res[:H]
    second_ref[...] = res[H:]


def pair_fwd(pair, gain, w_rows, deps=(), U=8):
    R, T, C = pair.shape
    G = 8
    H = w_rows.shape[0] // G
    return pl.pallas_call(
        functools.partial(pair_fwd_kernel, U),
        grid=(R // G,),
        in_specs=[
            pl.BlockSpec((G, T, C), lambda i: (i, 0, 0)),
            pl.BlockSpec((1, C), lambda i: (0, 0)),
            pl.BlockSpec((H * G, G * C), lambda i: (0, 0)),
        ]
        + [ANY] * len(deps),
        out_specs=[pl.BlockSpec((H // 2, G, T), lambda i: (0, i, 0))] * 2,
        out_shape=[jax.ShapeDtypeStruct((H // 2, R, T), bf16)] * 2,
        scratch_shapes=[pltpu.VMEM((T, G * C), bf16)],
        compiler_params=pltpu.CompilerParams(
            dimension_semantics=("arbitrary",), vmem_limit_bytes=40 << 20
        ),
        cost_estimate=cost(R * T * C * 3150, R * T * C * 3, R * T * C),
        name="pair_fwd",
    )(pair, gain, w_rows, *deps)


def pair_bwd_kernel(P, nd, U, pair_ref, gain_ref, wc_ref, *refs):
    firsts, seconds = refs[:P], refs[P : 2 * P]
    out_ref, gw_ref, acc, turned = refs[2 * P + nd :]
    G, T, C = pair_ref.shape
    H = 2 * firsts[0].shape[0]
    ones = jnp.full((C, C), 1.0 / C, bf16)

    @pl.when(pl.program_id(0) == 0)
    def _():
        acc[...] = jnp.zeros_like(acc)

    halves = []
    for parts in (firsts, seconds):
        total = parts[0][...].astype(f32)
        for p in range(1, P):
            total = total + parts[p][...].astype(f32)
        halves.append(total.reshape(H // 2 * G, T))
    flat = jnp.concatenate(halves, axis=0)
    low8 = flat.astype(bf16)
    cols = low8.T
    turned[:, : H * G] = cols
    turned[:, H * G :] = cols

    def rows(i, _):
        x = pair_ref[pl.ds(i * U, U)].reshape(U * T, C)
        n, inv = pair_norm(x, ones)
        low = (n * gain_ref[...]).astype(bf16)
        gs = []
        for u in range(U):
            acc[i * U + u] += dg(low8, low[u * T : (u + 1) * T], NN)
            gs.append(dg(turned[...], wc_ref[i * U + u], NN))
        g = jnp.concatenate(gs, axis=0) if U > 1 else gs[0]
        mean = dg((g * n).astype(bf16), ones, NN)
        out_ref[pl.ds(i * U, U)] = (inv * (g - n * mean)).astype(bf16).reshape(U, T, C)
        return 0

    if U == G:
        rows(0, 0)
    else:
        lax.fori_loop(0, G // U, rows, 0)

    @pl.when(pl.program_id(0) == pl.num_programs(0) - 1)
    def _():
        at = lax.broadcasted_iota(jnp.int32, (H * G, 1), 0) % G
        picked = jnp.zeros((H * G, C), f32)
        for i in range(G):
            picked = picked + jnp.where(at == i, acc[i], 0.0)
        gw_ref[...] = picked


def pair_bwd(pair, gain, wc, firsts, seconds, deps=(), U=8):
    R, T, C = pair.shape
    G = 8
    H = 2 * firsts[0].shape[0]
    P = len(firsts)
    rows = pl.BlockSpec((G, T, C), lambda i: (i, 0, 0))
    return pl.pallas_call(
        functools.partial(pair_bwd_kernel, P, len(deps), U),
        grid=(R // G,),
        in_specs=[
            rows,
            pl.BlockSpec((1, C), lambda i: (0, 0)),
            pl.BlockSpec((G, 2 * H * G, C), lambda i: (0, 0, 0)),
        ]
        + [pl.BlockSpec((H // 2, G, T), lambda i: (0, i, 0))] * (2 * P)
        + [ANY] * len(deps),
        out_specs=[
            rows,
            pl.BlockSpec((H * G, C), lambda i: (0, 0)),
        ],
        out_shape=[
            jax.ShapeDtypeStruct((R, T, C), bf16),
            jax.ShapeDtypeStruct((H * G, C), f32),
        ],
        scratch_shapes=[
            pltpu.VMEM((G, H * G, C), f32),
            pltpu.VMEM((T, 2 * H * G), bf16),
        ],
        compiler_params=pltpu.CompilerParams(
            dimension_semantics=("arbitrary",), vmem_limit_bytes=50 << 20
        ),
        cost_estimate=cost(R * T * C * 5500, R * T * C * 6, R * T * C),
        name="pair_bwd",
    )(pair, gain, wc, *firsts, *seconds, *deps)


def stats_of(x):
    mean = jnp.mean(x, axis=-1, keepdims=True)
    cen = x - mean
    inv = lax.rsqrt(jnp.mean(cen * cen, axis=-1, keepdims=True) + EPS)
    return cen * inv, inv


def sigmoid(x):
    return 1.0 / (1.0 + jnp.exp(-x))


def flat_rows(x):
    return x.reshape(x.shape[0] * x.shape[1], x.shape[2])


def over_samples(x, sb):
    R = x.shape[0] // sb
    total = x[:R]
    for i in range(1, sb):
        total = total + x[i * R : (i + 1) * R]
    return total


def tile_samples(x, sb):
    return x if sb == 1 else jnp.concatenate([x] * sb, axis=0)


def weight_copies(shapes, F, c, f, own, got, swapped, dst, sems):
    copies = []

    def add(src, to):
        copies.append(pltpu.make_async_copy(src, to, sems.at[len(copies)]))

    for i, (r, n) in enumerate(shapes):
        add(own[i], dst[i].at[pl.ds(pl.multiple_of(f * r, 16), r), :])
    for k in range(1, F):
        for packed, half in ((got[k - 1], c), (swapped[k - 1], 1 - c)):
            at = 0
            for i, (r, n) in enumerate(shapes):
                row = pl.multiple_of((f ^ k) * r, 16)
                for b in range(n // 2 // 384):
                    col = pl.multiple_of(half * (n // 2) + b * 384, 128)
                    add(
                        packed.at[pl.ds(at, r), :],
                        dst[i].at[pl.ds(row, r), pl.ds(col, 384)],
                    )
                    at += padded(r)
    return copies


def gathered_copies(shapes, F, c, got, swapped, dst, sems):
    copies = []
    for g in range(F):
        for packed, half in ((got, c), (swapped, 1 - c)):
            at = 0
            for i, (r, n) in enumerate(shapes):
                for b in range(n // 2 // 384):
                    col = pl.multiple_of(half * (n // 2) + b * 384, 128)
                    copies.append(
                        pltpu.make_async_copy(
                            packed.at[g, pl.ds(at, r), :],
                            dst[i].at[pl.ds(g * r, r), pl.ds(col, 384)],
                            sems.at[len(copies)],
                        )
                    )
                    at += padded(r)
    return copies


def padded(r):
    return -(-r // 16) * 16


def packed_rows(shapes):
    return sum(padded(r) * (n // 2 // 384) for r, n in shapes)


def part_map(p, nu):
    return lambda r, u, s: (jnp.where(r == p, u, jnp.where(r < p, 0, nu - 1)), 0, 0)


def part_specs(F, nu, sb, R, D, buffers=2):
    return [
        pl.BlockSpec((sb, R, D), part_map(p, nu), pipeline_mode=pl.Buffered(buffers))
        for p in range(F)
    ]


def choose(parts, scratch):
    for p, ref in enumerate(parts):

        @pl.when(pl.program_id(0) == p)
        def _(ref=ref):
            scratch[...] = ref[...]

    return flat_rows(scratch[...].astype(f32))


def store_part(parts, value):
    for p, ref in enumerate(parts):

        @pl.when(pl.program_id(0) == p)
        def _(ref=ref):
            ref[...] = value


def copies_in_group(shapes, F):
    return len(shapes) + (F - 1) * 2 * sum(n // 2 // 384 for _, n in shapes)


def pack_grads(shapes, F, c, accs, keep_ref, give_ref, stage=None, sems=None):
    copies = []
    for g in range(F):
        for x in copies:
            x.wait()
        at = 0
        for (r, n), acc in zip(shapes, accs):
            for b in range(n // 2 // 384):
                for i, (ref, half) in enumerate(((keep_ref, c), (give_ref, 1 - c))):
                    col = pl.multiple_of(half * (n // 2) + b * 384, 128)
                    block = acc[g * r : (g + 1) * r, pl.ds(col, 384)].astype(bf16)
                    if stage is None:
                        ref[g, at : at + r, :] = block
                    else:
                        stage[i, at : at + r, :] = block
                at += padded(r)
        if stage is not None:
            copies = [
                pltpu.make_async_copy(stage.at[i], ref.at[g], sems.at[i])
                for i, ref in enumerate((keep_ref, give_ref))
            ]
            for x in copies:
                x.start()
    for x in copies:
        x.wait()


def qkvg_kernel(F, shapes, ids, *refs):
    nin = 2 * (F - 1)
    acts, refs = refs[:F], refs[F:]
    cond_ref, bq_ref, wq_hbm = refs[:3]
    got, swapped = refs[3 : 3 + F - 1], refs[3 + F - 1 : 3 + nin]
    q_ref, k_ref, v_ref, g_ref, token_ref, w, xs, sems = refs[3 + nin :]
    token_ref[...] = jnp.zeros_like(token_ref)
    c, f = ids[F], ids[F + 1]

    @pl.when((pl.program_id(0) == 0) & (pl.program_id(1) == 0))
    def _():
        copies = weight_copies(shapes, F, c, f, (wq_hbm,), got, swapped, (w,), sems)
        for x in copies:
            x.start()
        for x in copies:
            x.wait()

    sb, R, D = xs.shape
    n, _ = stats_of(choose(acts, xs))
    scale = tile_samples(sigmoid(cond_ref[:, :D]), sb)
    shift = tile_samples(cond_ref[:, D : 2 * D], sb)
    x = (scale * n + shift).astype(bf16)
    q_ref[...] = (dg(x, w[:, :D], NN) + bq_ref[...]).astype(bf16).reshape(sb, R, D)
    k_ref[...] = dg(x, w[:, D : 2 * D], NN).astype(bf16).reshape(sb, R, D)
    v_ref[...] = dg(x, w[:, 2 * D : 3 * D], NN).astype(bf16).reshape(sb, R, D)
    g_ref[0] = sigmoid(dg(x, w[:, 3 * D :], NN)).reshape(sb, R, D)


def sub_samples(sl, R):
    sb = max(1, min(sl, 256 // R))
    return sb, sl // sb


def qkvg_call(ids, acts, cond, bq, wq, got, swapped):
    F = len(acts)
    sl, R, D = acts[0].shape
    T = F * R
    sb, nu = sub_samples(sl, R)
    shapes = [wq.shape]
    stacked = pl.BlockSpec((1, sb, R, D), lambda r, u, s: (r, u, 0, 0))
    natural = pl.BlockSpec((sb, R, D), lambda r, u, s: (u, s[r], 0))
    return pl.pallas_call(
        functools.partial(qkvg_kernel, F, shapes),
        grid_spec=pltpu.PrefetchScalarGridSpec(
            num_scalar_prefetch=1,
            grid=(F, nu),
            in_specs=part_specs(F, nu, sb, R, D)
            + [
                pl.BlockSpec((R, 2 * D), lambda r, u, s: (s[r], 0)),
                pl.BlockSpec((1, D), lambda r, u, s: (0, 0)),
            ]
            + [ANY] * (1 + 2 * (F - 1)),
            out_specs=[natural] * 3 + [stacked, pl.BlockSpec((1, 128), lambda r, u, s: (0, 0))],
            scratch_shapes=[
                pltpu.VMEM((D, 4 * D), bf16),
                pltpu.VMEM((sb, R, D), bf16),
                pltpu.SemaphoreType.DMA((copies_in_group(shapes, F),)),
            ],
        ),
        out_shape=[jax.ShapeDtypeStruct((sl, T, D), bf16)] * 3
        + [jax.ShapeDtypeStruct((F, sl, R, D), f32), jax.ShapeDtypeStruct((1, 128), f32)],
        compiler_params=pltpu.CompilerParams(
            dimension_semantics=("arbitrary", "arbitrary"), vmem_limit_bytes=60 << 20
        ),
        cost_estimate=cost(19 * sl * T * D * D, 2 * sl * T * D * 6 + 8 * D * D, sl * T * D),
        name="qkvg",
    )(ids, *acts, cond, bq, wq, *got, *swapped)


def middle_kernel(F, shapes, ids, *refs):
    acts, cots, refs = refs[:F], refs[F : 2 * F], refs[2 * F :]
    mix_a, mix_b, gate_ref, gone_ref, ctwo_ref = refs[:5]
    got, swapped = refs[5:7]
    outs, refs = refs[7 : 7 + F], refs[7 + F :]
    (
        da_ref,
        gpg_ref,
        mg_ref,
        ctg_ref,
        gog_ref,
        keep_ref,
        give_ref,
        wo,
        wab,
        wout,
        ao,
        aab,
        aout,
        xs,
        ys,
        stage,
        sems,
        out_sems,
    ) = refs
    c = ids[F]
    first = (pl.program_id(0) == 0) & (pl.program_id(1) == 0)
    last = (pl.program_id(0) == pl.num_programs(0) - 1) & (
        pl.program_id(1) == pl.num_programs(1) - 1
    )

    @pl.when(first)
    def _():
        copies = gathered_copies(shapes, F, c, got, swapped, (wo, wab, wout), sems)
        for x in copies:
            x.start()
        ao[...] = jnp.zeros_like(ao)
        aab[...] = jnp.zeros_like(aab)
        aout[...] = jnp.zeros_like(aout)
        for x in copies:
            x.wait()

    sb, R, D = xs.shape
    H = wout.shape[0]
    gate = flat_rows(gate_ref[0])
    mix = jnp.concatenate([flat_rows(mix_a[...]), flat_rows(mix_b[...])], axis=1)
    branch = (gate * mix).astype(bf16)
    attn_out = dg(branch, wo[...], NN)
    sig_one = sigmoid(gone_ref[...])
    gate_one = tile_samples(sig_one, sb)
    middle = choose(acts, xs) + gate_one * attn_out
    n, inv = stats_of(middle)
    sig_scale = sigmoid(ctwo_ref[:, :D])
    scale = tile_samples(sig_scale, sb)
    x2 = (scale * n + tile_samples(ctwo_ref[:, D : 2 * D], sb)).astype(bf16)
    up = dg(x2, wab[:, H:], NN)
    gp = dg(x2, wab[:, :H], NN)
    sg = sigmoid(gp)
    silu = gp * sg
    hidden = (silu * up).astype(bf16)
    ffn = dg(hidden, wout[...], NN)
    sig_two = sigmoid(ctwo_ref[:, 2 * D :])
    gate_two = tile_samples(sig_two, sb)
    store_part(outs, (middle + gate_two * ffn).astype(bf16).reshape(sb, R, D))

    upstream = choose(cots, ys)
    fg = (upstream * gate_two).astype(bf16)
    g_two = over_samples(upstream * ffn, sb) * (sig_two * (1.0 - sig_two))
    aout[...] += dg(hidden, fg, TN)
    hg = dg(fg, wout[...], NT)
    ga = (hg * up * sg * (1.0 + gp * (1.0 - sg))).astype(bf16)
    gb = (hg * silu).astype(bf16)
    aab[:, :H] += dg(x2, ga, TN)
    aab[:, H:] += dg(x2, gb, TN)
    xg = dg(ga, wab[:, :H], NT) + dg(gb, wab[:, H:], NT)
    g_scale = over_samples(xg * n, sb) * (sig_scale * (1.0 - sig_scale))
    g_shift = over_samples(xg, sb)
    inc = xg * scale
    mg = upstream + inv * (
        inc
        - jnp.mean(inc, axis=-1, keepdims=True)
        - n * jnp.mean(inc * n, axis=-1, keepdims=True)
    )
    mg_ref[0] = mg.reshape(sb, R, D)
    og = (mg * gate_one).astype(bf16)
    g_one = over_samples(mg * attn_out, sb) * (sig_one * (1.0 - sig_one))
    ao[...] += dg(branch, og, TN)
    bg = dg(og, wo[...], NT)
    da_ref[...] = (bg * gate).astype(bf16).reshape(sb, R, D)
    gpg_ref[0] = (bg * mix * (gate * (1.0 - gate))).astype(bf16).reshape(sb, R, D)

    @pl.when(pl.program_id(1) == 0)
    def _():
        ctg_ref[:, :D] = g_scale
        ctg_ref[:, D : 2 * D] = g_shift
        ctg_ref[:, 2 * D :] = g_two
        gog_ref[...] = g_one

    @pl.when(pl.program_id(1) > 0)
    def _():
        ctg_ref[:, :D] += g_scale
        ctg_ref[:, D : 2 * D] += g_shift
        ctg_ref[:, 2 * D :] += g_two
        gog_ref[...] += g_one

    @pl.when(last)
    def _():
        pack_grads(shapes, F, c, (ao, aab, aout), keep_ref, give_ref, stage, out_sems)


def middle_call(ids, acts, cots, mix_a, mix_b, gate, cond_one, cond_two, shapes, got, swapped):
    F = len(acts)
    sl, R, D = acts[0].shape
    T = F * R
    H = shapes[2][0] * F
    sb, nu = sub_samples(sl, R)
    copies = 2 * F * sum(n // 2 // 384 for _, n in shapes)
    rows = packed_rows(shapes)
    stacked = pl.BlockSpec((1, sb, R, D), lambda r, u, s: (r, u, 0, 0))
    natural = pl.BlockSpec((sb, R, D), lambda r, u, s: (u, s[r], 0))
    lanes = pl.BlockSpec((sb, R, D // 2), lambda r, u, s: (u, s[r], 0))
    flops = 12 * sl * T * D * (D + 3 * H)
    res = pl.pallas_call(
        functools.partial(middle_kernel, F, shapes),
        grid_spec=pltpu.PrefetchScalarGridSpec(
            num_scalar_prefetch=1,
            grid=(F, nu),
            in_specs=part_specs(F, nu, sb, R, D) * 2
            + [
                lanes,
                lanes,
                stacked,
                pl.BlockSpec((R, D), lambda r, u, s: (s[r], 2)),
                pl.BlockSpec((R, 3 * D), lambda r, u, s: (s[r], 0)),
            ]
            + [ANY] * 2,
            out_specs=part_specs(F, nu, sb, R, D)
            + [
                natural,
                stacked,
                stacked,
                pl.BlockSpec((R, 3 * D), lambda r, u, s: (s[r], 0)),
                pl.BlockSpec((R, D), lambda r, u, s: (s[r], 0)),
                ANY,
                ANY,
            ],
            scratch_shapes=[
                pltpu.VMEM((D, D), bf16),
                pltpu.VMEM((D, 2 * H), bf16),
                pltpu.VMEM((H, D), bf16),
                pltpu.VMEM((D, D), f32),
                pltpu.VMEM((D, 2 * H), f32),
                pltpu.VMEM((H, D), f32),
                pltpu.VMEM((sb, R, D), bf16),
                pltpu.VMEM((sb, R, D), bf16),
                pltpu.VMEM((2, rows, 384), bf16),
                pltpu.SemaphoreType.DMA((copies,)),
                pltpu.SemaphoreType.DMA((2,)),
            ],
        ),
        out_shape=[jax.ShapeDtypeStruct((sl, R, D), bf16)] * F
        + [
            jax.ShapeDtypeStruct((sl, T, D), bf16),
            jax.ShapeDtypeStruct((F, sl, R, D), bf16),
            jax.ShapeDtypeStruct((F, sl, R, D), f32),
            jax.ShapeDtypeStruct((T, 3 * D), f32),
            jax.ShapeDtypeStruct((T, D), f32),
            jax.ShapeDtypeStruct((F, rows, 384), bf16),
            jax.ShapeDtypeStruct((F, rows, 384), bf16),
        ],
        compiler_params=pltpu.CompilerParams(
            dimension_semantics=("arbitrary", "arbitrary"), vmem_limit_bytes=63 << 20
        ),
        cost_estimate=cost(flops, sl * T * D * 24, sl * T * H),
        name="middle",
    )(ids, *acts, *cots, mix_a, mix_b, gate, cond_one, cond_two, got, swapped)
    return list(res[:F]), *res[F:]


def back_weight_kernel(F, nd, shapes, ids, *refs):
    acts, refs = refs[:F], refs[F:]
    cond_ref, dq_a, dq_b, dk_a, dk_b, dv_a, dv_b, gpg_ref = refs[:8]
    bq_ref, keep_ref, give_ref, acc, xs = refs[8 + nd :]
    D = acts[0].shape[2]
    first = (pl.program_id(0) == 0) & (pl.program_id(1) == 0)
    last = (pl.program_id(0) == pl.num_programs(0) - 1) & (
        pl.program_id(1) == pl.num_programs(1) - 1
    )

    @pl.when(first)
    def _():
        acc[...] = jnp.zeros_like(acc)
        bq_ref[...] = jnp.zeros_like(bq_ref)

    sb = xs.shape[0]
    n, _ = stats_of(choose(acts, xs))
    scale = tile_samples(sigmoid(cond_ref[:, :D]), sb)
    x = (scale * n + tile_samples(cond_ref[:, D : 2 * D], sb)).astype(bf16)
    for i, refs_i in enumerate(((dq_a, dq_b), (dk_a, dk_b), (dv_a, dv_b))):
        g = jnp.concatenate([flat_rows(y[...]) for y in refs_i], axis=1)
        if i == 0:
            bq_ref[...] += jnp.sum(g, axis=0, keepdims=True)
        acc[:, i * D : (i + 1) * D] += dg(x, g.astype(bf16), TN)
    acc[:, 3 * D :] += dg(x, flat_rows(gpg_ref[0]), TN)

    @pl.when(last)
    def _():
        pack_grads(shapes, F, ids[F], (acc,), keep_ref, give_ref)


def back_data_kernel(F, nd, shapes, cshape, ids, *refs):
    nin = 2 * (F - 1)
    acts, refs = refs[:F], refs[F:]
    cond_ref, dq_a, dq_b, dk_a, dk_b, dv_a, dv_b, gpg_ref, mg_ref = refs[:9]
    s_ref, gog_ref, wc_ref, wq_hbm = refs[9:13]
    got, swapped = refs[13 : 13 + F - 1], refs[13 + F - 1 : 13 + nin]
    ags, refs = refs[13 + nin + nd : 13 + nin + nd + F], refs[13 + nin + nd + F :]
    sg_ref, sum_ref, keep_ref, give_ref, w, cg, acc, xs, sems = refs
    c, f = ids[F], ids[F + 1]
    last = (pl.program_id(0) == pl.num_programs(0) - 1) & (
        pl.program_id(1) == pl.num_programs(1) - 1
    )
    first = (pl.program_id(0) == 0) & (pl.program_id(1) == 0)

    @pl.when(first)
    def _():
        copies = weight_copies(shapes, F, c, f, (wq_hbm,), got, swapped, (w,), sems)
        for x in copies:
            x.start()
        for x in copies:
            x.wait()

    sb, R, D = xs.shape
    n, inv = stats_of(choose(acts, xs))
    sig_scale = sigmoid(cond_ref[:, :D])
    scale = tile_samples(sig_scale, sb)
    xg = dg(flat_rows(gpg_ref[0]), w[:, 3 * D :], NT)
    for i, refs_i in enumerate(((dq_a, dq_b), (dk_a, dk_b), (dv_a, dv_b))):
        g = jnp.concatenate([flat_rows(y[...]) for y in refs_i], axis=1).astype(bf16)
        xg = xg + dg(g, w[:, i * D : (i + 1) * D], NT)
    g_scale = over_samples(xg * n, sb) * (sig_scale * (1.0 - sig_scale))
    g_shift = over_samples(xg, sb)
    inc = xg * scale
    ag = flat_rows(mg_ref[0]) + inv * (
        inc
        - jnp.mean(inc, axis=-1, keepdims=True)
        - n * jnp.mean(inc * n, axis=-1, keepdims=True)
    )
    store_part(ags, ag.astype(bf16).reshape(sb, R, D))

    rows = pl.ds(pl.multiple_of(ids[pl.program_id(0)] * R, 16), R)

    @pl.when(pl.program_id(1) == 0)
    def _():
        cg[rows, :D] = g_scale
        cg[rows, D : 2 * D] = g_shift
        cg[rows, 2 * D :] = gog_ref[rows, :]

    @pl.when(pl.program_id(1) > 0)
    def _():
        cg[rows, :D] += g_scale
        cg[rows, D : 2 * D] += g_shift

    @pl.when(last)
    def _():
        cond_grads(F, cshape, c, s_ref, cg[...], wc_ref, sg_ref, sum_ref, keep_ref, give_ref, acc)


def back_weight(ids, acts, cond, dqkv, gpg, wq_shape, deps=()):
    F = len(acts)
    sl, R, D = acts[0].shape
    T = F * R
    sb, nu = sub_samples(sl, R)
    rows = packed_rows([wq_shape])
    stacked = pl.BlockSpec((1, sb, R, D), lambda r, u, s: (r, u, 0, 0))
    lanes = pl.BlockSpec((sb, R, D // 2), lambda r, u, s: (u, s[r], 0))
    whole = pl.BlockSpec((F, rows, 384), lambda r, u, s: (0, 0, 0), pipeline_mode=pl.Buffered(1))
    return pl.pallas_call(
        functools.partial(back_weight_kernel, F, len(deps), [wq_shape]),
        grid_spec=pltpu.PrefetchScalarGridSpec(
            num_scalar_prefetch=1,
            grid=(F, nu),
            in_specs=part_specs(F, nu, sb, R, D)
            + [pl.BlockSpec((R, 2 * D), lambda r, u, s: (s[r], 0))]
            + [lanes] * 6
            + [stacked]
            + [ANY] * len(deps),
            out_specs=[pl.BlockSpec((1, D), lambda r, u, s: (0, 0)), whole, whole],
            scratch_shapes=[pltpu.VMEM((D, 4 * D), f32), pltpu.VMEM((sb, R, D), bf16)],
        ),
        out_shape=[
            jax.ShapeDtypeStruct((1, D), f32),
            jax.ShapeDtypeStruct((F, rows, 384), bf16),
            jax.ShapeDtypeStruct((F, rows, 384), bf16),
        ],
        compiler_params=pltpu.CompilerParams(
            dimension_semantics=("arbitrary", "arbitrary"), vmem_limit_bytes=60 << 20
        ),
        cost_estimate=cost(17 * sl * T * D * D, sl * T * D * 16 + 12 * D * D, sl * T),
        name="back_weight",
    )(ids, *acts, cond, *dqkv, gpg, *deps)


def back_data(ids, acts, cond, dqkv, gpg, mg, s_low, gog, wc, wq, got, swapped, deps=()):
    F = len(acts)
    sl, R, D = acts[0].shape
    T = F * R
    sb, nu = sub_samples(sl, R)
    shapes = [wq.shape]
    C, N = s_low.shape[1], wc.shape[2]
    cshape = (C // F, N)
    crows = packed_rows([cshape])

    def once(shape):
        return pl.BlockSpec(
            shape, lambda r, u, s: (0,) * len(shape), pipeline_mode=pl.Buffered(1)
        )

    outs = [
        jax.ShapeDtypeStruct((T, C), f32),
        jax.ShapeDtypeStruct((1, N), f32),
        jax.ShapeDtypeStruct((F, crows, 384), bf16),
        jax.ShapeDtypeStruct((F, crows, 384), bf16),
    ]
    stacked = pl.BlockSpec((1, sb, R, D), lambda r, u, s: (r, u, 0, 0))
    lanes = pl.BlockSpec((sb, R, D // 2), lambda r, u, s: (u, s[r], 0))
    res = pl.pallas_call(
        functools.partial(back_data_kernel, F, len(deps), shapes, cshape),
        grid_spec=pltpu.PrefetchScalarGridSpec(
            num_scalar_prefetch=1,
            grid=(F, nu),
            in_specs=part_specs(F, nu, sb, R, D)
            + [pl.BlockSpec((R, 2 * D), lambda r, u, s: (s[r], 0))]
            + [lanes] * 6
            + [stacked, stacked]
            + [once(x.shape) for x in (s_low, gog, wc)]
            + [ANY] * (1 + 2 * (F - 1) + len(deps)),
            out_specs=part_specs(F, nu, sb, R, D) + [once(x.shape) for x in outs],
            scratch_shapes=[
                pltpu.VMEM((D, 4 * D), bf16),
                pltpu.VMEM((T, N), f32),
                pltpu.VMEM((C, N), f32),
                pltpu.VMEM((sb, R, D), bf16),
                pltpu.SemaphoreType.DMA((copies_in_group(shapes, F),)),
            ],
        ),
        out_shape=[jax.ShapeDtypeStruct((sl, R, D), bf16)] * F + outs,
        compiler_params=pltpu.CompilerParams(
            dimension_semantics=("arbitrary", "arbitrary"), vmem_limit_bytes=60 << 20
        ),
        cost_estimate=cost(17 * sl * T * D * D, sl * T * D * 22 + 8 * D * D, sl * T),
        name="back_data",
    )(ids, *acts, cond, *dqkv, gpg, mg, s_low, gog, wc, wq, *got, *swapped, *deps)
    return list(res[:F]), *res[F:]


def prepare_kernel(F, nd, groups, ids, *refs):
    xs, refs = refs[:F], refs[F:]
    weights = sum(len(g) for g in groups)
    ws, refs = list(refs[:weights]), refs[weights + nd :]
    for x, out in zip(xs, refs):
        out[...] = x[...]

    @pl.when(pl.program_id(0) == 0)
    def _():
        for shapes, packed in zip(groups, refs[F:]):
            at = 0
            for r, n in shapes:
                w = ws.pop(0)
                for b in range(n // 2 // 384):
                    col = pl.multiple_of(ids[F] * (n // 2) + b * 384, 128)
                    packed[at : at + r, :] = w[:, pl.ds(col, 384)]
                    at += padded(r)


def prepare(ids, x, groups=(), deps=()):
    S, R, D = x.shape
    F = (ids.shape[0] - 2) // 3
    sl = S // F
    steps = 4
    shapes = [[w.shape for w in g] for g in groups]
    rows = [packed_rows(s) for s in shapes]

    def group(p):
        return pl.BlockSpec((sl, R // steps, D), lambda i, s: (s[2 * F + 2 + p], i, 0))

    part = pl.BlockSpec((sl, R // steps, D), lambda i, s: (0, i, 0))
    weights = [w for g in groups for w in g]
    res = pl.pallas_call(
        functools.partial(prepare_kernel, F, len(deps), shapes),
        grid_spec=pltpu.PrefetchScalarGridSpec(
            num_scalar_prefetch=1,
            grid=(steps,),
            in_specs=[group(p) for p in range(F)]
            + [pl.BlockSpec(w.shape, lambda i, s: (0, 0)) for w in weights]
            + [ANY] * len(deps),
            out_specs=[part] * F + [pl.BlockSpec((n, 384), lambda i, s: (0, 0)) for n in rows],
        ),
        out_shape=[jax.ShapeDtypeStruct((sl, R, D), x.dtype)] * F
        + [jax.ShapeDtypeStruct((n, 384), bf16) for n in rows],
        compiler_params=pltpu.CompilerParams(
            dimension_semantics=("arbitrary",), vmem_limit_bytes=40 << 20
        ),
        cost_estimate=cost(5e9, S * R * D * 4),
        name="prepare",
    )(ids, *([x] * F), *weights, *deps)
    return list(res[:F]), *res[F:]


def place_kernel(F, ids, *refs):
    parts, out = refs[:F], refs[-1]
    for p, ref in enumerate(parts):

        @pl.when(pl.program_id(0) == p)
        def _(ref=ref):
            out[...] = ref[...]


def place(ids, parts, deps=()):
    F = len(parts)
    sl, R, D = parts[0].shape

    def fetch(p):
        return pl.BlockSpec((sl, R, D), lambda i, s: (0, 0, 0), pipeline_mode=pl.Buffered(1))

    return pl.pallas_call(
        functools.partial(place_kernel, F),
        grid_spec=pltpu.PrefetchScalarGridSpec(
            num_scalar_prefetch=1,
            grid=(F,),
            in_specs=[fetch(p) for p in range(F)] + [ANY] * len(deps),
            out_specs=pl.BlockSpec((sl, R, D), lambda i, s: (s[2 * F + 2 + i], 0, 0)),
        ),
        out_shape=jax.ShapeDtypeStruct((F * sl, R, D), parts[0].dtype),
        compiler_params=pltpu.CompilerParams(
            dimension_semantics=("arbitrary",), vmem_limit_bytes=40 << 20
        ),
        cost_estimate=cost(4e9, F * sl * R * D * 4),
        name="place",
    )(ids, *parts, *deps)


def terms_kernel(F, n, ids, *refs):
    outs = refs[-F:]
    for p in range(F):

        @pl.when(pl.program_id(0) == p)
        def _(p=p):
            at = 0
            for own, got in zip(refs[:n], refs[n : 2 * n]):
                rows = own.shape[1]
                outs[p][at : at + rows, :] = (own[0].astype(f32) + got[0].astype(f32)).astype(bf16)
                at += rows


def terms(ids, keeps, gots, deps=()):
    F, _, W = keeps[0].shape
    rows = sum(x.shape[1] for x in keeps)
    shards = [
        pl.BlockSpec((1, x.shape[1], W), lambda k, s: (s[F + 1] ^ k, 0, 0)) for x in keeps
    ]
    out = pl.BlockSpec((rows, W), lambda k, s: (0, 0), pipeline_mode=pl.Buffered(1))
    return pl.pallas_call(
        functools.partial(terms_kernel, F, len(keeps)),
        grid_spec=pltpu.PrefetchScalarGridSpec(
            num_scalar_prefetch=1,
            grid=(F,),
            in_specs=shards * 2 + [ANY] * len(deps),
            out_specs=[out] * F,
        ),
        out_shape=[jax.ShapeDtypeStruct((rows, W), bf16)] * F,
        compiler_params=pltpu.CompilerParams(
            dimension_semantics=("arbitrary",), vmem_limit_bytes=40 << 20
        ),
        cost_estimate=cost(5e9, F * rows * W * 6),
        name="terms",
    )(ids, *keeps, *gots, *deps)


def cond_grads(F, shape, c, s_ref, cg, w_ref, sg_ref, sum_ref, keep_ref, give_ref, acc):
    sum_ref[...] = jnp.sum(cg, axis=0, keepdims=True)
    low = cg.astype(bf16)
    acc[...] = dg(s_ref[...], low, TN)
    r = shape[0]
    sg_ref[...] = jnp.concatenate([dg(low, w_ref[g, :r, :], NT) for g in range(F)], axis=1)
    pack_grads([shape], F, c, (acc,), keep_ref, give_ref)


def cond_back_kernel(F, shape, ids, s_ref, cg_ref, w_ref, *refs):
    sg_ref, sum_ref, keep_ref, give_ref, acc = refs[-5:]
    cond_grads(
        F, shape, ids[F], s_ref, cg_ref[...], w_ref, sg_ref, sum_ref, keep_ref, give_ref, acc
    )


def cond_back(ids, s_low, cg, w, F, deps=()):
    T, C = s_low.shape
    N = cg.shape[1]
    shape = (C // F, N)
    rows = packed_rows([shape])
    vmem = pl.BlockSpec(memory_space=pltpu.VMEM)
    return pl.pallas_call(
        functools.partial(cond_back_kernel, F, shape),
        in_specs=[pl.BlockSpec(memory_space=pltpu.SMEM)] + [vmem] * 3 + [ANY] * len(deps),
        out_specs=[vmem] * 4,
        out_shape=[
            jax.ShapeDtypeStruct((T, C), f32),
            jax.ShapeDtypeStruct((1, N), f32),
            jax.ShapeDtypeStruct((F, rows, 384), bf16),
            jax.ShapeDtypeStruct((F, rows, 384), bf16),
        ],
        scratch_shapes=[pltpu.VMEM((C, N), f32)],
        compiler_params=pltpu.CompilerParams(vmem_limit_bytes=50 << 20),
        cost_estimate=cost(8e9, T * N * 4),
        name="cond_back",
    )(ids, s_low, cg, w, *deps)


def unpack_kernel(groups, ids_c, *refs):
    n = len(groups)
    c = ids_c[0]
    outs = list(refs[2 * n :])
    for i, shapes in enumerate(groups):
        at = 0
        for r, cols in shapes:
            out = outs.pop(0)
            for b in range(cols // 2 // 384):
                for ref, half in ((refs[2 * i], c), (refs[2 * i + 1], 1 - c)):
                    col = pl.multiple_of(half * (cols // 2) + b * 384, 128)
                    out[:, pl.ds(col, 384)] = ref[at : at + r, :].astype(f32)
                at += padded(r)


def unpack(c, groups):
    vmem = pl.BlockSpec(memory_space=pltpu.VMEM)
    shapes = [s for _, _, g in groups for s in g]
    return pl.pallas_call(
        functools.partial(unpack_kernel, [g for _, _, g in groups]),
        in_specs=[pl.BlockSpec(memory_space=pltpu.SMEM)] + [vmem] * (2 * len(groups)),
        out_specs=[vmem] * len(shapes),
        out_shape=[jax.ShapeDtypeStruct(s, f32) for s in shapes],
        compiler_params=pltpu.CompilerParams(vmem_limit_bytes=40 << 20),
        cost_estimate=cost(5e9, sum(r * n for r, n in shapes) * 6),
        name="unpack",
    )(c.reshape(1).astype(jnp.int32), *[x for a, b, _ in groups for x in (a, b)])


def cond_fwd_kernel(F, shape, at, natural, ids, single_ref, gain_ref, bias_ref, *refs):
    r, n = shape
    refs, (s_ref, cond_ref, w) = refs[:-3], refs[-3:]
    c, f = ids[F], ids[F + 1]
    step = padded(r)

    def put(g, packed, half):
        for b in range(n // 2 // 384):
            col = pl.multiple_of(half * (n // 2) + b * 384, 128)
            w[g, :r, pl.ds(col, 384)] = packed(at + b * step)

    if natural:
        for g in range(F):
            for ref, half in zip(refs, (c, 1 - c)):
                put(g, lambda row, ref=ref, g=g: ref[g, row : row + r, :], half)
    else:
        w[f, :r, :] = refs[0][...]
        for k in range(1, F):
            for ref, half in ((refs[k], c), (refs[F - 1 + k], 1 - c)):
                put(f ^ k, lambda row, ref=ref: ref[row : row + r, :], half)
    x, _ = stats_of(single_ref[...])
    s_ref[...] = (x * gain_ref[...]).astype(bf16)
    total = bias_ref[...]
    for g in range(F):
        total = total + dg(s_ref[:, g * r : (g + 1) * r], w[g, :r, :], NN)
    cond_ref[...] = total


def cond_fwd(ids, single, gain, bias, shape, at, arrays, natural):
    T, C = single.shape
    r, n = shape
    F = C // r
    vmem = pl.BlockSpec(memory_space=pltpu.VMEM)
    return pl.pallas_call(
        functools.partial(cond_fwd_kernel, F, shape, at, natural),
        in_specs=[pl.BlockSpec(memory_space=pltpu.SMEM)] + [vmem] * (3 + len(arrays)),
        out_specs=[vmem] * 3,
        out_shape=[
            jax.ShapeDtypeStruct((T, C), bf16),
            jax.ShapeDtypeStruct((T, n), f32),
            jax.ShapeDtypeStruct((F, padded(r), n), bf16),
        ],
        compiler_params=pltpu.CompilerParams(vmem_limit_bytes=60 << 20),
        cost_estimate=cost(6e9, T * n * 4),
        name="cond_fwd",
    )(ids, single, gain, bias, *arrays)


class Net:
    def __init__(self, dp, fsdp):
        self.Z, self.F, self.Fh = dp // 2, fsdp, fsdp // 2
        self.z, self.c = lax.axis_index("z"), lax.axis_index("core")
        self.f = lax.axis_index("fsdp")
        self.fh, self.fl = self.f // self.Fh, self.f % self.Fh
        r = jnp.arange(self.F, dtype=jnp.int32)
        blocks = (self.c ^ (r % 2)) * self.Fh + (self.fl ^ (r // 2))
        rows = ((self.c + r // self.Fh) % 2) * self.Fh + (self.fl ^ (r % self.Fh))
        groups = (self.fl ^ (r // 2)) * 2 + (self.fh ^ (r % 2))
        self.ids = jnp.concatenate(
            [blocks, jnp.stack([self.c, self.f]), rows, groups]
        ).astype(jnp.int32)

    def send(self, x, fn):
        F = self.F
        pairs = []
        for z in range(self.Z):
            for c in range(2):
                for f in range(F):
                    z2, c2, f2 = fn(z, c, f)
                    pairs.append(((z * 2 + c) * F + f, (z2 * 2 + c2) * F + f2))
        others = [p for p in pairs if p[0] != p[1]]
        got = lax.ppermute(x, ("z", "core", "fsdp"), others)
        return got if len(others) == len(pairs) else jnp.where(self.c == self.fh, x, got)

    def core_swap(self, x):
        return self.send(x, lambda z, c, f: (z, 1 - c, f))

    def to_owner(self, x, a):
        Fh = self.Fh
        return self.send(x, lambda z, c, f: (z, f // Fh, c * Fh + ((f % Fh) ^ a)))

    def exchange_in(self, parts):
        Fh = self.Fh
        return [
            self.send(
                p,
                lambda z, c, f: (z, (f // Fh) ^ (i % 2), c * Fh + ((f % Fh) ^ (i // 2))),
            )
            for i, p in enumerate(parts)
        ]

    def exchange_out(self, parts):
        Fh = self.Fh
        return [
            self.send(
                p,
                lambda z, c, f: (z, f // Fh, (c ^ (i % 2)) * Fh + ((f % Fh) ^ (i // 2))),
            )
            for i, p in enumerate(parts)
        ]

    def gather_rows(self, x):
        own = [self.to_owner(x, a) for a in range(self.Fh)]
        return own + [self.core_swap(p) for p in own]

    def chip_sum(self, parts):
        Fh = self.Fh
        out = []
        for a in range(Fh):
            got = self.core_swap(parts[Fh + a])
            out.append((parts[a].astype(f32) + got.astype(f32)).astype(got.dtype))
        return out

    def to_owners(self, parts):
        return [self.to_owner(p, a) for a, p in enumerate(parts)]

    def gather_packed(self, packed, *held):
        F = self.F
        got = [self.send(packed, lambda z, c, f: (z, c, f ^ k)) for k in range(1, F)]
        got, *held = tie(got, *held)
        return got, [self.core_swap(g) for g in got], *held

    def plane_send(self, parts):
        return list(parts[:1]) + [
            self.send(parts[k], lambda z, c, f: (z, c, f ^ k)) for k in range(1, self.F)
        ]

    def all_steps(self):
        pairs = [lambda z, c, f: (z, 1 - c, f)]
        bit = 1
        while bit < self.F:
            pairs.append(lambda z, c, f, bit=bit: (z, c, f ^ bit))
            bit *= 2
        bit = 1
        while bit < self.Z:
            pairs.append(lambda z, c, f, bit=bit: (z ^ bit, c, f))
            bit *= 2
        return [lambda x, fn=fn: x + self.send(x, fn) for fn in pairs]

    def z_steps(self):
        def add(x, bit):
            got = self.send(x, lambda z, c, f: (z ^ bit, c, f))
            return (x.astype(f32) + got.astype(f32)).astype(bf16)

        steps, bit = [], 1
        while bit < self.Z:
            steps.append(functools.partial(add, bit=bit))
            bit *= 2
        return steps + [lambda x: (x, self.core_swap(x))]


def total_of(parts):
    return functools.reduce(jnp.add, [p.astype(f32) for p in parts])


def lockstep(*lanes):
    values = [v for v, _ in lanes]
    for i in range(max(len(steps) for _, steps in lanes)):
        values = [steps[i](v) if i < len(steps) else v for v, (_, steps) in zip(values, lanes)]
        values = tie(*values)
    return values


def tie(*xs):
    return lax.optimization_barrier(xs)


def body(
    dp,
    fsdp,
    act,
    single,
    pair,
    segment,
    padding,
    cotangent,
    gain_s1,
    w_cond1,
    b_cond1,
    w_qkvg,
    b_q,
    gain_z,
    w_pair,
    w_o,
    gain_s2,
    w_cond2,
    b_cond2,
    w_ab,
    w_out,
):
    net = Net(dp, fsdp)
    F, ids = net.F, net.ids
    act, single, pair, segment, padding, cotangent = (
        x[0] for x in (act, single, pair, segment, padding, cotangent)
    )
    S, R, D = act.shape
    T = R * F
    COND = single.shape[1]

    vecs = [gain_s1, b_cond1, b_q, gain_z, w_pair, gain_s2, b_cond2]
    sizes = [v.size for v in vecs]
    COND = single.shape[1]
    wide = COND + 128
    vrows = -(-sum(sizes) // (8 * wide)) * 8
    flat = jnp.concatenate([v.reshape(-1) for v in vecs]).astype(f32)
    flat = jnp.pad(flat, (0, vrows * wide - flat.shape[0])).reshape(vrows, wide)
    tag = jnp.where(padding == 1, -1, segment)
    cols = jnp.stack([segment.astype(f32), tag.astype(f32)], axis=1)
    table = jnp.concatenate([single, jnp.pad(cols, ((0, 0), (0, 126)))], axis=1)
    table = jnp.concatenate([table, flat], axis=0)
    table = lax.all_gather(table, ("core", "fsdp"))
    mid_weights = [w_o, w_ab, w_out, w_cond2]
    mid_shapes = [w.shape for w in mid_weights]
    acts, packed, mid_packed = prepare(ids, act, [[w_qkvg, w_cond1], mid_weights])
    acts = net.exchange_in(acts)
    share = mid_packed.shape[0] // net.Z
    mid_got = lax.dynamic_slice_in_dim(mid_packed, net.z * share, share, 0)
    table, mid_got = tie(table, mid_got)
    mid_got = lax.all_gather(mid_got, ("fsdp", "z")).reshape(F, net.Z * share, 384)

    table = lax.dynamic_slice_in_dim(table, net.fh * F, F, 0)
    single_all = table[:, :R, :COND].reshape(T, COND)
    seg_col = table[:, :R, COND].reshape(T, 1)
    tag_row = table[:, :R, COND + 1].reshape(1, T)
    smalls = table[:, R:].reshape(F, vrows * wide)
    full, at = [], 0
    for v, n in zip(vecs, sizes):
        full.append(smalls[:, at : at + n].reshape((F * v.shape[0],) + v.shape[1:]))
        at += n
    gs1, bc1, bq, gz, wp, gs2, bc2 = full

    wt = wp.T
    eye = jnp.eye(8, dtype=f32)
    w_rows = (wt[:, None, None, :] * eye[None, :, :, None]).reshape(HEADS * 8, -1).astype(bf16)
    gz_row = gz.reshape(1, -1)
    bias_a, bias_b = pair_fwd(pair, gz_row, w_rows)
    acts, packed, bias_a, bias_b = tie(acts, packed, bias_a, bias_b)
    one_got, one_swapped, bias_a, bias_b = net.gather_packed(packed, bias_a, bias_b)
    bias_a, bias_b = net.gather_rows(bias_a), net.gather_rows(bias_b)

    single_first, cond_one, wc1 = cond_fwd(
        ids,
        single_all,
        gs1.reshape(1, -1),
        bc1.reshape(1, -1),
        w_cond1.shape,
        packed_rows([w_qkvg.shape]),
        [w_cond1, *one_got, *one_swapped],
        False,
    )
    q, k, v, gate, token = qkvg_call(
        ids, acts, cond_one, bq.reshape(1, D), w_qkvg, one_got, one_swapped
    )

    cots = net.exchange_in(prepare(ids, cotangent, deps=[token])[0])
    mix_a, lse_a = attn_fwd(ids, seg_col, tag_row, q, k, v, bias_a, 0)
    mid_got, mix_a = tie(mid_got, mix_a)
    mid_swapped = net.core_swap(mid_got)
    mix_b, lse_b = attn_fwd(ids, seg_col, tag_row, q, k, v, bias_b, 1)
    single_second, cond_two, wc2 = cond_fwd(
        ids,
        single_all,
        gs2.reshape(1, -1),
        bc2.reshape(1, -1),
        w_cond2.shape,
        packed_rows(mid_shapes[:3]),
        [mid_got, mid_swapped],
        True,
    )
    outs, d_attn, gate_proj, mid_grad, cond_two_grad, gate_one_grad, keep, give = middle_call(
        ids, acts, cots, mix_a, mix_b, gate, cond_one, cond_two, mid_shapes[:3], mid_got, mid_swapped
    )
    outs = net.exchange_out(outs)
    got = net.core_swap(give)
    s_two_grad, grad_b_cond2, keep_c, give_c = cond_back(ids, single_second, cond_two_grad, wc2, F)
    got_c = net.core_swap(give_c)
    mid_sum = []
    for x, y in ((keep, got), (keep_c, got_c)):
        x = (x.astype(f32) + y.astype(f32)).astype(bf16)
        mid_sum.append(jnp.swapaxes(x.reshape(F, net.Z, x.shape[1] // net.Z, 384), 0, 1))
    mid_sum = jnp.concatenate(mid_sum, axis=2)

    dq_a, dk_a, dv_a, db_a = attn_bwd(
        ids, seg_col, tag_row, q, k, v, d_attn, lse_a, bias_a, 0, deps=[mid_sum]
    )
    mid_sum = lax.psum_scatter(mid_sum, "z", scatter_dimension=0)
    outs, db_a = tie(outs, db_a)
    db_a = net.chip_sum(db_a)
    dq_b, dk_b, dv_b, db_b = attn_bwd(
        ids, seg_col, tag_row, q, k, v, d_attn, lse_b, bias_b, 1, deps=db_a
    )
    db_a, db_b, mid_sum = tie(net.to_owners(db_a), db_b, mid_sum)
    db_b = net.chip_sum(db_b)
    mid_sum = net.plane_send(
        [lax.dynamic_index_in_dim(mid_sum, net.f ^ k_, 0, keepdims=False) for k_ in range(F)]
    )
    dqkv = (dq_a, dq_b, dk_a, dk_b, dv_a, dv_b)
    bq_grad, keep, give = back_weight(
        ids, acts, cond_one, dqkv, gate_proj, w_qkvg.shape, deps=db_b
    )
    db_b, give, mid_sum = tie(net.to_owners(db_b), give, mid_sum)
    mid_sum = lax.all_gather(total_of(mid_sum).astype(bf16), "z", axis=0)
    block_out = place(ids, outs, deps=[give])
    wq_parts = terms(ids, [keep], [net.core_swap(give)], deps=[block_out])
    ags, s_one_grad, grad_b_cond1, keep, give = back_data(
        ids,
        acts,
        cond_one,
        dqkv,
        gate_proj,
        mid_grad,
        single_first,
        gate_one_grad,
        wc1,
        w_qkvg,
        one_got,
        one_swapped,
        deps=wq_parts[:1],
    )
    wq_parts, keep, give, ags = tie(net.plane_send(wq_parts), keep, give, ags)
    wq_sum = lax.psum(total_of(wq_parts).astype(bf16), "z")
    late_parts = terms(ids, [keep], [net.core_swap(give)])
    ags = net.exchange_out(ags)

    wc = wt * gz_row
    wc = wc - jnp.mean(wc, axis=1, keepdims=True)
    wc = (wc[None, :, None, :] * eye[:, None, :, None]).reshape(8, HEADS * 8, -1)
    wc_hi = wc.astype(bf16)
    wc = jnp.concatenate([wc_hi, (wc - wc_hi.astype(f32)).astype(bf16)], axis=1)
    pair_grad, gw = pair_bwd(pair, gz_row, wc, db_a, db_b, deps=late_parts[:1])
    late_parts, gw, s_one_grad, mid_sum, wq_sum, ags = tie(
        late_parts, gw, s_one_grad, mid_sum, wq_sum, ags
    )

    s_grad = s_one_grad * gs1 + s_two_grad * gs2
    s_parts = [
        lax.dynamic_slice_in_dim(s_grad, ids[F + 2 + p] * R, R, 0) for p in range(F)
    ]
    flat = [grad_b_cond1, bq_grad, grad_b_cond2, jnp.sum(gw.reshape(HEADS, 8, -1), axis=1)]
    flat = jnp.concatenate([g.reshape(-1, 128) for g in flat], axis=0)
    shares = [packed_rows(mid_shapes[:3]) // net.Z, packed_rows(mid_shapes[3:]) // net.Z]
    mid_sum = jnp.concatenate(
        [mid_sum[:, : shares[0]].reshape(-1, 384), mid_sum[:, shares[0] :].reshape(-1, 384)], axis=0
    )
    late_sum, flat, s_parts, mid_sum, wq_sum = lockstep(
        (late_parts, [lambda x: total_of(net.plane_send(x)).astype(bf16)] + net.z_steps()),
        (flat, net.all_steps()),
        (s_parts, [net.chip_sum, net.to_owners]),
        (mid_sum, [lambda x: (x, net.core_swap(x))]),
        (wq_sum, [lambda x: (x, net.core_swap(x))]),
    )
    total_wo, total_wab, total_wout, total_wc2, total_wq = unpack(
        net.c, [(*mid_sum, mid_shapes), (*wq_sum, [w_qkvg.shape])]
    )
    (total_wc1,) = unpack(net.c, [(*late_sum, [w_cond1.shape])])
    local_n, local_inv = norm_stats(single)
    single_grad = norm_back(local_n, local_inv, functools.reduce(jnp.add, s_parts))[None]
    grad_w_pair = flat[-HEADS:].T
    grad_gain_z = jnp.sum(wp * grad_w_pair, axis=1) / gz
    small, at = [], 0
    for n in (3 * D, D, 3 * D):
        small.append(flat[at // 128 : (at + n) // 128].reshape(-1))
        at += n
    small = [*small[:2], grad_gain_z, grad_w_pair, small[2]]
    total_bc1, total_bq, total_gz, total_wp, total_bc2 = (
        lax.dynamic_slice_in_dim(g, net.f * v_.shape[0], v_.shape[0], 0)
        for g, v_ in zip(small, [b_cond1, b_q, gain_z, w_pair, b_cond2])
    )
    total_gs1, total_gs2 = (
        jnp.sum(w.astype(f32) * g, axis=1) / gain.astype(f32)
        for w, g, gain in ((w_cond1, total_wc1, gain_s1), (w_cond2, total_wc2, gain_s2))
    )
    return (
        block_out[None],
        place(ids, ags, deps=[gw])[None],
        single_grad,
        pair_grad[None],
        total_gs1,
        total_wc1,
        total_bc1,
        total_wq,
        total_bq,
        total_gz,
        total_wp,
        total_wo,
        total_gs2,
        total_wc2,
        total_bc2,
        total_wab,
        total_wout,
    )


def solution(mesh):
    dp, fsdp = mesh.shape["dp"], mesh.shape["fsdp"]
    split = Mesh(mesh.devices.reshape(dp // 2, 2, fsdp), ("z", "core", "fsdp"))
    return jax.shard_map(
        functools.partial(body, dp, fsdp),
        mesh=split,
        in_specs=(
            P(("z", "core"), None, "fsdp", None),
            P(("z", "core"), "fsdp", None),
            P(("z", "core"), "fsdp", None, None),
            P(("z", "core"), "fsdp"),
            P(("z", "core"), "fsdp"),
            P(("z", "core"), None, "fsdp", None),
            P("fsdp"),
            P("fsdp", None),
            P("fsdp"),
            P("fsdp", None),
            P("fsdp"),
            P("fsdp"),
            P("fsdp", None),
            P("fsdp", None),
            P("fsdp"),
            P("fsdp", None),
            P("fsdp"),
            P("fsdp", None),
            P("fsdp", None),
        ),
        out_specs=(
            P(("z", "core"), None, "fsdp", None),
            P(("z", "core"), None, "fsdp", None),
            P(("z", "core"), "fsdp", None),
            P(("z", "core"), "fsdp", None, None),
            P("fsdp"),
            P("fsdp", None),
            P("fsdp"),
            P("fsdp", None),
            P("fsdp"),
            P("fsdp"),
            P("fsdp", None),
            P("fsdp", None),
            P("fsdp"),
            P("fsdp", None),
            P("fsdp"),
            P("fsdp", None),
            P("fsdp", None),
        ),
        check_vma=False,
    )
```

```python
import functools

import jax
import jax.numpy as jnp
from jax import lax
from jax.experimental import pallas as pl
from jax.experimental.pallas import tpu as pltpu
from jax.sharding import Mesh
from jax.sharding import PartitionSpec as P

HEADS = 16
HEAD = 48
FF = 1536
EPS = 1e-05
LOG2E = 1.4426950408889634
NEG = -1000000000.0
f32 = jnp.float32
bf16 = jnp.bfloat16
NT = (((1,), (1,)), ((), ()))
NN = (((1,), (0,)), ((), ()))
TN = (((0,), (0,)), ((), ()))


def norm_stats(values):
    average = jnp.mean(values, axis=-1, keepdims=True)
    centred = values - average
    inverse = lax.rsqrt(jnp.mean(centred * centred, axis=-1, keepdims=True) + EPS)
    return (centred * inverse, inverse)


def norm_back(normed, inverse, incoming):
    return inverse * (
        incoming
        - jnp.mean(incoming, axis=-1, keepdims=True)
        - normed * jnp.mean(incoming * normed, axis=-1, keepdims=True)
    )


def sig_slope(values):
    sigma_val = jax.nn.sigmoid(values)
    return sigma_val * (1.0 - sigma_val)


def dg(a, b, dims):
    return lax.dot_general(a, b, dims, preferred_element_type=f32)


def cost(flops, nbytes, trans=0):
    return pl.CostEstimate(flops=int(flops), bytes_accessed=int(nbytes), transcendentals=int(trans))


ANY = pl.BlockSpec(memory_space=pl.ANY)


def head_window(h, D):
    tile = jnp.minimum((h * HEAD) // 128, D // 128 - 2)
    return pl.multiple_of(tile * 128, 128), h * HEAD - tile * 128


def masked_bias(F, ids, seg_ref, tag_ref, parts, bm):
    for p in range(F):
        R = parts[p].shape[1]
        row = pl.multiple_of(ids[F + 2 + p] * R, 16)
        bm[pl.ds(row, R), :] = jnp.where(
            seg_ref[pl.ds(row, R), :] == tag_ref[...], parts[p][0].astype(f32) * LOG2E, -jnp.inf
        )


def head_scores(q, k, bm):
    s = dg(q, k, NT)
    return jnp.where(bm > -jnp.inf, s * (HEAD**-0.5 * LOG2E) + bm, NEG * LOG2E)


def attn_fwd_kernel(F, nd, RB, ids, seg_ref, tag_ref, q_ref, k_ref, v_ref, *refs):
    parts = refs[:F]
    o_ref, lse_ref, bm = refs[F + nd :]
    Sl, T, D = q_ref.shape
    h = pl.program_id(0)

    @pl.when(h == 0)
    def _():
        o_ref[...] = jnp.zeros_like(o_ref)
        lse_ref[...] = jnp.zeros_like(lse_ref)

    start, off = head_window(h, D)
    masked_bias(F, ids, seg_ref, tag_ref, parts, bm)
    lane = lax.broadcasted_iota(jnp.int32, (1, 256), 1)
    mine = (lane >= off) & (lane < off + HEAD)
    column = lax.broadcasted_iota(jnp.int32, (1, 128), 1) == h
    win = pl.ds(start, 256)

    def sample(s, _):
        kw = k_ref[s, :, win]
        vw = v_ref[s, :, win]
        vw = jnp.where(mine, vw, jnp.zeros_like(vw))
        for r in range(0, T, RB):
            rows = pl.ds(r, RB)
            qw = q_ref[s, rows, win]
            sc = head_scores(jnp.where(mine, qw, jnp.zeros_like(qw)), kw, bm[rows, :])
            m = jnp.max(sc, axis=-1, keepdims=True)
            p = jnp.exp2(sc - m)
            l = jnp.sum(p, axis=-1, keepdims=True)
            o_ref[s, rows, win] += dg(p.astype(bf16), vw, NN) * (1.0 / l)
            lse_ref[s, rows, :] = jnp.where(column, m + jnp.log2(l), lse_ref[s, rows, :])
        return 0

    lax.fori_loop(0, Sl, sample, 0, unroll=min(Sl, 4))


def resident(shape, last=0):
    at = (0,) * (len(shape) - 1) + (last,)
    return pl.BlockSpec(shape, lambda h, s: at, pipeline_mode=pl.Buffered(1))


def attn_fwd(ids, seg, tag, q, k, v, parts, group, deps=()):
    Sl, T, D = q.shape
    F = len(parts)
    H, R = parts[0].shape[:2]
    W = H * HEAD
    lanes = resident((Sl, T, W), group)
    part = pl.BlockSpec((1, R, T), lambda h, s: (h, 0, 0))
    outs = [jax.ShapeDtypeStruct((Sl, T, W), f32), jax.ShapeDtypeStruct((Sl, T, 128), f32)]
    return pl.pallas_call(
        functools.partial(attn_fwd_kernel, F, len(deps), min(T, 256)),
        grid_spec=pltpu.PrefetchScalarGridSpec(
            num_scalar_prefetch=1,
            grid=(H,),
            in_specs=[resident(seg.shape), resident(tag.shape), lanes, lanes, lanes]
            + [part] * F
            + [ANY] * len(deps),
            out_specs=[resident(x.shape) for x in outs],
            scratch_shapes=[pltpu.VMEM((T, T), f32)],
        ),
        out_shape=outs,
        compiler_params=pltpu.CompilerParams(
            dimension_semantics=("arbitrary",), vmem_limit_bytes=60 << 20
        ),
        cost_estimate=cost(Sl * H * T * T * 3700, Sl * T * W * 10 + H * T * T * 2, Sl * H * T * T),
        name="attn_fwd",
    )(ids, seg, tag, q, k, v, *parts, *deps)


def attn_bwd_kernel(F, nd, RB, ids, seg_ref, tag_ref, q_ref, k_ref, v_ref, do_ref, lse_ref, *refs):
    parts, refs = refs[:F], refs[nd:]
    dq_ref, dk_ref, dv_ref = refs[F : F + 3]
    db_refs = refs[F + 3 : F + 3 + F]
    bm, dbacc, pb, dsb, qt, dot, dkt, dvt = refs[F + 3 + F :]
    Sl, T, D = q_ref.shape
    h = pl.program_id(0)

    @pl.when(h == 0)
    def _():
        dq_ref[...] = jnp.zeros_like(dq_ref)

        def turn(s, _):
            qt[s] = q_ref[s].T
            dot[s] = do_ref[s].T
            return 0

        lax.fori_loop(0, Sl, turn, 0)

    start, off = head_window(h, D)
    masked_bias(F, ids, seg_ref, tag_ref, parts, bm)
    lane = lax.broadcasted_iota(jnp.int32, (1, 256), 1)
    mine = (lane >= off) & (lane < off + HEAD)
    column = lax.broadcasted_iota(jnp.int32, (1, 128), 1) == h
    win = pl.ds(start, 256)
    here = pl.ds(pl.multiple_of(h * HEAD, 16), HEAD)
    root = HEAD**-0.5
    dbacc[...] = jnp.zeros_like(dbacc)

    U = min(Sl, 2)

    def sample(s, u):
        kw = k_ref[s, :, win]
        vw = v_ref[s, :, win]
        km = jnp.where(mine, kw, jnp.zeros_like(kw))
        for r in range(0, T, RB):
            rows = pl.ds(r, RB)
            qw = q_ref[s, rows, win]
            gw = do_ref[s, rows, win]
            sc = head_scores(jnp.where(mine, qw, jnp.zeros_like(qw)), kw, bm[rows, :])
            lse = jnp.sum(
                jnp.where(column, lse_ref[s, rows, :], 0.0), axis=-1, keepdims=True
            )
            p = jnp.exp2(sc - lse)
            dp = dg(jnp.where(mine, gw, jnp.zeros_like(gw)), vw, NT)
            delta = jnp.sum(p * dp, axis=-1, keepdims=True)
            ds = (p * (dp - delta)).astype(bf16)
            pb[u, rows, :] = p.astype(bf16)
            dsb[u, rows, :] = ds
            dbacc[rows, :] += ds.astype(f32)
            dq_ref[s, rows, win] += dg(ds, km, NN) * root
        dvt[s, here, :] = dg(dot[s, here, :], pb[u], NN).astype(bf16)
        dkt[s, here, :] = (dg(qt[s, here, :], dsb[u], NN) * root).astype(bf16)

    def samples(i, _):
        for u in range(U):
            sample(i * U + u, u)
        return 0

    lax.fori_loop(0, Sl // U, samples, 0)
    for p in range(F):
        R = db_refs[p].shape[1]
        row = pl.multiple_of(ids[F + 2 + p] * R, 16)
        db_refs[p][0] = dbacc[pl.ds(row, R), :].astype(bf16)

    @pl.when(h == pl.num_programs(0) - 1)
    def _():
        def turn(s, _):
            dk_ref[s] = dkt[s].T
            dv_ref[s] = dvt[s].T
            return 0

        lax.fori_loop(0, Sl, turn, 0)


def attn_bwd(ids, seg, tag, q, k, v, do, lse, parts, group, deps=()):
    Sl, T, D = q.shape
    F = len(parts)
    H, R = parts[0].shape[:2]
    W = H * HEAD
    lanes = resident((Sl, T, W), group)
    part = pl.BlockSpec((1, R, T), lambda h, s: (h, 0, 0))
    outs = [
        jax.ShapeDtypeStruct((Sl, T, W), f32),
        jax.ShapeDtypeStruct((Sl, T, W), bf16),
        jax.ShapeDtypeStruct((Sl, T, W), bf16),
    ]
    res = pl.pallas_call(
        functools.partial(attn_bwd_kernel, F, len(deps), min(T, 512)),
        grid_spec=pltpu.PrefetchScalarGridSpec(
            num_scalar_prefetch=1,
            grid=(H,),
            in_specs=[resident(seg.shape), resident(tag.shape)]
            + [lanes] * 4
            + [resident(lse.shape)]
            + [part] * F
            + [ANY] * len(deps),
            out_specs=[resident(x.shape) for x in outs] + [part] * F,
            scratch_shapes=[
                pltpu.VMEM((T, T), f32),
                pltpu.VMEM((T, T), f32),
                pltpu.VMEM((2, T, T), bf16),
                pltpu.VMEM((2, T, T), bf16),
                pltpu.VMEM((Sl, W, T), bf16),
                pltpu.VMEM((Sl, W, T), bf16),
                pltpu.VMEM((Sl, W, T), bf16),
                pltpu.VMEM((Sl, W, T), bf16),
            ],
        ),
        out_shape=outs + [jax.ShapeDtypeStruct((H, R, T), bf16)] * F,
        compiler_params=pltpu.CompilerParams(
            dimension_semantics=("arbitrary",), vmem_limit_bytes=63 << 20
        ),
        cost_estimate=cost(Sl * H * T * T * 6200, Sl * T * W * 16 + H * T * T * 4, Sl * H * T * T),
        name="attn_bwd",
    )(ids, seg, tag, q, k, v, do, lse, *parts, *deps)
    return res[0], res[1], res[2], list(res[3:])


def pair_norm(x, ones):
    cen = x.astype(f32) - dg(x, ones, NN)
    inv = lax.rsqrt(dg((cen * cen).astype(bf16), ones, NN) + EPS)
    return cen * inv, inv


def pair_fwd_kernel(U, pair_ref, gain_ref, w_ref, *refs):
    first_ref, second_ref, low = refs[-3:]
    G, T, C = pair_ref.shape
    ones = jnp.full((C, C), 1.0 / C, bf16)

    def rows(i, _):
        x = pair_ref[pl.ds(i * U, U)].reshape(U * T, C)
        n, _ = pair_norm(x, ones)
        y = (n * gain_ref[...]).astype(bf16)
        for u in range(U):
            low[:, pl.ds(pl.multiple_of((i * U + u) * C, 128), C)] = y[u * T : (u + 1) * T]
        return 0

    if U == G:
        rows(0, 0)
    else:
        lax.fori_loop(0, G // U, rows, 0)
    res = dg(w_ref[...], low[...], NT)
    res = res.reshape(res.shape[0] // G, G, T).astype(bf16)
    H = res.shape[0] // 2
    first_ref[...] = res[:H]
    second_ref[...] = res[H:]


def pair_fwd(pair, gain, w_rows, deps=(), U=8):
    R, T, C = pair.shape
    G = 8
    H = w_rows.shape[0] // G
    return pl.pallas_call(
        functools.partial(pair_fwd_kernel, U),
        grid=(R // G,),
        in_specs=[
            pl.BlockSpec((G, T, C), lambda i: (i, 0, 0)),
            pl.BlockSpec((1, C), lambda i: (0, 0)),
            pl.BlockSpec((H * G, G * C), lambda i: (0, 0)),
        ]
        + [ANY] * len(deps),
        out_specs=[pl.BlockSpec((H // 2, G, T), lambda i: (0, i, 0))] * 2,
        out_shape=[jax.ShapeDtypeStruct((H // 2, R, T), bf16)] * 2,
        scratch_shapes=[pltpu.VMEM((T, G * C), bf16)],
        compiler_params=pltpu.CompilerParams(
            dimension_semantics=("arbitrary",), vmem_limit_bytes=40 << 20
        ),
        cost_estimate=cost(R * T * C * 3150, R * T * C * 3, R * T * C),
        name="pair_fwd",
    )(pair, gain, w_rows, *deps)


def pair_bwd_kernel(P, nd, U, pair_ref, gain_ref, wc_ref, *refs):
    firsts, seconds = refs[:P], refs[P : 2 * P]
    out_ref, gw_ref, acc, turned = refs[2 * P + nd :]
    G, T, C = pair_ref.shape
    H = 2 * firsts[0].shape[0]
    ones = jnp.full((C, C), 1.0 / C, bf16)

    @pl.when(pl.program_id(0) == 0)
    def _():
        acc[...] = jnp.zeros_like(acc)

    halves = []
    for parts in (firsts, seconds):
        total = parts[0][...].astype(f32)
        for p in range(1, P):
            total = total + parts[p][...].astype(f32)
        halves.append(total.reshape(H // 2 * G, T))
    flat = jnp.concatenate(halves, axis=0)
    low8 = flat.astype(bf16)
    cols = low8.T
    turned[:, : H * G] = cols
    turned[:, H * G :] = cols

    def rows(i, _):
        x = pair_ref[pl.ds(i * U, U)].reshape(U * T, C)
        n, inv = pair_norm(x, ones)
        low = (n * gain_ref[...]).astype(bf16)
        gs = []
        for u in range(U):
            acc[i * U + u] += dg(low8, low[u * T : (u + 1) * T], NN)
            gs.append(dg(turned[...], wc_ref[i * U + u], NN))
        g = jnp.concatenate(gs, axis=0) if U > 1 else gs[0]
        mean = dg((g * n).astype(bf16), ones, NN)
        out_ref[pl.ds(i * U, U)] = (inv * (g - n * mean)).astype(bf16).reshape(U, T, C)
        return 0

    if U == G:
        rows(0, 0)
    else:
        lax.fori_loop(0, G // U, rows, 0)

    @pl.when(pl.program_id(0) == pl.num_programs(0) - 1)
    def _():
        at = lax.broadcasted_iota(jnp.int32, (H * G, 1), 0) % G
        picked = jnp.zeros((H * G, C), f32)
        for i in range(G):
            picked = picked + jnp.where(at == i, acc[i], 0.0)
        gw_ref[...] = picked


def pair_bwd(pair, gain, wc, firsts, seconds, deps=(), U=8):
    R, T, C = pair.shape
    G = 8
    H = 2 * firsts[0].shape[0]
    P = len(firsts)
    rows = pl.BlockSpec((G, T, C), lambda i: (i, 0, 0))
    return pl.pallas_call(
        functools.partial(pair_bwd_kernel, P, len(deps), U),
        grid=(R // G,),
        in_specs=[
            rows,
            pl.BlockSpec((1, C), lambda i: (0, 0)),
            pl.BlockSpec((G, 2 * H * G, C), lambda i: (0, 0, 0)),
        ]
        + [pl.BlockSpec((H // 2, G, T), lambda i: (0, i, 0))] * (2 * P)
        + [ANY] * len(deps),
        out_specs=[
            rows,
            pl.BlockSpec((H * G, C), lambda i: (0, 0)),
        ],
        out_shape=[
            jax.ShapeDtypeStruct((R, T, C), bf16),
            jax.ShapeDtypeStruct((H * G, C), f32),
        ],
        scratch_shapes=[
            pltpu.VMEM((G, H * G, C), f32),
            pltpu.VMEM((T, 2 * H * G), bf16),
        ],
        compiler_params=pltpu.CompilerParams(
            dimension_semantics=("arbitrary",), vmem_limit_bytes=50 << 20
        ),
        cost_estimate=cost(R * T * C * 5500, R * T * C * 6, R * T * C),
        name="pair_bwd",
    )(pair, gain, wc, *firsts, *seconds, *deps)


def stats_of(x):
    mean = jnp.mean(x, axis=-1, keepdims=True)
    cen = x - mean
    inv = lax.rsqrt(jnp.mean(cen * cen, axis=-1, keepdims=True) + EPS)
    return cen * inv, inv


def sigmoid(x):
    return 1.0 / (1.0 + jnp.exp(-x))


def flat_rows(x):
    return x.reshape(x.shape[0] * x.shape[1], x.shape[2])


def over_samples(x, sb):
    R = x.shape[0] // sb
    total = x[:R]
    for i in range(1, sb):
        total = total + x[i * R : (i + 1) * R]
    return total


def tile_samples(x, sb):
    return x if sb == 1 else jnp.concatenate([x] * sb, axis=0)


def weight_copies(shapes, F, c, f, own, got, swapped, dst, sems):
    copies = []

    def add(src, to):
        copies.append(pltpu.make_async_copy(src, to, sems.at[len(copies)]))

    for i, (r, n) in enumerate(shapes):
        add(own[i], dst[i].at[pl.ds(pl.multiple_of(f * r, 16), r), :])
    for k in range(1, F):
        for packed, half in ((got[k - 1], c), (swapped[k - 1], 1 - c)):
            at = 0
            for i, (r, n) in enumerate(shapes):
                row = pl.multiple_of((f ^ k) * r, 16)
                for b in range(n // 2 // 384):
                    col = pl.multiple_of(half * (n // 2) + b * 384, 128)
                    add(
                        packed.at[pl.ds(at, r), :],
                        dst[i].at[pl.ds(row, r), pl.ds(col, 384)],
                    )
                    at += padded(r)
    return copies


def gathered_copies(shapes, F, c, got, swapped, dst, sems):
    copies = []
    for g in range(F):
        for packed, half in ((got, c), (swapped, 1 - c)):
            at = 0
            for i, (r, n) in enumerate(shapes):
                for b in range(n // 2 // 384):
                    col = pl.multiple_of(half * (n // 2) + b * 384, 128)
                    copies.append(
                        pltpu.make_async_copy(
                            packed.at[g, pl.ds(at, r), :],
                            dst[i].at[pl.ds(g * r, r), pl.ds(col, 384)],
                            sems.at[len(copies)],
                        )
                    )
                    at += padded(r)
    return copies


def padded(r):
    return -(-r // 16) * 16


def packed_rows(shapes):
    return sum(padded(r) * (n // 2 // 384) for r, n in shapes)


def part_map(p, nu):
    return lambda r, u, s: (jnp.where(r == p, u, jnp.where(r < p, 0, nu - 1)), 0, 0)


def part_specs(F, nu, sb, R, D, buffers=2):
    return [
        pl.BlockSpec((sb, R, D), part_map(p, nu), pipeline_mode=pl.Buffered(buffers))
        for p in range(F)
    ]


def arrived_specs(F, nu, sb, R, D):
    specs = part_specs(F, nu, sb, R, D)
    return specs + specs[:1]


def arrivals(parts, ids):
    F = len(parts) - 1
    step = pl.program_id(0)
    own = ids[F] == ids[F + 1] // (F // 2)
    whens = [(step == 0) & ~own] + [step == p for p in range(1, F)] + [(step == 0) & own]
    return zip(whens, parts)


def choose(parts, scratch, ids):
    for when, ref in arrivals(parts, ids):

        @pl.when(when)
        def _(ref=ref):
            scratch[...] = ref[...]

    return flat_rows(scratch[...].astype(f32))


def store_part(parts, value):
    for p, ref in enumerate(parts):

        @pl.when(pl.program_id(0) == p)
        def _(ref=ref):
            ref[...] = value


def copies_in_group(shapes, F):
    return len(shapes) + (F - 1) * 2 * sum(n // 2 // 384 for _, n in shapes)


def pack_grads(shapes, F, c, accs, keep_ref, give_ref, stage=None, sems=None):
    copies = []
    for g in range(F):
        for x in copies:
            x.wait()
        at = 0
        for (r, n), acc in zip(shapes, accs):
            for b in range(n // 2 // 384):
                for i, (ref, half) in enumerate(((keep_ref, c), (give_ref, 1 - c))):
                    col = pl.multiple_of(half * (n // 2) + b * 384, 128)
                    block = acc[g * r : (g + 1) * r, pl.ds(col, 384)].astype(bf16)
                    if stage is None:
                        ref[g, at : at + r, :] = block
                    else:
                        stage[i, at : at + r, :] = block
                at += padded(r)
        if stage is not None:
            copies = [
                pltpu.make_async_copy(stage.at[i], ref.at[g], sems.at[i])
                for i, ref in enumerate((keep_ref, give_ref))
            ]
            for x in copies:
                x.start()
    for x in copies:
        x.wait()


def qkvg_kernel(F, shapes, ids, *refs):
    nin = 2 * (F - 1)
    acts, refs = refs[: F + 1], refs[F + 1 :]
    cond_ref, bq_ref, wq_hbm = refs[:3]
    got, swapped = refs[3 : 3 + F - 1], refs[3 + F - 1 : 3 + nin]
    q_ref, k_ref, v_ref, g_ref, token_ref, w, xs, sems = refs[3 + nin :]
    token_ref[...] = jnp.zeros_like(token_ref)
    c, f = ids[F], ids[F + 1]

    @pl.when((pl.program_id(0) == 0) & (pl.program_id(1) == 0))
    def _():
        copies = weight_copies(shapes, F, c, f, (wq_hbm,), got, swapped, (w,), sems)
        for x in copies:
            x.start()
        for x in copies:
            x.wait()

    sb, R, D = xs.shape
    n, _ = stats_of(choose(acts, xs, ids))
    scale = tile_samples(sigmoid(cond_ref[:, :D]), sb)
    shift = tile_samples(cond_ref[:, D : 2 * D], sb)
    x = (scale * n + shift).astype(bf16)
    q_ref[...] = (dg(x, w[:, :D], NN) + bq_ref[...]).astype(bf16).reshape(sb, R, D)
    k_ref[...] = dg(x, w[:, D : 2 * D], NN).astype(bf16).reshape(sb, R, D)
    v_ref[...] = dg(x, w[:, 2 * D : 3 * D], NN).astype(bf16).reshape(sb, R, D)
    g_ref[0] = sigmoid(dg(x, w[:, 3 * D :], NN)).reshape(sb, R, D)


def sub_samples(sl, R):
    sb = max(1, min(sl, 256 // R))
    return sb, sl // sb


def qkvg_call(ids, acts, cond, bq, wq, got, swapped):
    F = len(acts) - 1
    sl, R, D = acts[0].shape
    T = F * R
    sb, nu = sub_samples(sl, R)
    shapes = [wq.shape]
    stacked = pl.BlockSpec((1, sb, R, D), lambda r, u, s: (r, u, 0, 0))
    natural = pl.BlockSpec((sb, R, D), lambda r, u, s: (u, s[r], 0))
    return pl.pallas_call(
        functools.partial(qkvg_kernel, F, shapes),
        grid_spec=pltpu.PrefetchScalarGridSpec(
            num_scalar_prefetch=1,
            grid=(F, nu),
            in_specs=arrived_specs(F, nu, sb, R, D)
            + [
                pl.BlockSpec((R, 2 * D), lambda r, u, s: (s[r], 0)),
                pl.BlockSpec((1, D), lambda r, u, s: (0, 0)),
            ]
            + [ANY] * (1 + 2 * (F - 1)),
            out_specs=[natural] * 3 + [stacked, pl.BlockSpec((1, 128), lambda r, u, s: (0, 0))],
            scratch_shapes=[
                pltpu.VMEM((D, 4 * D), bf16),
                pltpu.VMEM((sb, R, D), bf16),
                pltpu.SemaphoreType.DMA((copies_in_group(shapes, F),)),
            ],
        ),
        out_shape=[jax.ShapeDtypeStruct((sl, T, D), bf16)] * 3
        + [jax.ShapeDtypeStruct((F, sl, R, D), f32), jax.ShapeDtypeStruct((1, 128), f32)],
        compiler_params=pltpu.CompilerParams(
            dimension_semantics=("arbitrary", "arbitrary"), vmem_limit_bytes=60 << 20
        ),
        cost_estimate=cost(19 * sl * T * D * D, 2 * sl * T * D * 6 + 8 * D * D, sl * T * D),
        name="qkvg",
    )(ids, *acts, cond, bq, wq, *got, *swapped)


def middle_kernel(F, shapes, ids, *refs):
    acts, cots, refs = refs[: F + 1], refs[F + 1 : 2 * F + 2], refs[2 * F + 2 :]
    mix_a, mix_b, gate_ref, gone_ref, ctwo_ref = refs[:5]
    got, swapped = refs[5:7]
    outs, refs = refs[7 : 7 + F], refs[7 + F :]
    (
        da_ref,
        gpg_ref,
        mg_ref,
        ctg_ref,
        gog_ref,
        keep_ref,
        give_ref,
        wo,
        wab,
        wout,
        ao,
        aab,
        aout,
        xs,
        ys,
        stage,
        sems,
        out_sems,
    ) = refs
    c = ids[F]
    first = (pl.program_id(0) == 0) & (pl.program_id(1) == 0)
    last = (pl.program_id(0) == pl.num_programs(0) - 1) & (
        pl.program_id(1) == pl.num_programs(1) - 1
    )

    @pl.when(first)
    def _():
        copies = gathered_copies(shapes, F, c, got, swapped, (wo, wab, wout), sems)
        for x in copies:
            x.start()
        ao[...] = jnp.zeros_like(ao)
        aab[...] = jnp.zeros_like(aab)
        aout[...] = jnp.zeros_like(aout)
        for x in copies:
            x.wait()

    sb, R, D = xs.shape
    H = wout.shape[0]
    gate = flat_rows(gate_ref[0])
    mix = jnp.concatenate([flat_rows(mix_a[...]), flat_rows(mix_b[...])], axis=1)
    branch = (gate * mix).astype(bf16)
    attn_out = dg(branch, wo[...], NN)
    sig_one = sigmoid(gone_ref[...])
    gate_one = tile_samples(sig_one, sb)
    middle = choose(acts, xs, ids) + gate_one * attn_out
    n, inv = stats_of(middle)
    sig_scale = sigmoid(ctwo_ref[:, :D])
    scale = tile_samples(sig_scale, sb)
    x2 = (scale * n + tile_samples(ctwo_ref[:, D : 2 * D], sb)).astype(bf16)
    up = dg(x2, wab[:, H:], NN)
    gp = dg(x2, wab[:, :H], NN)
    sg = sigmoid(gp)
    silu = gp * sg
    hidden = (silu * up).astype(bf16)
    ffn = dg(hidden, wout[...], NN)
    sig_two = sigmoid(ctwo_ref[:, 2 * D :])
    gate_two = tile_samples(sig_two, sb)
    store_part(outs, (middle + gate_two * ffn).astype(bf16).reshape(sb, R, D))

    upstream = choose(cots, ys, ids)
    fg = (upstream * gate_two).astype(bf16)
    g_two = over_samples(upstream * ffn, sb) * (sig_two * (1.0 - sig_two))
    aout[...] += dg(hidden, fg, TN)
    hg = dg(fg, wout[...], NT)
    ga = (hg * up * sg * (1.0 + gp * (1.0 - sg))).astype(bf16)
    gb = (hg * silu).astype(bf16)
    aab[:, :H] += dg(x2, ga, TN)
    aab[:, H:] += dg(x2, gb, TN)
    xg = dg(ga, wab[:, :H], NT) + dg(gb, wab[:, H:], NT)
    g_scale = over_samples(xg * n, sb) * (sig_scale * (1.0 - sig_scale))
    g_shift = over_samples(xg, sb)
    inc = xg * scale
    mg = upstream + inv * (
        inc
        - jnp.mean(inc, axis=-1, keepdims=True)
        - n * jnp.mean(inc * n, axis=-1, keepdims=True)
    )
    mg_ref[0] = mg.reshape(sb, R, D)
    og = (mg * gate_one).astype(bf16)
    g_one = over_samples(mg * attn_out, sb) * (sig_one * (1.0 - sig_one))
    ao[...] += dg(branch, og, TN)
    bg = dg(og, wo[...], NT)
    da_ref[...] = (bg * gate).astype(bf16).reshape(sb, R, D)
    gpg_ref[0] = (bg * mix * (gate * (1.0 - gate))).astype(bf16).reshape(sb, R, D)

    @pl.when(pl.program_id(1) == 0)
    def _():
        ctg_ref[:, :D] = g_scale
        ctg_ref[:, D : 2 * D] = g_shift
        ctg_ref[:, 2 * D :] = g_two
        gog_ref[...] = g_one

    @pl.when(pl.program_id(1) > 0)
    def _():
        ctg_ref[:, :D] += g_scale
        ctg_ref[:, D : 2 * D] += g_shift
        ctg_ref[:, 2 * D :] += g_two
        gog_ref[...] += g_one

    @pl.when(last)
    def _():
        pack_grads(shapes, F, c, (ao, aab, aout), keep_ref, give_ref, stage, out_sems)


def middle_call(ids, acts, cots, mix_a, mix_b, gate, cond_one, cond_two, shapes, got, swapped):
    F = len(acts) - 1
    sl, R, D = acts[0].shape
    T = F * R
    H = shapes[2][0] * F
    sb, nu = sub_samples(sl, R)
    copies = 2 * F * sum(n // 2 // 384 for _, n in shapes)
    rows = packed_rows(shapes)
    stacked = pl.BlockSpec((1, sb, R, D), lambda r, u, s: (r, u, 0, 0))
    natural = pl.BlockSpec((sb, R, D), lambda r, u, s: (u, s[r], 0))
    lanes = pl.BlockSpec((sb, R, D // 2), lambda r, u, s: (u, s[r], 0))
    flops = 12 * sl * T * D * (D + 3 * H)
    res = pl.pallas_call(
        functools.partial(middle_kernel, F, shapes),
        grid_spec=pltpu.PrefetchScalarGridSpec(
            num_scalar_prefetch=1,
            grid=(F, nu),
            in_specs=arrived_specs(F, nu, sb, R, D) * 2
            + [
                lanes,
                lanes,
                stacked,
                pl.BlockSpec((R, D), lambda r, u, s: (s[r], 2)),
                pl.BlockSpec((R, 3 * D), lambda r, u, s: (s[r], 0)),
            ]
            + [ANY] * 2,
            out_specs=part_specs(F, nu, sb, R, D)
            + [
                natural,
                stacked,
                stacked,
                pl.BlockSpec((R, 3 * D), lambda r, u, s: (s[r], 0)),
                pl.BlockSpec((R, D), lambda r, u, s: (s[r], 0)),
                ANY,
                ANY,
            ],
            scratch_shapes=[
                pltpu.VMEM((D, D), bf16),
                pltpu.VMEM((D, 2 * H), bf16),
                pltpu.VMEM((H, D), bf16),
                pltpu.VMEM((D, D), f32),
                pltpu.VMEM((D, 2 * H), f32),
                pltpu.VMEM((H, D), f32),
                pltpu.VMEM((sb, R, D), bf16),
                pltpu.VMEM((sb, R, D), bf16),
                pltpu.VMEM((2, rows, 384), bf16),
                pltpu.SemaphoreType.DMA((copies,)),
                pltpu.SemaphoreType.DMA((2,)),
            ],
        ),
        out_shape=[jax.ShapeDtypeStruct((sl, R, D), bf16)] * F
        + [
            jax.ShapeDtypeStruct((sl, T, D), bf16),
            jax.ShapeDtypeStruct((F, sl, R, D), bf16),
            jax.ShapeDtypeStruct((F, sl, R, D), f32),
            jax.ShapeDtypeStruct((T, 3 * D), f32),
            jax.ShapeDtypeStruct((T, D), f32),
            jax.ShapeDtypeStruct((F, rows, 384), bf16),
            jax.ShapeDtypeStruct((F, rows, 384), bf16),
        ],
        compiler_params=pltpu.CompilerParams(
            dimension_semantics=("arbitrary", "arbitrary"), vmem_limit_bytes=63 << 20
        ),
        cost_estimate=cost(flops, sl * T * D * 24, sl * T * H),
        name="middle",
    )(ids, *acts, *cots, mix_a, mix_b, gate, cond_one, cond_two, got, swapped)
    return list(res[:F]), *res[F:]


def back_weight_kernel(F, nd, shapes, ids, *refs):
    acts, refs = refs[: F + 1], refs[F + 1 :]
    cond_ref, dq_a, dq_b, dk_a, dk_b, dv_a, dv_b, gpg_ref = refs[:8]
    bq_ref, keep_ref, give_ref, acc, xs = refs[8 + nd :]
    D = acts[0].shape[2]
    first = (pl.program_id(0) == 0) & (pl.program_id(1) == 0)
    last = (pl.program_id(0) == pl.num_programs(0) - 1) & (
        pl.program_id(1) == pl.num_programs(1) - 1
    )

    @pl.when(first)
    def _():
        acc[...] = jnp.zeros_like(acc)
        bq_ref[...] = jnp.zeros_like(bq_ref)

    sb = xs.shape[0]
    n, _ = stats_of(choose(acts, xs, ids))
    scale = tile_samples(sigmoid(cond_ref[:, :D]), sb)
    x = (scale * n + tile_samples(cond_ref[:, D : 2 * D], sb)).astype(bf16)
    for i, refs_i in enumerate(((dq_a, dq_b), (dk_a, dk_b), (dv_a, dv_b))):
        g = jnp.concatenate([flat_rows(y[...]) for y in refs_i], axis=1)
        if i == 0:
            bq_ref[...] += jnp.sum(g, axis=0, keepdims=True)
        acc[:, i * D : (i + 1) * D] += dg(x, g.astype(bf16), TN)
    acc[:, 3 * D :] += dg(x, flat_rows(gpg_ref[0]), TN)

    @pl.when(last)
    def _():
        pack_grads(shapes, F, ids[F], (acc,), keep_ref, give_ref)


def back_data_kernel(F, nd, shapes, cshape, ids, *refs):
    nin = 2 * (F - 1)
    acts, refs = refs[: F + 1], refs[F + 1 :]
    cond_ref, dq_a, dq_b, dk_a, dk_b, dv_a, dv_b, gpg_ref, mg_ref = refs[:9]
    s_ref, gog_ref, wc_ref, wq_hbm = refs[9:13]
    got, swapped = refs[13 : 13 + F - 1], refs[13 + F - 1 : 13 + nin]
    ags, refs = refs[13 + nin + nd : 13 + nin + nd + F], refs[13 + nin + nd + F :]
    sg_ref, sum_ref, keep_ref, give_ref, w, cg, acc, xs, sems = refs
    c, f = ids[F], ids[F + 1]
    last = (pl.program_id(0) == pl.num_programs(0) - 1) & (
        pl.program_id(1) == pl.num_programs(1) - 1
    )
    first = (pl.program_id(0) == 0) & (pl.program_id(1) == 0)

    @pl.when(first)
    def _():
        copies = weight_copies(shapes, F, c, f, (wq_hbm,), got, swapped, (w,), sems)
        for x in copies:
            x.start()
        for x in copies:
            x.wait()

    sb, R, D = xs.shape
    n, inv = stats_of(choose(acts, xs, ids))
    sig_scale = sigmoid(cond_ref[:, :D])
    scale = tile_samples(sig_scale, sb)
    xg = dg(flat_rows(gpg_ref[0]), w[:, 3 * D :], NT)
    for i, refs_i in enumerate(((dq_a, dq_b), (dk_a, dk_b), (dv_a, dv_b))):
        g = jnp.concatenate([flat_rows(y[...]) for y in refs_i], axis=1).astype(bf16)
        xg = xg + dg(g, w[:, i * D : (i + 1) * D], NT)
    g_scale = over_samples(xg * n, sb) * (sig_scale * (1.0 - sig_scale))
    g_shift = over_samples(xg, sb)
    inc = xg * scale
    ag = flat_rows(mg_ref[0]) + inv * (
        inc
        - jnp.mean(inc, axis=-1, keepdims=True)
        - n * jnp.mean(inc * n, axis=-1, keepdims=True)
    )
    store_part(ags, ag.astype(bf16).reshape(sb, R, D))

    rows = pl.ds(pl.multiple_of(ids[pl.program_id(0)] * R, 16), R)

    @pl.when(pl.program_id(1) == 0)
    def _():
        cg[rows, :D] = g_scale
        cg[rows, D : 2 * D] = g_shift
        cg[rows, 2 * D :] = gog_ref[rows, :]

    @pl.when(pl.program_id(1) > 0)
    def _():
        cg[rows, :D] += g_scale
        cg[rows, D : 2 * D] += g_shift

    @pl.when(last)
    def _():
        cond_grads(F, cshape, c, s_ref, cg[...], wc_ref, sg_ref, sum_ref, keep_ref, give_ref, acc)


def back_weight(ids, acts, cond, dqkv, gpg, wq_shape, deps=()):
    F = len(acts) - 1
    sl, R, D = acts[0].shape
    T = F * R
    sb, nu = sub_samples(sl, R)
    rows = packed_rows([wq_shape])
    stacked = pl.BlockSpec((1, sb, R, D), lambda r, u, s: (r, u, 0, 0))
    lanes = pl.BlockSpec((sb, R, D // 2), lambda r, u, s: (u, s[r], 0))
    whole = pl.BlockSpec((F, rows, 384), lambda r, u, s: (0, 0, 0), pipeline_mode=pl.Buffered(1))
    return pl.pallas_call(
        functools.partial(back_weight_kernel, F, len(deps), [wq_shape]),
        grid_spec=pltpu.PrefetchScalarGridSpec(
            num_scalar_prefetch=1,
            grid=(F, nu),
            in_specs=arrived_specs(F, nu, sb, R, D)
            + [pl.BlockSpec((R, 2 * D), lambda r, u, s: (s[r], 0))]
            + [lanes] * 6
            + [stacked]
            + [ANY] * len(deps),
            out_specs=[pl.BlockSpec((1, D), lambda r, u, s: (0, 0)), whole, whole],
            scratch_shapes=[pltpu.VMEM((D, 4 * D), f32), pltpu.VMEM((sb, R, D), bf16)],
        ),
        out_shape=[
            jax.ShapeDtypeStruct((1, D), f32),
            jax.ShapeDtypeStruct((F, rows, 384), bf16),
            jax.ShapeDtypeStruct((F, rows, 384), bf16),
        ],
        compiler_params=pltpu.CompilerParams(
            dimension_semantics=("arbitrary", "arbitrary"), vmem_limit_bytes=60 << 20
        ),
        cost_estimate=cost(17 * sl * T * D * D, sl * T * D * 16 + 12 * D * D, sl * T),
        name="back_weight",
    )(ids, *acts, cond, *dqkv, gpg, *deps)


def back_data(ids, acts, cond, dqkv, gpg, mg, s_low, gog, wc, wq, got, swapped, deps=()):
    F = len(acts) - 1
    sl, R, D = acts[0].shape
    T = F * R
    sb, nu = sub_samples(sl, R)
    shapes = [wq.shape]
    C, N = s_low.shape[1], wc.shape[2]
    cshape = (C // F, N)
    crows = packed_rows([cshape])

    def once(shape):
        return pl.BlockSpec(
            shape, lambda r, u, s: (0,) * len(shape), pipeline_mode=pl.Buffered(1)
        )

    outs = [
        jax.ShapeDtypeStruct((T, C), f32),
        jax.ShapeDtypeStruct((1, N), f32),
        jax.ShapeDtypeStruct((F, crows, 384), bf16),
        jax.ShapeDtypeStruct((F, crows, 384), bf16),
    ]
    stacked = pl.BlockSpec((1, sb, R, D), lambda r, u, s: (r, u, 0, 0))
    lanes = pl.BlockSpec((sb, R, D // 2), lambda r, u, s: (u, s[r], 0))
    res = pl.pallas_call(
        functools.partial(back_data_kernel, F, len(deps), shapes, cshape),
        grid_spec=pltpu.PrefetchScalarGridSpec(
            num_scalar_prefetch=1,
            grid=(F, nu),
            in_specs=arrived_specs(F, nu, sb, R, D)
            + [pl.BlockSpec((R, 2 * D), lambda r, u, s: (s[r], 0))]
            + [lanes] * 6
            + [stacked, stacked]
            + [once(x.shape) for x in (s_low, gog, wc)]
            + [ANY] * (1 + 2 * (F - 1) + len(deps)),
            out_specs=part_specs(F, nu, sb, R, D) + [once(x.shape) for x in outs],
            scratch_shapes=[
                pltpu.VMEM((D, 4 * D), bf16),
                pltpu.VMEM((T, N), f32),
                pltpu.VMEM((C, N), f32),
                pltpu.VMEM((sb, R, D), bf16),
                pltpu.SemaphoreType.DMA((copies_in_group(shapes, F),)),
            ],
        ),
        out_shape=[jax.ShapeDtypeStruct((sl, R, D), bf16)] * F + outs,
        compiler_params=pltpu.CompilerParams(
            dimension_semantics=("arbitrary", "arbitrary"), vmem_limit_bytes=60 << 20
        ),
        cost_estimate=cost(17 * sl * T * D * D, sl * T * D * 22 + 8 * D * D, sl * T),
        name="back_data",
    )(ids, *acts, cond, *dqkv, gpg, mg, s_low, gog, wc, wq, *got, *swapped, *deps)
    return list(res[:F]), *res[F:]


def prepare_kernel(F, nd, groups, ids, *refs):
    xs, refs = refs[:F], refs[F:]
    weights = sum(len(g) for g in groups)
    ws, refs = list(refs[:weights]), refs[weights + nd :]
    for x, out in zip(xs, refs):
        out[...] = x[...]

    @pl.when(pl.program_id(0) == 0)
    def _():
        for shapes, packed in zip(groups, refs[F:]):
            at = 0
            for r, n in shapes:
                w = ws.pop(0)
                for b in range(n // 2 // 384):
                    col = pl.multiple_of(ids[F] * (n // 2) + b * 384, 128)
                    packed[at : at + r, :] = w[:, pl.ds(col, 384)]
                    at += padded(r)


def prepare(ids, x, groups=(), deps=()):
    S, R, D = x.shape
    F = (ids.shape[0] - 2) // 3
    sl = S // F
    steps = 4
    shapes = [[w.shape for w in g] for g in groups]
    rows = [packed_rows(s) for s in shapes]

    def group(p):
        return pl.BlockSpec((sl, R // steps, D), lambda i, s: (s[2 * F + 2 + p], i, 0))

    part = pl.BlockSpec((sl, R // steps, D), lambda i, s: (0, i, 0))
    weights = [w for g in groups for w in g]
    res = pl.pallas_call(
        functools.partial(prepare_kernel, F, len(deps), shapes),
        grid_spec=pltpu.PrefetchScalarGridSpec(
            num_scalar_prefetch=1,
            grid=(steps,),
            in_specs=[group(p) for p in range(F)]
            + [pl.BlockSpec(w.shape, lambda i, s: (0, 0)) for w in weights]
            + [ANY] * len(deps),
            out_specs=[part] * F + [pl.BlockSpec((n, 384), lambda i, s: (0, 0)) for n in rows],
        ),
        out_shape=[jax.ShapeDtypeStruct((sl, R, D), x.dtype)] * F
        + [jax.ShapeDtypeStruct((n, 384), bf16) for n in rows],
        compiler_params=pltpu.CompilerParams(
            dimension_semantics=("arbitrary",), vmem_limit_bytes=40 << 20
        ),
        cost_estimate=cost(5e9, S * R * D * 4),
        name="prepare",
    )(ids, *([x] * F), *weights, *deps)
    return list(res[:F]), *res[F:]


def place_kernel(F, ids, *refs):
    out = refs[-1]
    for when, ref in arrivals(refs[: F + 1], ids):

        @pl.when(when)
        def _(ref=ref):
            out[...] = ref[...]


def place(ids, parts, deps=()):
    F = len(parts) - 1
    sl, R, D = parts[0].shape
    fetch = pl.BlockSpec((sl, R, D), lambda i, s: (0, 0, 0), pipeline_mode=pl.Buffered(1))
    return pl.pallas_call(
        functools.partial(place_kernel, F),
        grid_spec=pltpu.PrefetchScalarGridSpec(
            num_scalar_prefetch=1,
            grid=(F,),
            in_specs=[fetch] * (F + 1) + [ANY] * len(deps),
            out_specs=pl.BlockSpec((sl, R, D), lambda i, s: (s[2 * F + 2 + i], 0, 0)),
        ),
        out_shape=jax.ShapeDtypeStruct((F * sl, R, D), parts[0].dtype),
        compiler_params=pltpu.CompilerParams(
            dimension_semantics=("arbitrary",), vmem_limit_bytes=40 << 20
        ),
        cost_estimate=cost(4e9, F * sl * R * D * 4),
        name="place",
    )(ids, *parts, *deps)


def terms_kernel(F, n, ids, *refs):
    outs = refs[-F:]
    for p in range(F):

        @pl.when(pl.program_id(0) == p)
        def _(p=p):
            at = 0
            for own, got in zip(refs[:n], refs[n : 2 * n]):
                rows = own.shape[1]
                outs[p][at : at + rows, :] = (own[0].astype(f32) + got[0].astype(f32)).astype(bf16)
                at += rows


def terms(ids, keeps, gots, deps=()):
    F, _, W = keeps[0].shape
    rows = sum(x.shape[1] for x in keeps)
    shards = [
        pl.BlockSpec((1, x.shape[1], W), lambda k, s: (s[F + 1] ^ k, 0, 0)) for x in keeps
    ]
    out = pl.BlockSpec((rows, W), lambda k, s: (0, 0), pipeline_mode=pl.Buffered(1))
    return pl.pallas_call(
        functools.partial(terms_kernel, F, len(keeps)),
        grid_spec=pltpu.PrefetchScalarGridSpec(
            num_scalar_prefetch=1,
            grid=(F,),
            in_specs=shards * 2 + [ANY] * len(deps),
            out_specs=[out] * F,
        ),
        out_shape=[jax.ShapeDtypeStruct((rows, W), bf16)] * F,
        compiler_params=pltpu.CompilerParams(
            dimension_semantics=("arbitrary",), vmem_limit_bytes=40 << 20
        ),
        cost_estimate=cost(5e9, F * rows * W * 6),
        name="terms",
    )(ids, *keeps, *gots, *deps)


def cond_grads(F, shape, c, s_ref, cg, w_ref, sg_ref, sum_ref, keep_ref, give_ref, acc):
    sum_ref[...] = jnp.sum(cg, axis=0, keepdims=True)
    low = cg.astype(bf16)
    acc[...] = dg(s_ref[...], low, TN)
    r = shape[0]
    sg_ref[...] = jnp.concatenate([dg(low, w_ref[g, :r, :], NT) for g in range(F)], axis=1)
    pack_grads([shape], F, c, (acc,), keep_ref, give_ref)


def cond_back_kernel(F, shape, ids, s_ref, cg_ref, w_ref, *refs):
    sg_ref, sum_ref, keep_ref, give_ref, acc = refs[-5:]
    cond_grads(
        F, shape, ids[F], s_ref, cg_ref[...], w_ref, sg_ref, sum_ref, keep_ref, give_ref, acc
    )


def cond_back(ids, s_low, cg, w, F, deps=()):
    T, C = s_low.shape
    N = cg.shape[1]
    shape = (C // F, N)
    rows = packed_rows([shape])
    vmem = pl.BlockSpec(memory_space=pltpu.VMEM)
    return pl.pallas_call(
        functools.partial(cond_back_kernel, F, shape),
        in_specs=[pl.BlockSpec(memory_space=pltpu.SMEM)] + [vmem] * 3 + [ANY] * len(deps),
        out_specs=[vmem] * 4,
        out_shape=[
            jax.ShapeDtypeStruct((T, C), f32),
            jax.ShapeDtypeStruct((1, N), f32),
            jax.ShapeDtypeStruct((F, rows, 384), bf16),
            jax.ShapeDtypeStruct((F, rows, 384), bf16),
        ],
        scratch_shapes=[pltpu.VMEM((C, N), f32)],
        compiler_params=pltpu.CompilerParams(vmem_limit_bytes=50 << 20),
        cost_estimate=cost(8e9, T * N * 4),
        name="cond_back",
    )(ids, s_low, cg, w, *deps)


def unpack_kernel(groups, ids_c, *refs):
    n = len(groups)
    c = ids_c[0]
    outs = list(refs[2 * n :])
    for i, shapes in enumerate(groups):
        at = 0
        for r, cols in shapes:
            out = outs.pop(0)
            for b in range(cols // 2 // 384):
                for ref, half in ((refs[2 * i], c), (refs[2 * i + 1], 1 - c)):
                    col = pl.multiple_of(half * (cols // 2) + b * 384, 128)
                    out[:, pl.ds(col, 384)] = ref[at : at + r, :].astype(f32)
                at += padded(r)


def unpack(c, groups):
    vmem = pl.BlockSpec(memory_space=pltpu.VMEM)
    shapes = [s for _, _, g in groups for s in g]
    return pl.pallas_call(
        functools.partial(unpack_kernel, [g for _, _, g in groups]),
        in_specs=[pl.BlockSpec(memory_space=pltpu.SMEM)] + [vmem] * (2 * len(groups)),
        out_specs=[vmem] * len(shapes),
        out_shape=[jax.ShapeDtypeStruct(s, f32) for s in shapes],
        compiler_params=pltpu.CompilerParams(vmem_limit_bytes=40 << 20),
        cost_estimate=cost(5e9, sum(r * n for r, n in shapes) * 6),
        name="unpack",
    )(c.reshape(1).astype(jnp.int32), *[x for a, b, _ in groups for x in (a, b)])


def cond_fwd_kernel(F, shape, at, natural, ids, single_ref, gain_ref, bias_ref, *refs):
    r, n = shape
    refs, (s_ref, cond_ref, w) = refs[:-3], refs[-3:]
    c, f = ids[F], ids[F + 1]
    step = padded(r)

    def put(g, packed, half):
        for b in range(n // 2 // 384):
            col = pl.multiple_of(half * (n // 2) + b * 384, 128)
            w[g, :r, pl.ds(col, 384)] = packed(at + b * step)

    if natural:
        for g in range(F):
            for ref, half in zip(refs, (c, 1 - c)):
                put(g, lambda row, ref=ref, g=g: ref[g, row : row + r, :], half)
    else:
        w[f, :r, :] = refs[0][...]
        for k in range(1, F):
            for ref, half in ((refs[k], c), (refs[F - 1 + k], 1 - c)):
                put(f ^ k, lambda row, ref=ref: ref[row : row + r, :], half)
    x, _ = stats_of(single_ref[...])
    s_ref[...] = (x * gain_ref[...]).astype(bf16)
    total = bias_ref[...]
    for g in range(F):
        total = total + dg(s_ref[:, g * r : (g + 1) * r], w[g, :r, :], NN)
    cond_ref[...] = total


def cond_fwd(ids, single, gain, bias, shape, at, arrays, natural):
    T, C = single.shape
    r, n = shape
    F = C // r
    vmem = pl.BlockSpec(memory_space=pltpu.VMEM)
    return pl.pallas_call(
        functools.partial(cond_fwd_kernel, F, shape, at, natural),
        in_specs=[pl.BlockSpec(memory_space=pltpu.SMEM)] + [vmem] * (3 + len(arrays)),
        out_specs=[vmem] * 3,
        out_shape=[
            jax.ShapeDtypeStruct((T, C), bf16),
            jax.ShapeDtypeStruct((T, n), f32),
            jax.ShapeDtypeStruct((F, padded(r), n), bf16),
        ],
        compiler_params=pltpu.CompilerParams(vmem_limit_bytes=60 << 20),
        cost_estimate=cost(6e9, T * n * 4),
        name="cond_fwd",
    )(ids, single, gain, bias, *arrays)


class Net:
    def __init__(self, dp, fsdp):
        self.Z, self.F, self.Fh = dp // 2, fsdp, fsdp // 2
        self.z, self.c = lax.axis_index("z"), lax.axis_index("core")
        self.f = lax.axis_index("fsdp")
        self.fh, self.fl = self.f // self.Fh, self.f % self.Fh
        r = jnp.arange(self.F, dtype=jnp.int32)
        blocks = (self.c ^ (r % 2)) * self.Fh + (self.fl ^ (r // 2))
        rows = ((self.c + r // self.Fh) % 2) * self.Fh + (self.fl ^ (r % self.Fh))
        groups = (self.fl ^ (r // 2)) * 2 + (self.fh ^ (r % 2))
        self.ids = jnp.concatenate(
            [blocks, jnp.stack([self.c, self.f]), rows, groups]
        ).astype(jnp.int32)

    def send(self, x, fn, raw=False):
        F = self.F
        pairs = []
        for z in range(self.Z):
            for c in range(2):
                for f in range(F):
                    z2, c2, f2 = fn(z, c, f)
                    pairs.append(((z * 2 + c) * F + f, (z2 * 2 + c2) * F + f2))
        others = [p for p in pairs if p[0] != p[1]]
        got = lax.ppermute(x, ("z", "core", "fsdp"), others)
        if len(others) == len(pairs) or raw:
            return got
        return jnp.where(self.c == self.fh, x, got)

    def core_swap(self, x):
        return self.send(x, lambda z, c, f: (z, 1 - c, f))

    def to_owner(self, x, a):
        Fh = self.Fh
        return self.send(x, lambda z, c, f: (z, f // Fh, c * Fh + ((f % Fh) ^ a)))

    def exchange_in(self, parts):
        Fh = self.Fh
        return [
            self.send(
                p,
                lambda z, c, f: (z, (f // Fh) ^ (i % 2), c * Fh + ((f % Fh) ^ (i // 2))),
                raw=True,
            )
            for i, p in enumerate(parts)
        ] + [parts[0]]

    def exchange_out(self, parts):
        Fh = self.Fh
        return [
            self.send(
                p,
                lambda z, c, f: (z, f // Fh, (c ^ (i % 2)) * Fh + ((f % Fh) ^ (i // 2))),
                raw=True,
            )
            for i, p in enumerate(parts)
        ] + [parts[0]]

    def gather_rows(self, x):
        return [self.to_owner(x, a) for a in range(self.Fh)]

    def both_cores(self, own):
        return own + [self.core_swap(p) for p in own]

    def chip_sum(self, parts):
        Fh = self.Fh
        out = []
        for a in range(Fh):
            got = self.core_swap(parts[Fh + a])
            out.append((parts[a].astype(f32) + got.astype(f32)).astype(got.dtype))
        return out

    def to_owners(self, parts):
        return [self.to_owner(p, a) for a, p in enumerate(parts)]

    def gather_packed(self, packed, mid, *held):
        F = self.F
        got = [self.send(packed, lambda z, c, f: (z, c, f ^ k)) for k in range(1, F)]
        got[:-1], mid = tie(got[:-1], mid)
        got, *held = tie(got, *held)
        return got, [self.core_swap(g) for g in got], mid, *held

    def plane_send(self, parts):
        return list(parts[:1]) + [
            self.send(parts[k], lambda z, c, f: (z, c, f ^ k)) for k in range(1, self.F)
        ]

    def tree(self, x, count, fn):
        parts = [x] + [
            self.send(x, lambda z, c, f: fn(z, c, f, k)) for k in range(1, count)
        ]
        parts = [p.astype(f32) for p in parts]
        while len(parts) > 1:
            parts = [parts[i] + parts[i + 1] for i in range(0, len(parts), 2)]
        return parts[0].astype(x.dtype)

    def over_z(self, x):
        return self.tree(x, self.Z, lambda z, c, f, k: (z ^ k, c, f))

    def all_steps(self):
        return [
            lambda x: x + self.core_swap(x),
            lambda x: self.tree(x, self.F, lambda z, c, f, k: (z, c, f ^ k)),
            self.over_z,
        ]


def total_of(parts):
    return functools.reduce(jnp.add, [p.astype(f32) for p in parts])


def lockstep(*lanes):
    values = [v for v, _ in lanes]
    for i in range(max(len(steps) for _, steps in lanes)):
        values = [steps[i](v) if i < len(steps) else v for v, (_, steps) in zip(values, lanes)]
        values = tie(*values)
    return values


def tie(*xs):
    return lax.optimization_barrier(xs)


def body(
    dp,
    fsdp,
    act,
    single,
    pair,
    segment,
    padding,
    cotangent,
    gain_s1,
    w_cond1,
    b_cond1,
    w_qkvg,
    b_q,
    gain_z,
    w_pair,
    w_o,
    gain_s2,
    w_cond2,
    b_cond2,
    w_ab,
    w_out,
):
    net = Net(dp, fsdp)
    F, ids = net.F, net.ids
    act, single, pair, segment, padding, cotangent = (
        x[0] for x in (act, single, pair, segment, padding, cotangent)
    )
    S, R, D = act.shape
    T = R * F
    COND = single.shape[1]

    vecs = [gain_s1, b_cond1, b_q, gain_z, w_pair, gain_s2, b_cond2]
    sizes = [v.size for v in vecs]
    COND = single.shape[1]
    tag = jnp.where(padding == 1, -1, segment)
    flat = jnp.concatenate([x.reshape(-1).astype(f32) for x in (segment, tag, *vecs)])
    vrows = -(-flat.shape[0] // (8 * COND)) * 8
    flat = jnp.pad(flat, (0, vrows * COND - flat.shape[0])).reshape(vrows, COND)
    table = lax.all_gather(jnp.concatenate([single, flat], axis=0), ("core", "fsdp"))
    mid_weights = [w_o, w_ab, w_out, w_cond2]
    mid_shapes = [w.shape for w in mid_weights]
    acts, packed, mid_packed = prepare(ids, act, [[w_qkvg, w_cond1], mid_weights])
    acts = net.exchange_in(acts)
    share = mid_packed.shape[0] // net.Z
    mid_got = lax.dynamic_slice_in_dim(mid_packed, net.z * share, share, 0)
    table = lax.dynamic_slice_in_dim(table, net.fh * F, F, 0)
    smalls = table[:, R:].reshape(F, vrows * COND)

    single_all = table[:, :R].reshape(T, COND)
    seg_col = smalls[:, :R].reshape(T, 1)
    tag_row = smalls[:, R : 2 * R].reshape(1, T)
    full, at = [], 2 * R
    for v, n in zip(vecs, sizes):
        full.append(smalls[:, at : at + n].reshape((F * v.shape[0],) + v.shape[1:]))
        at += n
    gs1, bc1, bq, gz, wp, gs2, bc2 = full

    wt = wp.T
    eye = jnp.eye(8, dtype=f32)
    w_rows = (wt[:, None, None, :] * eye[None, :, :, None]).reshape(HEADS * 8, -1).astype(bf16)
    gz_row = gz.reshape(1, -1)
    bias_a, bias_b = pair_fwd(pair, gz_row, w_rows)
    acts, packed, bias_a, bias_b = tie(acts, packed, bias_a, bias_b)
    one_got, one_swapped, mid_got, bias_a, bias_b = net.gather_packed(
        packed, mid_got, bias_a, bias_b
    )
    mid_got = lax.all_gather(mid_got, ("fsdp", "z")).reshape(F, net.Z * share, 384)
    bias_a, bias_b = net.both_cores(net.gather_rows(bias_a)), net.gather_rows(bias_b)

    single_first, cond_one, wc1 = cond_fwd(
        ids,
        single_all,
        gs1.reshape(1, -1),
        bc1.reshape(1, -1),
        w_cond1.shape,
        packed_rows([w_qkvg.shape]),
        [w_cond1, *one_got, *one_swapped],
        False,
    )
    q, k, v, gate, token = qkvg_call(
        ids, acts, cond_one, bq.reshape(1, D), w_qkvg, one_got, one_swapped
    )

    cots = prepare(ids, cotangent, deps=[token])[0]
    mix_a, lse_a = attn_fwd(ids, seg_col, tag_row, q, k, v, bias_a, 0, deps=cots)
    cots = net.exchange_in(cots)
    mid_got, mix_a, bias_b, cots[1:3] = tie(mid_got, mix_a, bias_b, cots[1:3])
    bias_b = net.both_cores(bias_b)
    mid_swapped = net.core_swap(mid_got)
    mix_b, lse_b = attn_fwd(ids, seg_col, tag_row, q, k, v, bias_b, 1)
    single_second, cond_two, wc2 = cond_fwd(
        ids,
        single_all,
        gs2.reshape(1, -1),
        bc2.reshape(1, -1),
        w_cond2.shape,
        packed_rows(mid_shapes[:3]),
        [mid_got, mid_swapped],
        True,
    )
    outs, d_attn, gate_proj, mid_grad, cond_two_grad, gate_one_grad, keep, give = middle_call(
        ids, acts, cots, mix_a, mix_b, gate, cond_one, cond_two, mid_shapes[:3], mid_got, mid_swapped
    )
    outs = net.exchange_out(outs)
    got = net.core_swap(give)
    s_two_grad, grad_b_cond2, keep_c, give_c = cond_back(ids, single_second, cond_two_grad, wc2, F)
    got_c = net.core_swap(give_c)
    mid_sum = []
    for x, y in ((keep, got), (keep_c, got_c)):
        x = (x.astype(f32) + y.astype(f32)).astype(bf16)
        mid_sum.append(jnp.swapaxes(x.reshape(F, net.Z, x.shape[1] // net.Z, 384), 0, 1))
    mid_sum = jnp.concatenate(mid_sum, axis=2)

    dq_a, dk_a, dv_a, db_a = attn_bwd(
        ids, seg_col, tag_row, q, k, v, d_attn, lse_a, bias_a, 0, deps=[mid_sum]
    )
    mid_sum = lax.psum_scatter(mid_sum, "z", scatter_dimension=0)
    outs, db_a = tie(outs, db_a)
    db_a = net.chip_sum(db_a)
    dq_b, dk_b, dv_b, db_b = attn_bwd(
        ids, seg_col, tag_row, q, k, v, d_attn, lse_b, bias_b, 1, deps=db_a
    )
    db_a, db_b, mid_sum = tie(net.to_owners(db_a), db_b, mid_sum)
    db_b = net.chip_sum(db_b)
    mid_sum = net.plane_send(
        [lax.dynamic_index_in_dim(mid_sum, net.f ^ k_, 0, keepdims=False) for k_ in range(F)]
    )
    dqkv = (dq_a, dq_b, dk_a, dk_b, dv_a, dv_b)
    bq_grad, keep, give = back_weight(
        ids, acts, cond_one, dqkv, gate_proj, w_qkvg.shape, deps=db_b
    )
    db_b, give, mid_sum = tie(net.to_owners(db_b), give, mid_sum)
    mid_sum = lax.all_gather(total_of(mid_sum).astype(bf16), "z", axis=0)
    block_out = place(ids, outs, deps=[give])
    wq_parts = terms(ids, [keep], [net.core_swap(give)], deps=[block_out])
    ags, s_one_grad, grad_b_cond1, keep, give = back_data(
        ids,
        acts,
        cond_one,
        dqkv,
        gate_proj,
        mid_grad,
        single_first,
        gate_one_grad,
        wc1,
        w_qkvg,
        one_got,
        one_swapped,
        deps=wq_parts[:1],
    )
    wq_parts, keep, give, ags = tie(net.plane_send(wq_parts), keep, give, ags)
    wq_sum = lax.psum(total_of(wq_parts).astype(bf16), "z")
    late_parts = terms(ids, [keep], [net.core_swap(give)])
    ags = net.exchange_out(ags)

    wc = wt * gz_row
    wc = wc - jnp.mean(wc, axis=1, keepdims=True)
    wc = (wc[None, :, None, :] * eye[:, None, :, None]).reshape(8, HEADS * 8, -1)
    wc_hi = wc.astype(bf16)
    wc = jnp.concatenate([wc_hi, (wc - wc_hi.astype(f32)).astype(bf16)], axis=1)
    pair_grad, gw = pair_bwd(pair, gz_row, wc, db_a, db_b, deps=late_parts[:1])
    late_parts, gw, s_one_grad, mid_sum, wq_sum, ags = tie(
        late_parts, gw, s_one_grad, mid_sum, wq_sum, ags
    )

    s_grad = s_one_grad * gs1 + s_two_grad * gs2
    s_parts = [
        lax.dynamic_slice_in_dim(s_grad, ids[F + 2 + p] * R, R, 0) for p in range(F)
    ]
    flat = [grad_b_cond1, bq_grad, grad_b_cond2, jnp.sum(gw.reshape(HEADS, 8, -1), axis=1)]
    flat = jnp.concatenate([g.reshape(-1, 128) for g in flat], axis=0)
    shares = [packed_rows(mid_shapes[:3]) // net.Z, packed_rows(mid_shapes[3:]) // net.Z]
    mid_sum = jnp.concatenate(
        [mid_sum[:, : shares[0]].reshape(-1, 384), mid_sum[:, shares[0] :].reshape(-1, 384)], axis=0
    )
    late_sum, flat, s_parts, mid_sum, wq_sum = lockstep(
        (
            late_parts,
            [
                lambda x: total_of(net.plane_send(x)).astype(bf16),
                net.over_z,
                lambda x: (x, net.core_swap(x)),
            ],
        ),
        (flat, net.all_steps()),
        (s_parts, [net.chip_sum, net.to_owners]),
        (mid_sum, [lambda x: (x, net.core_swap(x))]),
        (wq_sum, [lambda x: (x, net.core_swap(x))]),
    )
    total_wo, total_wab, total_wout, total_wc2, total_wq = unpack(
        net.c, [(*mid_sum, mid_shapes), (*wq_sum, [w_qkvg.shape])]
    )
    (total_wc1,) = unpack(net.c, [(*late_sum, [w_cond1.shape])])
    local_n, local_inv = norm_stats(single)
    single_grad = norm_back(local_n, local_inv, functools.reduce(jnp.add, s_parts))[None]
    grad_w_pair = flat[-HEADS:].T
    grad_gain_z = jnp.sum(wp * grad_w_pair, axis=1) / gz
    small, at = [], 0
    for n in (3 * D, D, 3 * D):
        small.append(flat[at // 128 : (at + n) // 128].reshape(-1))
        at += n
    small = [*small[:2], grad_gain_z, grad_w_pair, small[2]]
    total_bc1, total_bq, total_gz, total_wp, total_bc2 = (
        lax.dynamic_slice_in_dim(g, net.f * v_.shape[0], v_.shape[0], 0)
        for g, v_ in zip(small, [b_cond1, b_q, gain_z, w_pair, b_cond2])
    )
    total_gs1, total_gs2 = (
        jnp.sum(w.astype(f32) * g, axis=1) / gain.astype(f32)
        for w, g, gain in ((w_cond1, total_wc1, gain_s1), (w_cond2, total_wc2, gain_s2))
    )
    return (
        block_out[None],
        place(ids, ags, deps=[gw])[None],
        single_grad,
        pair_grad[None],
        total_gs1,
        total_wc1,
        total_bc1,
        total_wq,
        total_bq,
        total_gz,
        total_wp,
        total_wo,
        total_gs2,
        total_wc2,
        total_bc2,
        total_wab,
        total_wout,
    )


def solution(mesh):
    dp, fsdp = mesh.shape["dp"], mesh.shape["fsdp"]
    split = Mesh(mesh.devices.reshape(dp // 2, 2, fsdp), ("z", "core", "fsdp"))
    return jax.shard_map(
        functools.partial(body, dp, fsdp),
        mesh=split,
        in_specs=(
            P(("z", "core"), None, "fsdp", None),
            P(("z", "core"), "fsdp", None),
            P(("z", "core"), "fsdp", None, None),
            P(("z", "core"), "fsdp"),
            P(("z", "core"), "fsdp"),
            P(("z", "core"), None, "fsdp", None),
            P("fsdp"),
            P("fsdp", None),
            P("fsdp"),
            P("fsdp", None),
            P("fsdp"),
            P("fsdp"),
            P("fsdp", None),
            P("fsdp", None),
            P("fsdp"),
            P("fsdp", None),
            P("fsdp"),
            P("fsdp", None),
            P("fsdp", None),
        ),
        out_specs=(
            P(("z", "core"), None, "fsdp", None),
            P(("z", "core"), None, "fsdp", None),
            P(("z", "core"), "fsdp", None),
            P(("z", "core"), "fsdp", None, None),
            P("fsdp"),
            P("fsdp", None),
            P("fsdp"),
            P("fsdp", None),
            P("fsdp"),
            P("fsdp"),
            P("fsdp", None),
            P("fsdp", None),
            P("fsdp"),
            P("fsdp", None),
            P("fsdp"),
            P("fsdp", None),
            P("fsdp", None),
        ),
        check_vma=False,
    )
```

```python
import functools

import jax
import jax.numpy as jnp
from jax import lax
from jax.experimental import pallas as pl
from jax.experimental.pallas import tpu as pltpu
from jax.sharding import Mesh
from jax.sharding import PartitionSpec as P

HEADS = 16
HEAD = 48
FF = 1536
EPS = 1e-05
LOG2E = 1.4426950408889634
NEG = -1000000000.0
f32 = jnp.float32
bf16 = jnp.bfloat16
NT = (((1,), (1,)), ((), ()))
NN = (((1,), (0,)), ((), ()))
TN = (((0,), (0,)), ((), ()))


def norm_stats(values):
    average = jnp.mean(values, axis=-1, keepdims=True)
    centred = values - average
    inverse = lax.rsqrt(jnp.mean(centred * centred, axis=-1, keepdims=True) + EPS)
    return (centred * inverse, inverse)


def norm_back(normed, inverse, incoming):
    return inverse * (
        incoming
        - jnp.mean(incoming, axis=-1, keepdims=True)
        - normed * jnp.mean(incoming * normed, axis=-1, keepdims=True)
    )


def sig_slope(values):
    sigma_val = jax.nn.sigmoid(values)
    return sigma_val * (1.0 - sigma_val)


def dg(a, b, dims):
    return lax.dot_general(a, b, dims, preferred_element_type=f32)


def cost(flops, nbytes, trans=0):
    return pl.CostEstimate(flops=int(flops), bytes_accessed=int(nbytes), transcendentals=int(trans))


ANY = pl.BlockSpec(memory_space=pl.ANY)


def head_window(h, D):
    tile = jnp.minimum((h * HEAD) // 128, D // 128 - 2)
    return pl.multiple_of(tile * 128, 128), h * HEAD - tile * 128


def masked_bias(F, ids, seg_ref, tag_ref, parts, bm):
    for p in range(F):
        R = parts[p].shape[1]
        row = pl.multiple_of(ids[F + 2 + p] * R, 16)
        bm[pl.ds(row, R), :] = jnp.where(
            seg_ref[pl.ds(row, R), :] == tag_ref[...], parts[p][0].astype(f32) * LOG2E, -jnp.inf
        )


def head_scores(q, k, bm):
    s = dg(q, k, NT)
    return jnp.where(bm > -jnp.inf, s * (HEAD**-0.5 * LOG2E) + bm, NEG * LOG2E)


def attn_fwd_kernel(F, nd, RB, ids, seg_ref, tag_ref, q_ref, k_ref, v_ref, *refs):
    parts = refs[:F]
    o_ref, lse_ref, bm = refs[F + nd :]
    Sl, T, D = q_ref.shape
    h = pl.program_id(0)

    @pl.when(h == 0)
    def _():
        o_ref[...] = jnp.zeros_like(o_ref)
        lse_ref[...] = jnp.zeros_like(lse_ref)

    start, off = head_window(h, D)
    masked_bias(F, ids, seg_ref, tag_ref, parts, bm)
    lane = lax.broadcasted_iota(jnp.int32, (1, 256), 1)
    mine = (lane >= off) & (lane < off + HEAD)
    column = lax.broadcasted_iota(jnp.int32, (1, 128), 1) == h
    win = pl.ds(start, 256)

    def sample(s, _):
        kw = k_ref[s, :, win]
        vw = v_ref[s, :, win]
        vw = jnp.where(mine, vw, jnp.zeros_like(vw))
        for r in range(0, T, RB):
            rows = pl.ds(r, RB)
            qw = q_ref[s, rows, win]
            sc = head_scores(jnp.where(mine, qw, jnp.zeros_like(qw)), kw, bm[rows, :])
            m = jnp.max(sc, axis=-1, keepdims=True)
            p = jnp.exp2(sc - m)
            l = jnp.sum(p, axis=-1, keepdims=True)
            o_ref[s, rows, win] += dg(p.astype(bf16), vw, NN) * (1.0 / l)
            lse_ref[s, rows, :] = jnp.where(column, m + jnp.log2(l), lse_ref[s, rows, :])
        return 0

    lax.fori_loop(0, Sl, sample, 0, unroll=min(Sl, 4))


def resident(shape, last=0):
    at = (0,) * (len(shape) - 1) + (last,)
    return pl.BlockSpec(shape, lambda h, s: at, pipeline_mode=pl.Buffered(1))


def attn_fwd(ids, seg, tag, q, k, v, parts, group, deps=()):
    Sl, T, D = q.shape
    F = len(parts)
    H, R = parts[0].shape[:2]
    W = H * HEAD
    lanes = resident((Sl, T, W), group)
    part = pl.BlockSpec((1, R, T), lambda h, s: (h, 0, 0))
    outs = [jax.ShapeDtypeStruct((Sl, T, W), f32), jax.ShapeDtypeStruct((Sl, T, 128), f32)]
    return pl.pallas_call(
        functools.partial(attn_fwd_kernel, F, len(deps), min(T, 256)),
        grid_spec=pltpu.PrefetchScalarGridSpec(
            num_scalar_prefetch=1,
            grid=(H,),
            in_specs=[resident(seg.shape), resident(tag.shape), lanes, lanes, lanes]
            + [part] * F
            + [ANY] * len(deps),
            out_specs=[resident(x.shape) for x in outs],
            scratch_shapes=[pltpu.VMEM((T, T), f32)],
        ),
        out_shape=outs,
        compiler_params=pltpu.CompilerParams(
            dimension_semantics=("arbitrary",), vmem_limit_bytes=60 << 20
        ),
        cost_estimate=cost(Sl * H * T * T * 3700, Sl * T * W * 10 + H * T * T * 2, Sl * H * T * T),
        name="attn_fwd",
    )(ids, seg, tag, q, k, v, *parts, *deps)


def attn_bwd_kernel(F, nd, RB, ids, seg_ref, tag_ref, q_ref, k_ref, v_ref, do_ref, lse_ref, *refs):
    parts, refs = refs[:F], refs[nd:]
    dq_ref, dk_ref, dv_ref = refs[F : F + 3]
    db_refs = refs[F + 3 : F + 3 + F]
    bm, dbacc, pb, dsb, qt, dot, dkt, dvt = refs[F + 3 + F :]
    Sl, T, D = q_ref.shape
    h = pl.program_id(0)

    @pl.when(h == 0)
    def _():
        dq_ref[...] = jnp.zeros_like(dq_ref)

        def turn(s, _):
            qt[s] = q_ref[s].T
            dot[s] = do_ref[s].T
            return 0

        lax.fori_loop(0, Sl, turn, 0)

    start, off = head_window(h, D)
    masked_bias(F, ids, seg_ref, tag_ref, parts, bm)
    lane = lax.broadcasted_iota(jnp.int32, (1, 256), 1)
    mine = (lane >= off) & (lane < off + HEAD)
    column = lax.broadcasted_iota(jnp.int32, (1, 128), 1) == h
    win = pl.ds(start, 256)
    here = pl.ds(pl.multiple_of(h * HEAD, 16), HEAD)
    root = HEAD**-0.5
    dbacc[...] = jnp.zeros_like(dbacc)

    U = min(Sl, 2)

    def sample(s, u):
        kw = k_ref[s, :, win]
        vw = v_ref[s, :, win]
        km = jnp.where(mine, kw, jnp.zeros_like(kw))
        for r in range(0, T, RB):
            rows = pl.ds(r, RB)
            qw = q_ref[s, rows, win]
            gw = do_ref[s, rows, win]
            sc = head_scores(jnp.where(mine, qw, jnp.zeros_like(qw)), kw, bm[rows, :])
            lse = jnp.sum(
                jnp.where(column, lse_ref[s, rows, :], 0.0), axis=-1, keepdims=True
            )
            p = jnp.exp2(sc - lse)
            dp = dg(jnp.where(mine, gw, jnp.zeros_like(gw)), vw, NT)
            delta = jnp.sum(p * dp, axis=-1, keepdims=True)
            ds = (p * (dp - delta)).astype(bf16)
            pb[u, rows, :] = p.astype(bf16)
            dsb[u, rows, :] = ds
            dbacc[rows, :] += ds.astype(f32)
            dq_ref[s, rows, win] += dg(ds, km, NN) * root
        dvt[s, here, :] = dg(dot[s, here, :], pb[u], NN).astype(bf16)
        dkt[s, here, :] = (dg(qt[s, here, :], dsb[u], NN) * root).astype(bf16)

    def samples(i, _):
        for u in range(U):
            sample(i * U + u, u)
        return 0

    lax.fori_loop(0, Sl // U, samples, 0)
    for p in range(F):
        R = db_refs[p].shape[1]
        row = pl.multiple_of(ids[F + 2 + p] * R, 16)
        db_refs[p][0] = dbacc[pl.ds(row, R), :].astype(bf16)

    @pl.when(h == pl.num_programs(0) - 1)
    def _():
        def turn(s, _):
            dk_ref[s] = dkt[s].T
            dv_ref[s] = dvt[s].T
            return 0

        lax.fori_loop(0, Sl, turn, 0)


def attn_bwd(ids, seg, tag, q, k, v, do, lse, parts, group, deps=()):
    Sl, T, D = q.shape
    F = len(parts)
    H, R = parts[0].shape[:2]
    W = H * HEAD
    lanes = resident((Sl, T, W), group)
    part = pl.BlockSpec((1, R, T), lambda h, s: (h, 0, 0))
    outs = [
        jax.ShapeDtypeStruct((Sl, T, W), f32),
        jax.ShapeDtypeStruct((Sl, T, W), bf16),
        jax.ShapeDtypeStruct((Sl, T, W), bf16),
    ]
    res = pl.pallas_call(
        functools.partial(attn_bwd_kernel, F, len(deps), min(T, 512)),
        grid_spec=pltpu.PrefetchScalarGridSpec(
            num_scalar_prefetch=1,
            grid=(H,),
            in_specs=[resident(seg.shape), resident(tag.shape)]
            + [lanes] * 4
            + [resident(lse.shape)]
            + [part] * F
            + [ANY] * len(deps),
            out_specs=[resident(x.shape) for x in outs] + [part] * F,
            scratch_shapes=[
                pltpu.VMEM((T, T), f32),
                pltpu.VMEM((T, T), f32),
                pltpu.VMEM((2, T, T), bf16),
                pltpu.VMEM((2, T, T), bf16),
                pltpu.VMEM((Sl, W, T), bf16),
                pltpu.VMEM((Sl, W, T), bf16),
                pltpu.VMEM((Sl, W, T), bf16),
                pltpu.VMEM((Sl, W, T), bf16),
            ],
        ),
        out_shape=outs + [jax.ShapeDtypeStruct((H, R, T), bf16)] * F,
        compiler_params=pltpu.CompilerParams(
            dimension_semantics=("arbitrary",), vmem_limit_bytes=63 << 20
        ),
        cost_estimate=cost(Sl * H * T * T * 6200, Sl * T * W * 16 + H * T * T * 4, Sl * H * T * T),
        name="attn_bwd",
    )(ids, seg, tag, q, k, v, do, lse, *parts, *deps)
    return res[0], res[1], res[2], list(res[3:])


def pair_norm(x, ones):
    cen = x.astype(f32) - dg(x, ones, NN)
    inv = lax.rsqrt(dg((cen * cen).astype(bf16), ones, NN) + EPS)
    return cen * inv, inv


def pair_fwd_kernel(U, pair_ref, gain_ref, w_ref, *refs):
    first_ref, second_ref, low = refs[-3:]
    G, T, C = pair_ref.shape
    ones = jnp.full((C, C), 1.0 / C, bf16)

    def rows(i, _):
        x = pair_ref[pl.ds(i * U, U)].reshape(U * T, C)
        n, _ = pair_norm(x, ones)
        y = (n * gain_ref[...]).astype(bf16)
        for u in range(U):
            low[:, pl.ds(pl.multiple_of((i * U + u) * C, 128), C)] = y[u * T : (u + 1) * T]
        return 0

    if U == G:
        rows(0, 0)
    else:
        lax.fori_loop(0, G // U, rows, 0)
    res = dg(w_ref[...], low[...], NT)
    res = res.reshape(res.shape[0] // G, G, T).astype(bf16)
    H = res.shape[0] // 2
    first_ref[...] = res[:H]
    second_ref[...] = res[H:]


def pair_fwd(pair, gain, w_rows, deps=(), U=8):
    R, T, C = pair.shape
    G = 8
    H = w_rows.shape[0] // G
    return pl.pallas_call(
        functools.partial(pair_fwd_kernel, U),
        grid=(R // G,),
        in_specs=[
            pl.BlockSpec((G, T, C), lambda i: (i, 0, 0)),
            pl.BlockSpec((1, C), lambda i: (0, 0)),
            pl.BlockSpec((H * G, G * C), lambda i: (0, 0)),
        ]
        + [ANY] * len(deps),
        out_specs=[pl.BlockSpec((H // 2, G, T), lambda i: (0, i, 0))] * 2,
        out_shape=[jax.ShapeDtypeStruct((H // 2, R, T), bf16)] * 2,
        scratch_shapes=[pltpu.VMEM((T, G * C), bf16)],
        compiler_params=pltpu.CompilerParams(
            dimension_semantics=("arbitrary",), vmem_limit_bytes=40 << 20
        ),
        cost_estimate=cost(R * T * C * 3150, R * T * C * 3, R * T * C),
        name="pair_fwd",
    )(pair, gain, w_rows, *deps)


def pair_bwd_kernel(P, nd, U, pair_ref, gain_ref, wc_ref, *refs):
    firsts, seconds = refs[:P], refs[P : 2 * P]
    out_ref, gw_ref, acc, turned = refs[2 * P + nd :]
    G, T, C = pair_ref.shape
    H = 2 * firsts[0].shape[0]
    ones = jnp.full((C, C), 1.0 / C, bf16)

    @pl.when(pl.program_id(0) == 0)
    def _():
        acc[...] = jnp.zeros_like(acc)

    halves = []
    for parts in (firsts, seconds):
        total = parts[0][...].astype(f32)
        for p in range(1, P):
            total = total + parts[p][...].astype(f32)
        halves.append(total.reshape(H // 2 * G, T))
    flat = jnp.concatenate(halves, axis=0)
    low8 = flat.astype(bf16)
    cols = low8.T
    turned[:, : H * G] = cols
    turned[:, H * G :] = cols

    def rows(i, _):
        x = pair_ref[pl.ds(i * U, U)].reshape(U * T, C)
        n, inv = pair_norm(x, ones)
        low = (n * gain_ref[...]).astype(bf16)
        gs = []
        for u in range(U):
            acc[i * U + u] += dg(low8, low[u * T : (u + 1) * T], NN)
            gs.append(dg(turned[...], wc_ref[i * U + u], NN))
        g = jnp.concatenate(gs, axis=0) if U > 1 else gs[0]
        mean = dg((g * n).astype(bf16), ones, NN)
        out_ref[pl.ds(i * U, U)] = (inv * (g - n * mean)).astype(bf16).reshape(U, T, C)
        return 0

    if U == G:
        rows(0, 0)
    else:
        lax.fori_loop(0, G // U, rows, 0)

    @pl.when(pl.program_id(0) == pl.num_programs(0) - 1)
    def _():
        at = lax.broadcasted_iota(jnp.int32, (H * G, 1), 0) % G
        picked = jnp.zeros((H * G, C), f32)
        for i in range(G):
            picked = picked + jnp.where(at == i, acc[i], 0.0)
        gw_ref[...] = picked


def pair_bwd(pair, gain, wc, firsts, seconds, deps=(), U=8):
    R, T, C = pair.shape
    G = 8
    H = 2 * firsts[0].shape[0]
    P = len(firsts)
    rows = pl.BlockSpec((G, T, C), lambda i: (i, 0, 0))
    return pl.pallas_call(
        functools.partial(pair_bwd_kernel, P, len(deps), U),
        grid=(R // G,),
        in_specs=[
            rows,
            pl.BlockSpec((1, C), lambda i: (0, 0)),
            pl.BlockSpec((G, 2 * H * G, C), lambda i: (0, 0, 0)),
        ]
        + [pl.BlockSpec((H // 2, G, T), lambda i: (0, i, 0))] * (2 * P)
        + [ANY] * len(deps),
        out_specs=[
            rows,
            pl.BlockSpec((H * G, C), lambda i: (0, 0)),
        ],
        out_shape=[
            jax.ShapeDtypeStruct((R, T, C), bf16),
            jax.ShapeDtypeStruct((H * G, C), f32),
        ],
        scratch_shapes=[
            pltpu.VMEM((G, H * G, C), f32),
            pltpu.VMEM((T, 2 * H * G), bf16),
        ],
        compiler_params=pltpu.CompilerParams(
            dimension_semantics=("arbitrary",), vmem_limit_bytes=50 << 20
        ),
        cost_estimate=cost(R * T * C * 5500, R * T * C * 6, R * T * C),
        name="pair_bwd",
    )(pair, gain, wc, *firsts, *seconds, *deps)


def stats_of(x):
    mean = jnp.mean(x, axis=-1, keepdims=True)
    cen = x - mean
    inv = lax.rsqrt(jnp.mean(cen * cen, axis=-1, keepdims=True) + EPS)
    return cen * inv, inv


def sigmoid(x):
    return 1.0 / (1.0 + jnp.exp(-x))


def flat_rows(x):
    return x.reshape(x.shape[0] * x.shape[1], x.shape[2])


def over_samples(x, sb):
    R = x.shape[0] // sb
    total = x[:R]
    for i in range(1, sb):
        total = total + x[i * R : (i + 1) * R]
    return total


def tile_samples(x, sb):
    return x if sb == 1 else jnp.concatenate([x] * sb, axis=0)


def weight_copies(shapes, F, c, f, own, got, swapped, dst, sems):
    copies = []

    def add(src, to):
        copies.append(pltpu.make_async_copy(src, to, sems.at[len(copies)]))

    for i, (r, n) in enumerate(shapes):
        add(own[i], dst[i].at[pl.ds(pl.multiple_of(f * r, 16), r), :])
    for k in range(1, F):
        for packed, half in ((got[k - 1], c), (swapped[k - 1], 1 - c)):
            at = 0
            for i, (r, n) in enumerate(shapes):
                row = pl.multiple_of((f ^ k) * r, 16)
                for b in range(n // 2 // 384):
                    col = pl.multiple_of(half * (n // 2) + b * 384, 128)
                    add(
                        packed.at[pl.ds(at, r), :],
                        dst[i].at[pl.ds(row, r), pl.ds(col, 384)],
                    )
                    at += padded(r)
    return copies


def gathered_copies(shapes, F, c, got, swapped, dst, sems):
    copies = []
    for g in range(F):
        for packed, half in ((got, c), (swapped, 1 - c)):
            at = 0
            for i, (r, n) in enumerate(shapes):
                for b in range(n // 2 // 384):
                    col = pl.multiple_of(half * (n // 2) + b * 384, 128)
                    copies.append(
                        pltpu.make_async_copy(
                            packed.at[g, pl.ds(at, r), :],
                            dst[i].at[pl.ds(g * r, r), pl.ds(col, 384)],
                            sems.at[len(copies)],
                        )
                    )
                    at += padded(r)
    return copies


def padded(r):
    return -(-r // 16) * 16


def packed_rows(shapes):
    return sum(padded(r) * (n // 2 // 384) for r, n in shapes)


def part_map(p, nu):
    return lambda r, u, s: (jnp.where(r == p, u, jnp.where(r < p, 0, nu - 1)), 0, 0)


def part_specs(F, nu, sb, R, D, buffers=2):
    return [
        pl.BlockSpec((sb, R, D), part_map(p, nu), pipeline_mode=pl.Buffered(buffers))
        for p in range(F)
    ]


def arrived_specs(F, nu, sb, R, D):
    specs = part_specs(F, nu, sb, R, D)
    return specs + specs[:1]


def arrivals(parts, ids):
    F = len(parts) - 1
    step = pl.program_id(0)
    own = ids[F] == ids[F + 1] // (F // 2)
    whens = [(step == 0) & ~own] + [step == p for p in range(1, F)] + [(step == 0) & own]
    return zip(whens, parts)


def choose(parts, scratch, ids):
    for when, ref in arrivals(parts, ids):

        @pl.when(when)
        def _(ref=ref):
            scratch[...] = ref[...]

    return flat_rows(scratch[...].astype(f32))


def store_part(parts, value):
    for p, ref in enumerate(parts):

        @pl.when(pl.program_id(0) == p)
        def _(ref=ref):
            ref[...] = value


def copies_in_group(shapes, F):
    return len(shapes) + (F - 1) * 2 * sum(n // 2 // 384 for _, n in shapes)


def pack_grads(shapes, F, c, accs, keep_ref, give_ref, stage=None, sems=None):
    copies = []
    for g in range(F):
        for x in copies:
            x.wait()
        at = 0
        for (r, n), acc in zip(shapes, accs):
            for b in range(n // 2 // 384):
                for i, (ref, half) in enumerate(((keep_ref, c), (give_ref, 1 - c))):
                    col = pl.multiple_of(half * (n // 2) + b * 384, 128)
                    block = acc[g * r : (g + 1) * r, pl.ds(col, 384)].astype(bf16)
                    if stage is None:
                        ref[g, at : at + r, :] = block
                    else:
                        stage[i, at : at + r, :] = block
                at += padded(r)
        if stage is not None:
            copies = [
                pltpu.make_async_copy(stage.at[i], ref.at[g], sems.at[i])
                for i, ref in enumerate((keep_ref, give_ref))
            ]
            for x in copies:
                x.start()
    for x in copies:
        x.wait()


def qkvg_kernel(F, shapes, ids, *refs):
    nin = 2 * (F - 1)
    acts, refs = refs[: F + 1], refs[F + 1 :]
    cond_ref, bq_ref, wq_hbm = refs[:3]
    got, swapped = refs[3 : 3 + F - 1], refs[3 + F - 1 : 3 + nin]
    q_ref, k_ref, v_ref, g_ref, token_ref, w, xs, sems = refs[3 + nin :]
    token_ref[...] = jnp.zeros_like(token_ref)
    c, f = ids[F], ids[F + 1]

    @pl.when((pl.program_id(0) == 0) & (pl.program_id(1) == 0))
    def _():
        copies = weight_copies(shapes, F, c, f, (wq_hbm,), got, swapped, (w,), sems)
        for x in copies:
            x.start()
        for x in copies:
            x.wait()

    sb, R, D = xs.shape
    n, _ = stats_of(choose(acts, xs, ids))
    scale = tile_samples(sigmoid(cond_ref[:, :D]), sb)
    shift = tile_samples(cond_ref[:, D : 2 * D], sb)
    x = (scale * n + shift).astype(bf16)
    q_ref[...] = (dg(x, w[:, :D], NN) + bq_ref[...]).astype(bf16).reshape(sb, R, D)
    k_ref[...] = dg(x, w[:, D : 2 * D], NN).astype(bf16).reshape(sb, R, D)
    v_ref[...] = dg(x, w[:, 2 * D : 3 * D], NN).astype(bf16).reshape(sb, R, D)
    g_ref[0] = sigmoid(dg(x, w[:, 3 * D :], NN)).reshape(sb, R, D)


def sub_samples(sl, R):
    sb = max(1, min(sl, 256 // R))
    return sb, sl // sb


def qkvg_call(ids, acts, cond, bq, wq, got, swapped):
    F = len(acts) - 1
    sl, R, D = acts[0].shape
    T = F * R
    sb, nu = sub_samples(sl, R)
    shapes = [wq.shape]
    stacked = pl.BlockSpec((1, sb, R, D), lambda r, u, s: (r, u, 0, 0))
    natural = pl.BlockSpec((sb, R, D), lambda r, u, s: (u, s[r], 0))
    return pl.pallas_call(
        functools.partial(qkvg_kernel, F, shapes),
        grid_spec=pltpu.PrefetchScalarGridSpec(
            num_scalar_prefetch=1,
            grid=(F, nu),
            in_specs=arrived_specs(F, nu, sb, R, D)
            + [
                pl.BlockSpec((R, 2 * D), lambda r, u, s: (s[r], 0)),
                pl.BlockSpec((1, D), lambda r, u, s: (0, 0)),
            ]
            + [ANY] * (1 + 2 * (F - 1)),
            out_specs=[natural] * 3 + [stacked, pl.BlockSpec((1, 128), lambda r, u, s: (0, 0))],
            scratch_shapes=[
                pltpu.VMEM((D, 4 * D), bf16),
                pltpu.VMEM((sb, R, D), bf16),
                pltpu.SemaphoreType.DMA((copies_in_group(shapes, F),)),
            ],
        ),
        out_shape=[jax.ShapeDtypeStruct((sl, T, D), bf16)] * 3
        + [jax.ShapeDtypeStruct((F, sl, R, D), f32), jax.ShapeDtypeStruct((1, 128), f32)],
        compiler_params=pltpu.CompilerParams(
            dimension_semantics=("arbitrary", "arbitrary"), vmem_limit_bytes=60 << 20
        ),
        cost_estimate=cost(19 * sl * T * D * D, 2 * sl * T * D * 6 + 8 * D * D, sl * T * D),
        name="qkvg",
    )(ids, *acts, cond, bq, wq, *got, *swapped)


def middle_kernel(F, shapes, ids, *refs):
    acts, cots, refs = refs[: F + 1], refs[F + 1 : 2 * F + 2], refs[2 * F + 2 :]
    mix_a, mix_b, gate_ref, gone_ref, ctwo_ref = refs[:5]
    got, swapped = refs[5:7]
    outs, refs = refs[7 : 7 + F], refs[7 + F :]
    (
        da_ref,
        gpg_ref,
        mg_ref,
        ctg_ref,
        gog_ref,
        keep_ref,
        give_ref,
        wo,
        wab,
        wout,
        ao,
        aab,
        aout,
        xs,
        ys,
        stage,
        sems,
        out_sems,
    ) = refs
    c = ids[F]
    first = (pl.program_id(0) == 0) & (pl.program_id(1) == 0)
    last = (pl.program_id(0) == pl.num_programs(0) - 1) & (
        pl.program_id(1) == pl.num_programs(1) - 1
    )

    @pl.when(first)
    def _():
        copies = gathered_copies(shapes, F, c, got, swapped, (wo, wab, wout), sems)
        for x in copies:
            x.start()
        ao[...] = jnp.zeros_like(ao)
        aab[...] = jnp.zeros_like(aab)
        aout[...] = jnp.zeros_like(aout)
        for x in copies:
            x.wait()

    sb, R, D = xs.shape
    H = wout.shape[0]
    gate = flat_rows(gate_ref[0])
    mix = jnp.concatenate([flat_rows(mix_a[...]), flat_rows(mix_b[...])], axis=1)
    branch = (gate * mix).astype(bf16)
    attn_out = dg(branch, wo[...], NN)
    sig_one = sigmoid(gone_ref[...])
    gate_one = tile_samples(sig_one, sb)
    middle = choose(acts, xs, ids) + gate_one * attn_out
    n, inv = stats_of(middle)
    sig_scale = sigmoid(ctwo_ref[:, :D])
    scale = tile_samples(sig_scale, sb)
    x2 = (scale * n + tile_samples(ctwo_ref[:, D : 2 * D], sb)).astype(bf16)
    up = dg(x2, wab[:, H:], NN)
    gp = dg(x2, wab[:, :H], NN)
    sg = sigmoid(gp)
    silu = gp * sg
    hidden = (silu * up).astype(bf16)
    ffn = dg(hidden, wout[...], NN)
    sig_two = sigmoid(ctwo_ref[:, 2 * D :])
    gate_two = tile_samples(sig_two, sb)
    store_part(outs, (middle + gate_two * ffn).astype(bf16).reshape(sb, R, D))

    upstream = choose(cots, ys, ids)
    fg = (upstream * gate_two).astype(bf16)
    g_two = over_samples(upstream * ffn, sb) * (sig_two * (1.0 - sig_two))
    aout[...] += dg(hidden, fg, TN)
    hg = dg(fg, wout[...], NT)
    ga = (hg * up * sg * (1.0 + gp * (1.0 - sg))).astype(bf16)
    gb = (hg * silu).astype(bf16)
    aab[:, :H] += dg(x2, ga, TN)
    aab[:, H:] += dg(x2, gb, TN)
    xg = dg(ga, wab[:, :H], NT) + dg(gb, wab[:, H:], NT)
    g_scale = over_samples(xg * n, sb) * (sig_scale * (1.0 - sig_scale))
    g_shift = over_samples(xg, sb)
    inc = xg * scale
    mg = upstream + inv * (
        inc
        - jnp.mean(inc, axis=-1, keepdims=True)
        - n * jnp.mean(inc * n, axis=-1, keepdims=True)
    )
    mg_ref[0] = mg.reshape(sb, R, D)
    og = (mg * gate_one).astype(bf16)
    g_one = over_samples(mg * attn_out, sb) * (sig_one * (1.0 - sig_one))
    ao[...] += dg(branch, og, TN)
    bg = dg(og, wo[...], NT)
    da_ref[...] = (bg * gate).astype(bf16).reshape(sb, R, D)
    gpg_ref[0] = (bg * mix * (gate * (1.0 - gate))).astype(bf16).reshape(sb, R, D)

    @pl.when(pl.program_id(1) == 0)
    def _():
        ctg_ref[:, :D] = g_scale
        ctg_ref[:, D : 2 * D] = g_shift
        ctg_ref[:, 2 * D :] = g_two
        gog_ref[...] = g_one

    @pl.when(pl.program_id(1) > 0)
    def _():
        ctg_ref[:, :D] += g_scale
        ctg_ref[:, D : 2 * D] += g_shift
        ctg_ref[:, 2 * D :] += g_two
        gog_ref[...] += g_one

    @pl.when(last)
    def _():
        pack_grads(shapes, F, c, (ao, aab, aout), keep_ref, give_ref, stage, out_sems)


def middle_call(ids, acts, cots, mix_a, mix_b, gate, cond_one, cond_two, shapes, got, swapped):
    F = len(acts) - 1
    sl, R, D = acts[0].shape
    T = F * R
    H = shapes[2][0] * F
    sb, nu = sub_samples(sl, R)
    copies = 2 * F * sum(n // 2 // 384 for _, n in shapes)
    rows = packed_rows(shapes)
    stacked = pl.BlockSpec((1, sb, R, D), lambda r, u, s: (r, u, 0, 0))
    natural = pl.BlockSpec((sb, R, D), lambda r, u, s: (u, s[r], 0))
    lanes = pl.BlockSpec((sb, R, D // 2), lambda r, u, s: (u, s[r], 0))
    flops = 12 * sl * T * D * (D + 3 * H)
    res = pl.pallas_call(
        functools.partial(middle_kernel, F, shapes),
        grid_spec=pltpu.PrefetchScalarGridSpec(
            num_scalar_prefetch=1,
            grid=(F, nu),
            in_specs=arrived_specs(F, nu, sb, R, D) * 2
            + [
                lanes,
                lanes,
                stacked,
                pl.BlockSpec((R, D), lambda r, u, s: (s[r], 2)),
                pl.BlockSpec((R, 3 * D), lambda r, u, s: (s[r], 0)),
            ]
            + [ANY] * 2,
            out_specs=part_specs(F, nu, sb, R, D)
            + [
                natural,
                stacked,
                stacked,
                pl.BlockSpec((R, 3 * D), lambda r, u, s: (s[r], 0)),
                pl.BlockSpec((R, D), lambda r, u, s: (s[r], 0)),
                ANY,
                ANY,
            ],
            scratch_shapes=[
                pltpu.VMEM((D, D), bf16),
                pltpu.VMEM((D, 2 * H), bf16),
                pltpu.VMEM((H, D), bf16),
                pltpu.VMEM((D, D), f32),
                pltpu.VMEM((D, 2 * H), f32),
                pltpu.VMEM((H, D), f32),
                pltpu.VMEM((sb, R, D), bf16),
                pltpu.VMEM((sb, R, D), bf16),
                pltpu.VMEM((2, rows, 384), bf16),
                pltpu.SemaphoreType.DMA((copies,)),
                pltpu.SemaphoreType.DMA((2,)),
            ],
        ),
        out_shape=[jax.ShapeDtypeStruct((sl, R, D), bf16)] * F
        + [
            jax.ShapeDtypeStruct((sl, T, D), bf16),
            jax.ShapeDtypeStruct((F, sl, R, D), bf16),
            jax.ShapeDtypeStruct((F, sl, R, D), f32),
            jax.ShapeDtypeStruct((T, 3 * D), f32),
            jax.ShapeDtypeStruct((T, D), f32),
            jax.ShapeDtypeStruct((F, rows, 384), bf16),
            jax.ShapeDtypeStruct((F, rows, 384), bf16),
        ],
        compiler_params=pltpu.CompilerParams(
            dimension_semantics=("arbitrary", "arbitrary"), vmem_limit_bytes=63 << 20
        ),
        cost_estimate=cost(flops, sl * T * D * 24, sl * T * H),
        name="middle",
    )(ids, *acts, *cots, mix_a, mix_b, gate, cond_one, cond_two, got, swapped)
    return list(res[:F]), *res[F:]


def back_weight_kernel(F, nd, shapes, ids, *refs):
    acts, refs = refs[: F + 1], refs[F + 1 :]
    cond_ref, dq_a, dq_b, dk_a, dk_b, dv_a, dv_b, gpg_ref = refs[:8]
    bq_ref, keep_ref, give_ref, acc, xs = refs[8 + nd :]
    D = acts[0].shape[2]
    first = (pl.program_id(0) == 0) & (pl.program_id(1) == 0)
    last = (pl.program_id(0) == pl.num_programs(0) - 1) & (
        pl.program_id(1) == pl.num_programs(1) - 1
    )

    @pl.when(first)
    def _():
        acc[...] = jnp.zeros_like(acc)
        bq_ref[...] = jnp.zeros_like(bq_ref)

    sb = xs.shape[0]
    n, _ = stats_of(choose(acts, xs, ids))
    scale = tile_samples(sigmoid(cond_ref[:, :D]), sb)
    x = (scale * n + tile_samples(cond_ref[:, D : 2 * D], sb)).astype(bf16)
    for i, refs_i in enumerate(((dq_a, dq_b), (dk_a, dk_b), (dv_a, dv_b))):
        g = jnp.concatenate([flat_rows(y[...]) for y in refs_i], axis=1)
        if i == 0:
            bq_ref[...] += jnp.sum(g, axis=0, keepdims=True)
        acc[:, i * D : (i + 1) * D] += dg(x, g.astype(bf16), TN)
    acc[:, 3 * D :] += dg(x, flat_rows(gpg_ref[0]), TN)

    @pl.when(last)
    def _():
        pack_grads(shapes, F, ids[F], (acc,), keep_ref, give_ref)


def back_data_kernel(F, nd, shapes, cshape, ids, *refs):
    nin = 2 * (F - 1)
    acts, refs = refs[: F + 1], refs[F + 1 :]
    cond_ref, dq_a, dq_b, dk_a, dk_b, dv_a, dv_b, gpg_ref, mg_ref = refs[:9]
    s_ref, gog_ref, wc_ref, wq_hbm = refs[9:13]
    got, swapped = refs[13 : 13 + F - 1], refs[13 + F - 1 : 13 + nin]
    ags, refs = refs[13 + nin + nd : 13 + nin + nd + F], refs[13 + nin + nd + F :]
    sg_ref, sum_ref, keep_ref, give_ref, w, cg, acc, xs, sems = refs
    c, f = ids[F], ids[F + 1]
    last = (pl.program_id(0) == pl.num_programs(0) - 1) & (
        pl.program_id(1) == pl.num_programs(1) - 1
    )
    first = (pl.program_id(0) == 0) & (pl.program_id(1) == 0)

    @pl.when(first)
    def _():
        copies = weight_copies(shapes, F, c, f, (wq_hbm,), got, swapped, (w,), sems)
        for x in copies:
            x.start()
        for x in copies:
            x.wait()

    sb, R, D = xs.shape
    n, inv = stats_of(choose(acts, xs, ids))
    sig_scale = sigmoid(cond_ref[:, :D])
    scale = tile_samples(sig_scale, sb)
    xg = dg(flat_rows(gpg_ref[0]), w[:, 3 * D :], NT)
    for i, refs_i in enumerate(((dq_a, dq_b), (dk_a, dk_b), (dv_a, dv_b))):
        g = jnp.concatenate([flat_rows(y[...]) for y in refs_i], axis=1).astype(bf16)
        xg = xg + dg(g, w[:, i * D : (i + 1) * D], NT)
    g_scale = over_samples(xg * n, sb) * (sig_scale * (1.0 - sig_scale))
    g_shift = over_samples(xg, sb)
    inc = xg * scale
    ag = flat_rows(mg_ref[0]) + inv * (
        inc
        - jnp.mean(inc, axis=-1, keepdims=True)
        - n * jnp.mean(inc * n, axis=-1, keepdims=True)
    )
    store_part(ags, ag.astype(bf16).reshape(sb, R, D))

    rows = pl.ds(pl.multiple_of(ids[pl.program_id(0)] * R, 16), R)

    @pl.when(pl.program_id(1) == 0)
    def _():
        cg[rows, :D] = g_scale
        cg[rows, D : 2 * D] = g_shift
        cg[rows, 2 * D :] = gog_ref[rows, :]

    @pl.when(pl.program_id(1) > 0)
    def _():
        cg[rows, :D] += g_scale
        cg[rows, D : 2 * D] += g_shift

    @pl.when(last)
    def _():
        cond_grads(F, cshape, c, s_ref, cg[...], wc_ref, sg_ref, sum_ref, keep_ref, give_ref, acc)


def back_weight(ids, acts, cond, dqkv, gpg, wq_shape, deps=()):
    F = len(acts) - 1
    sl, R, D = acts[0].shape
    T = F * R
    sb, nu = sub_samples(sl, R)
    rows = packed_rows([wq_shape])
    stacked = pl.BlockSpec((1, sb, R, D), lambda r, u, s: (r, u, 0, 0))
    lanes = pl.BlockSpec((sb, R, D // 2), lambda r, u, s: (u, s[r], 0))
    whole = pl.BlockSpec((F, rows, 384), lambda r, u, s: (0, 0, 0), pipeline_mode=pl.Buffered(1))
    return pl.pallas_call(
        functools.partial(back_weight_kernel, F, len(deps), [wq_shape]),
        grid_spec=pltpu.PrefetchScalarGridSpec(
            num_scalar_prefetch=1,
            grid=(F, nu),
            in_specs=arrived_specs(F, nu, sb, R, D)
            + [pl.BlockSpec((R, 2 * D), lambda r, u, s: (s[r], 0))]
            + [lanes] * 6
            + [stacked]
            + [ANY] * len(deps),
            out_specs=[pl.BlockSpec((1, D), lambda r, u, s: (0, 0)), whole, whole],
            scratch_shapes=[pltpu.VMEM((D, 4 * D), f32), pltpu.VMEM((sb, R, D), bf16)],
        ),
        out_shape=[
            jax.ShapeDtypeStruct((1, D), f32),
            jax.ShapeDtypeStruct((F, rows, 384), bf16),
            jax.ShapeDtypeStruct((F, rows, 384), bf16),
        ],
        compiler_params=pltpu.CompilerParams(
            dimension_semantics=("arbitrary", "arbitrary"), vmem_limit_bytes=60 << 20
        ),
        cost_estimate=cost(17 * sl * T * D * D, sl * T * D * 16 + 12 * D * D, sl * T),
        name="back_weight",
    )(ids, *acts, cond, *dqkv, gpg, *deps)


def back_data(ids, acts, cond, dqkv, gpg, mg, s_low, gog, wc, wq, got, swapped, deps=()):
    F = len(acts) - 1
    sl, R, D = acts[0].shape
    T = F * R
    sb, nu = sub_samples(sl, R)
    shapes = [wq.shape]
    C, N = s_low.shape[1], wc.shape[2]
    cshape = (C // F, N)
    crows = packed_rows([cshape])

    def once(shape):
        return pl.BlockSpec(
            shape, lambda r, u, s: (0,) * len(shape), pipeline_mode=pl.Buffered(1)
        )

    outs = [
        jax.ShapeDtypeStruct((T, C), f32),
        jax.ShapeDtypeStruct((1, N), f32),
        jax.ShapeDtypeStruct((F, crows, 384), bf16),
        jax.ShapeDtypeStruct((F, crows, 384), bf16),
    ]
    stacked = pl.BlockSpec((1, sb, R, D), lambda r, u, s: (r, u, 0, 0))
    lanes = pl.BlockSpec((sb, R, D // 2), lambda r, u, s: (u, s[r], 0))
    res = pl.pallas_call(
        functools.partial(back_data_kernel, F, len(deps), shapes, cshape),
        grid_spec=pltpu.PrefetchScalarGridSpec(
            num_scalar_prefetch=1,
            grid=(F, nu),
            in_specs=arrived_specs(F, nu, sb, R, D)
            + [pl.BlockSpec((R, 2 * D), lambda r, u, s: (s[r], 0))]
            + [lanes] * 6
            + [stacked, stacked]
            + [once(x.shape) for x in (s_low, gog, wc)]
            + [ANY] * (1 + 2 * (F - 1) + len(deps)),
            out_specs=part_specs(F, nu, sb, R, D) + [once(x.shape) for x in outs],
            scratch_shapes=[
                pltpu.VMEM((D, 4 * D), bf16),
                pltpu.VMEM((T, N), f32),
                pltpu.VMEM((C, N), f32),
                pltpu.VMEM((sb, R, D), bf16),
                pltpu.SemaphoreType.DMA((copies_in_group(shapes, F),)),
            ],
        ),
        out_shape=[jax.ShapeDtypeStruct((sl, R, D), bf16)] * F + outs,
        compiler_params=pltpu.CompilerParams(
            dimension_semantics=("arbitrary", "arbitrary"), vmem_limit_bytes=60 << 20
        ),
        cost_estimate=cost(17 * sl * T * D * D, sl * T * D * 22 + 8 * D * D, sl * T),
        name="back_data",
    )(ids, *acts, cond, *dqkv, gpg, mg, s_low, gog, wc, wq, *got, *swapped, *deps)
    return list(res[:F]), *res[F:]


def prepare_kernel(F, nd, groups, ids, *refs):
    xs, refs = refs[:F], refs[F:]
    weights = sum(len(g) for g in groups)
    ws, refs = list(refs[:weights]), refs[weights + nd :]
    for x, out in zip(xs, refs):
        out[...] = x[...]

    @pl.when(pl.program_id(0) == 0)
    def _():
        for shapes, packed in zip(groups, refs[F:]):
            at = 0
            for r, n in shapes:
                w = ws.pop(0)
                for b in range(n // 2 // 384):
                    col = pl.multiple_of(ids[F] * (n // 2) + b * 384, 128)
                    packed[at : at + r, :] = w[:, pl.ds(col, 384)]
                    at += padded(r)


def prepare(ids, x, groups=(), deps=()):
    S, R, D = x.shape
    F = (ids.shape[0] - 2) // 3
    sl = S // F
    steps = 4
    shapes = [[w.shape for w in g] for g in groups]
    rows = [packed_rows(s) for s in shapes]

    def group(p):
        return pl.BlockSpec((sl, R // steps, D), lambda i, s: (s[2 * F + 2 + p], i, 0))

    part = pl.BlockSpec((sl, R // steps, D), lambda i, s: (0, i, 0))
    weights = [w for g in groups for w in g]
    res = pl.pallas_call(
        functools.partial(prepare_kernel, F, len(deps), shapes),
        grid_spec=pltpu.PrefetchScalarGridSpec(
            num_scalar_prefetch=1,
            grid=(steps,),
            in_specs=[group(p) for p in range(F)]
            + [pl.BlockSpec(w.shape, lambda i, s: (0, 0)) for w in weights]
            + [ANY] * len(deps),
            out_specs=[part] * F + [pl.BlockSpec((n, 384), lambda i, s: (0, 0)) for n in rows],
        ),
        out_shape=[jax.ShapeDtypeStruct((sl, R, D), x.dtype)] * F
        + [jax.ShapeDtypeStruct((n, 384), bf16) for n in rows],
        compiler_params=pltpu.CompilerParams(
            dimension_semantics=("arbitrary",), vmem_limit_bytes=40 << 20
        ),
        cost_estimate=cost(5e9, S * R * D * 4),
        name="prepare",
    )(ids, *([x] * F), *weights, *deps)
    return list(res[:F]), *res[F:]


def place_kernel(F, ids, *refs):
    out = refs[-1]
    for when, ref in arrivals(refs[: F + 1], ids):

        @pl.when(when)
        def _(ref=ref):
            out[...] = ref[...]


def place(ids, parts, deps=()):
    F = len(parts) - 1
    sl, R, D = parts[0].shape
    fetch = pl.BlockSpec((sl, R, D), lambda i, s: (0, 0, 0), pipeline_mode=pl.Buffered(1))
    return pl.pallas_call(
        functools.partial(place_kernel, F),
        grid_spec=pltpu.PrefetchScalarGridSpec(
            num_scalar_prefetch=1,
            grid=(F,),
            in_specs=[fetch] * (F + 1) + [ANY] * len(deps),
            out_specs=pl.BlockSpec((sl, R, D), lambda i, s: (s[2 * F + 2 + i], 0, 0)),
        ),
        out_shape=jax.ShapeDtypeStruct((F * sl, R, D), parts[0].dtype),
        compiler_params=pltpu.CompilerParams(
            dimension_semantics=("arbitrary",), vmem_limit_bytes=40 << 20
        ),
        cost_estimate=cost(4e9, F * sl * R * D * 4),
        name="place",
    )(ids, *parts, *deps)


def terms_kernel(F, n, ids, *refs):
    outs = refs[-F:]
    for p in range(F):

        @pl.when(pl.program_id(0) == p)
        def _(p=p):
            at = 0
            for own, got in zip(refs[:n], refs[n : 2 * n]):
                rows = own.shape[1]
                outs[p][at : at + rows, :] = (own[0].astype(f32) + got[0].astype(f32)).astype(bf16)
                at += rows


def terms(ids, keeps, gots, deps=()):
    F, _, W = keeps[0].shape
    rows = sum(x.shape[1] for x in keeps)
    shards = [
        pl.BlockSpec((1, x.shape[1], W), lambda k, s: (s[F + 1] ^ k, 0, 0)) for x in keeps
    ]
    out = pl.BlockSpec((rows, W), lambda k, s: (0, 0), pipeline_mode=pl.Buffered(1))
    return pl.pallas_call(
        functools.partial(terms_kernel, F, len(keeps)),
        grid_spec=pltpu.PrefetchScalarGridSpec(
            num_scalar_prefetch=1,
            grid=(F,),
            in_specs=shards * 2 + [ANY] * len(deps),
            out_specs=[out] * F,
        ),
        out_shape=[jax.ShapeDtypeStruct((rows, W), bf16)] * F,
        compiler_params=pltpu.CompilerParams(
            dimension_semantics=("arbitrary",), vmem_limit_bytes=40 << 20
        ),
        cost_estimate=cost(5e9, F * rows * W * 6),
        name="terms",
    )(ids, *keeps, *gots, *deps)


def cond_grads(F, shape, c, s_ref, cg, w_ref, sg_ref, sum_ref, keep_ref, give_ref, acc):
    sum_ref[...] = jnp.sum(cg, axis=0, keepdims=True)
    low = cg.astype(bf16)
    acc[...] = dg(s_ref[...], low, TN)
    r = shape[0]
    sg_ref[...] = jnp.concatenate([dg(low, w_ref[g, :r, :], NT) for g in range(F)], axis=1)
    pack_grads([shape], F, c, (acc,), keep_ref, give_ref)


def cond_back_kernel(F, shape, ids, s_ref, cg_ref, w_ref, *refs):
    sg_ref, sum_ref, keep_ref, give_ref, acc = refs[-5:]
    cond_grads(
        F, shape, ids[F], s_ref, cg_ref[...], w_ref, sg_ref, sum_ref, keep_ref, give_ref, acc
    )


def cond_back(ids, s_low, cg, w, F, deps=()):
    T, C = s_low.shape
    N = cg.shape[1]
    shape = (C // F, N)
    rows = packed_rows([shape])
    vmem = pl.BlockSpec(memory_space=pltpu.VMEM)
    return pl.pallas_call(
        functools.partial(cond_back_kernel, F, shape),
        in_specs=[pl.BlockSpec(memory_space=pltpu.SMEM)] + [vmem] * 3 + [ANY] * len(deps),
        out_specs=[vmem] * 4,
        out_shape=[
            jax.ShapeDtypeStruct((T, C), f32),
            jax.ShapeDtypeStruct((1, N), f32),
            jax.ShapeDtypeStruct((F, rows, 384), bf16),
            jax.ShapeDtypeStruct((F, rows, 384), bf16),
        ],
        scratch_shapes=[pltpu.VMEM((C, N), f32)],
        compiler_params=pltpu.CompilerParams(vmem_limit_bytes=50 << 20),
        cost_estimate=cost(8e9, T * N * 4),
        name="cond_back",
    )(ids, s_low, cg, w, *deps)


def unpack_kernel(groups, ids_c, *refs):
    n = len(groups)
    c = ids_c[0]
    outs = list(refs[2 * n :])
    for i, shapes in enumerate(groups):
        at = 0
        for r, cols in shapes:
            out = outs.pop(0)
            for b in range(cols // 2 // 384):
                for ref, half in ((refs[2 * i], c), (refs[2 * i + 1], 1 - c)):
                    col = pl.multiple_of(half * (cols // 2) + b * 384, 128)
                    out[:, pl.ds(col, 384)] = ref[at : at + r, :].astype(f32)
                at += padded(r)


def unpack(c, groups):
    vmem = pl.BlockSpec(memory_space=pltpu.VMEM)
    shapes = [s for _, _, g in groups for s in g]
    return pl.pallas_call(
        functools.partial(unpack_kernel, [g for _, _, g in groups]),
        in_specs=[pl.BlockSpec(memory_space=pltpu.SMEM)] + [vmem] * (2 * len(groups)),
        out_specs=[vmem] * len(shapes),
        out_shape=[jax.ShapeDtypeStruct(s, f32) for s in shapes],
        compiler_params=pltpu.CompilerParams(vmem_limit_bytes=40 << 20),
        cost_estimate=cost(5e9, sum(r * n for r, n in shapes) * 6),
        name="unpack",
    )(c.reshape(1).astype(jnp.int32), *[x for a, b, _ in groups for x in (a, b)])


def cond_fwd_kernel(F, shape, at, natural, ids, single_ref, gain_ref, bias_ref, *refs):
    r, n = shape
    refs, (s_ref, cond_ref, w) = refs[:-3], refs[-3:]
    c, f = ids[F], ids[F + 1]
    step = padded(r)

    def put(g, packed, half):
        for b in range(n // 2 // 384):
            col = pl.multiple_of(half * (n // 2) + b * 384, 128)
            w[g, :r, pl.ds(col, 384)] = packed(at + b * step)

    if natural:
        for g in range(F):
            for ref, half in zip(refs, (c, 1 - c)):
                put(g, lambda row, ref=ref, g=g: ref[g, row : row + r, :], half)
    else:
        w[f, :r, :] = refs[0][...]
        for k in range(1, F):
            for ref, half in ((refs[k], c), (refs[F - 1 + k], 1 - c)):
                put(f ^ k, lambda row, ref=ref: ref[row : row + r, :], half)
    x, _ = stats_of(single_ref[...])
    s_ref[...] = (x * gain_ref[...]).astype(bf16)
    total = bias_ref[...]
    for g in range(F):
        total = total + dg(s_ref[:, g * r : (g + 1) * r], w[g, :r, :], NN)
    cond_ref[...] = total


def cond_fwd(ids, single, gain, bias, shape, at, arrays, natural):
    T, C = single.shape
    r, n = shape
    F = C // r
    vmem = pl.BlockSpec(memory_space=pltpu.VMEM)
    return pl.pallas_call(
        functools.partial(cond_fwd_kernel, F, shape, at, natural),
        in_specs=[pl.BlockSpec(memory_space=pltpu.SMEM)] + [vmem] * (3 + len(arrays)),
        out_specs=[vmem] * 3,
        out_shape=[
            jax.ShapeDtypeStruct((T, C), bf16),
            jax.ShapeDtypeStruct((T, n), f32),
            jax.ShapeDtypeStruct((F, padded(r), n), bf16),
        ],
        compiler_params=pltpu.CompilerParams(vmem_limit_bytes=60 << 20),
        cost_estimate=cost(6e9, T * n * 4),
        name="cond_fwd",
    )(ids, single, gain, bias, *arrays)


class Net:
    def __init__(self, dp, fsdp):
        self.Z, self.F, self.Fh = dp // 2, fsdp, fsdp // 2
        self.z, self.c = lax.axis_index("z"), lax.axis_index("core")
        self.f = lax.axis_index("fsdp")
        self.fh, self.fl = self.f // self.Fh, self.f % self.Fh
        r = jnp.arange(self.F, dtype=jnp.int32)
        blocks = (self.c ^ (r % 2)) * self.Fh + (self.fl ^ (r // 2))
        rows = ((self.c + r // self.Fh) % 2) * self.Fh + (self.fl ^ (r % self.Fh))
        groups = (self.fl ^ (r // 2)) * 2 + (self.fh ^ (r % 2))
        self.ids = jnp.concatenate(
            [blocks, jnp.stack([self.c, self.f]), rows, groups]
        ).astype(jnp.int32)

    def send(self, x, fn, raw=False):
        F = self.F
        pairs = []
        for z in range(self.Z):
            for c in range(2):
                for f in range(F):
                    z2, c2, f2 = fn(z, c, f)
                    pairs.append(((z * 2 + c) * F + f, (z2 * 2 + c2) * F + f2))
        others = [p for p in pairs if p[0] != p[1]]
        got = lax.ppermute(x, ("z", "core", "fsdp"), others)
        if len(others) == len(pairs) or raw:
            return got
        return jnp.where(self.c == self.fh, x, got)

    def core_swap(self, x):
        return self.send(x, lambda z, c, f: (z, 1 - c, f))

    def to_owner(self, x, a):
        Fh = self.Fh
        return self.send(x, lambda z, c, f: (z, f // Fh, c * Fh + ((f % Fh) ^ a)))

    def exchange_in(self, parts):
        Fh = self.Fh
        return [
            self.send(
                p,
                lambda z, c, f: (z, (f // Fh) ^ (i % 2), c * Fh + ((f % Fh) ^ (i // 2))),
                raw=True,
            )
            for i, p in enumerate(parts)
        ] + [parts[0]]

    def exchange_out(self, parts):
        Fh = self.Fh
        return [
            self.send(
                p,
                lambda z, c, f: (z, f // Fh, (c ^ (i % 2)) * Fh + ((f % Fh) ^ (i // 2))),
                raw=True,
            )
            for i, p in enumerate(parts)
        ] + [parts[0]]

    def gather_rows(self, x):
        return [self.to_owner(x, a) for a in range(self.Fh)]

    def both_cores(self, own):
        return own + [self.core_swap(p) for p in own]

    def chip_sum(self, parts):
        Fh = self.Fh
        out = []
        for a in range(Fh):
            got = self.core_swap(parts[Fh + a])
            out.append((parts[a].astype(f32) + got.astype(f32)).astype(got.dtype))
        return out

    def to_owners(self, parts):
        return [self.to_owner(p, a) for a, p in enumerate(parts)]

    def gather_packed(self, packed, mid, *held):
        F = self.F
        got = [self.send(packed, lambda z, c, f: (z, c, f ^ k)) for k in range(1, F)]
        got[:-1], mid = tie(got[:-1], mid)
        got, *held = tie(got, *held)
        return got, [self.core_swap(g) for g in got], mid, *held

    def plane_send(self, parts):
        return list(parts[:1]) + [
            self.send(parts[k], lambda z, c, f: (z, c, f ^ k)) for k in range(1, self.F)
        ]

    def tree(self, x, count, fn):
        parts = [x] + [
            self.send(x, lambda z, c, f: fn(z, c, f, k)) for k in range(1, count)
        ]
        parts = [p.astype(f32) for p in parts]
        while len(parts) > 1:
            parts = [parts[i] + parts[i + 1] for i in range(0, len(parts), 2)]
        return parts[0].astype(x.dtype)

    def over_z(self, x):
        return self.tree(x, self.Z, lambda z, c, f, k: (z ^ k, c, f))

    def z_steps(self):
        steps, bit = [], 1
        while bit < self.Z:
            fn = lambda z, c, f, bit=bit: (z ^ bit, c, f)
            steps.append(
                lambda x, fn=fn: (x.astype(f32) + self.send(x, fn).astype(f32)).astype(x.dtype)
            )
            bit *= 2
        return steps + [lambda x: (x, self.core_swap(x))]

    def all_steps(self):
        return [
            lambda x: x + self.core_swap(x),
            lambda x: self.tree(x, self.F, lambda z, c, f, k: (z, c, f ^ k)),
            self.over_z,
        ]


def total_of(parts):
    return functools.reduce(jnp.add, [p.astype(f32) for p in parts])


def lockstep(*lanes):
    values = [v for v, _ in lanes]
    for i in range(max(len(steps) for _, steps in lanes)):
        on = [n for n, (_, steps) in enumerate(lanes) if i < len(steps)]
        for n, v in zip(on, tie(*[lanes[n][1][i](values[n]) for n in on])):
            values[n] = v
    return values


def tie(*xs):
    return lax.optimization_barrier(xs)


def body(
    dp,
    fsdp,
    act,
    single,
    pair,
    segment,
    padding,
    cotangent,
    gain_s1,
    w_cond1,
    b_cond1,
    w_qkvg,
    b_q,
    gain_z,
    w_pair,
    w_o,
    gain_s2,
    w_cond2,
    b_cond2,
    w_ab,
    w_out,
):
    net = Net(dp, fsdp)
    F, ids = net.F, net.ids
    act, single, pair, segment, padding, cotangent = (
        x[0] for x in (act, single, pair, segment, padding, cotangent)
    )
    S, R, D = act.shape
    T = R * F
    COND = single.shape[1]

    vecs = [gain_s1, b_cond1, b_q, gain_z, w_pair, gain_s2, b_cond2]
    sizes = [v.size for v in vecs]
    COND = single.shape[1]
    tag = jnp.where(padding == 1, -1, segment)
    flat = jnp.concatenate([x.reshape(-1).astype(f32) for x in (segment, tag, *vecs)])
    vrows = -(-flat.shape[0] // (8 * COND)) * 8
    flat = jnp.pad(flat, (0, vrows * COND - flat.shape[0])).reshape(vrows, COND)
    table = lax.all_gather(jnp.concatenate([single, flat], axis=0), ("core", "fsdp"))
    mid_weights = [w_o, w_ab, w_out, w_cond2]
    mid_shapes = [w.shape for w in mid_weights]
    acts, packed, mid_packed = prepare(ids, act, [[w_qkvg, w_cond1], mid_weights])
    acts = net.exchange_in(acts)
    share = mid_packed.shape[0] // net.Z
    mid_got = lax.dynamic_slice_in_dim(mid_packed, net.z * share, share, 0)
    table = lax.dynamic_slice_in_dim(table, net.fh * F, F, 0)
    smalls = table[:, R:].reshape(F, vrows * COND)

    single_all = table[:, :R].reshape(T, COND)
    seg_col = smalls[:, :R].reshape(T, 1)
    tag_row = smalls[:, R : 2 * R].reshape(1, T)
    full, at = [], 2 * R
    for v, n in zip(vecs, sizes):
        full.append(smalls[:, at : at + n].reshape((F * v.shape[0],) + v.shape[1:]))
        at += n
    gs1, bc1, bq, gz, wp, gs2, bc2 = full

    wt = wp.T
    eye = jnp.eye(8, dtype=f32)
    w_rows = (wt[:, None, None, :] * eye[None, :, :, None]).reshape(HEADS * 8, -1).astype(bf16)
    gz_row = gz.reshape(1, -1)
    bias_a, bias_b = pair_fwd(pair, gz_row, w_rows)
    acts, packed, bias_a, bias_b = tie(acts, packed, bias_a, bias_b)
    one_got, one_swapped, mid_got, bias_a, bias_b = net.gather_packed(
        packed, mid_got, bias_a, bias_b
    )
    mid_got = lax.all_gather(mid_got, ("fsdp", "z")).reshape(F, net.Z * share, 384)
    bias_a, bias_b = net.gather_rows(bias_a), net.gather_rows(bias_b)

    single_first, cond_one, wc1 = cond_fwd(
        ids,
        single_all,
        gs1.reshape(1, -1),
        bc1.reshape(1, -1),
        w_cond1.shape,
        packed_rows([w_qkvg.shape]),
        [w_cond1, *one_got, *one_swapped],
        False,
    )
    q, k, v, gate, token = qkvg_call(
        ids, acts, cond_one, bq.reshape(1, D), w_qkvg, one_got, one_swapped
    )

    cots = prepare(ids, cotangent, deps=[token])[0]
    bias_a, q = tie(bias_a, q)
    bias_a = net.both_cores(bias_a)
    mix_a, lse_a = attn_fwd(ids, seg_col, tag_row, q, k, v, bias_a, 0, deps=cots)
    cots = net.exchange_in(cots)
    mix_a, bias_b = tie(mix_a, bias_b)
    bias_b = net.both_cores(bias_b)
    mix_b, lse_b = attn_fwd(ids, seg_col, tag_row, q, k, v, bias_b, 1)
    mid_got, mix_b, cots = tie(mid_got, mix_b, cots)
    two_got = mid_got[:, packed_rows(mid_shapes[:3]) :]
    two_swapped, mid_swapped = net.core_swap(two_got), net.core_swap(mid_got)
    single_second, cond_two, wc2 = cond_fwd(
        ids,
        single_all,
        gs2.reshape(1, -1),
        bc2.reshape(1, -1),
        w_cond2.shape,
        0,
        [two_got, two_swapped],
        True,
    )
    outs, d_attn, gate_proj, mid_grad, cond_two_grad, gate_one_grad, keep, give = middle_call(
        ids, acts, cots, mix_a, mix_b, gate, cond_one, cond_two, mid_shapes[:3], mid_got, mid_swapped
    )
    outs = net.exchange_out(outs)
    got = net.core_swap(give)
    s_two_grad, grad_b_cond2, keep_c, give_c = cond_back(ids, single_second, cond_two_grad, wc2, F)
    got_c = net.core_swap(give_c)
    mid_sum = []
    for x, y in ((keep, got), (keep_c, got_c)):
        x = (x.astype(f32) + y.astype(f32)).astype(bf16)
        mid_sum.append(jnp.swapaxes(x.reshape(F, net.Z, x.shape[1] // net.Z, 384), 0, 1))
    mid_sum = jnp.concatenate(mid_sum, axis=2)

    dq_a, dk_a, dv_a, db_a = attn_bwd(
        ids, seg_col, tag_row, q, k, v, d_attn, lse_a, bias_a, 0, deps=[mid_sum]
    )
    mid_sum = lax.psum_scatter(mid_sum, "z", scatter_dimension=0)
    outs, db_a = tie(outs, db_a)
    db_a = net.chip_sum(db_a)
    dq_b, dk_b, dv_b, db_b = attn_bwd(
        ids, seg_col, tag_row, q, k, v, d_attn, lse_b, bias_b, 1, deps=db_a
    )
    db_a, db_b, mid_sum = tie(net.to_owners(db_a), db_b, mid_sum)
    db_b = net.chip_sum(db_b)
    mid_sum = net.plane_send(
        [lax.dynamic_index_in_dim(mid_sum, net.f ^ k_, 0, keepdims=False) for k_ in range(F)]
    )
    dqkv = (dq_a, dq_b, dk_a, dk_b, dv_a, dv_b)
    bq_grad, keep, give = back_weight(
        ids, acts, cond_one, dqkv, gate_proj, w_qkvg.shape, deps=db_b
    )
    db_b, give, mid_sum = tie(net.to_owners(db_b), give, mid_sum)
    mid_sum = lax.all_gather(total_of(mid_sum).astype(bf16), "z", axis=0)
    block_out = place(ids, outs, deps=[give])
    wq_parts = terms(ids, [keep], [net.core_swap(give)], deps=[block_out])
    ags, s_one_grad, grad_b_cond1, keep, give = back_data(
        ids,
        acts,
        cond_one,
        dqkv,
        gate_proj,
        mid_grad,
        single_first,
        gate_one_grad,
        wc1,
        w_qkvg,
        one_got,
        one_swapped,
        deps=wq_parts[:1],
    )
    wq_parts, keep, give, ags = tie(net.plane_send(wq_parts), keep, give, ags)
    wq_sum = lax.psum(total_of(wq_parts).astype(bf16), "z")
    late_parts = terms(ids, [keep], [net.core_swap(give)])
    late_parts, ags = tie(late_parts, ags)
    late_send = net.plane_send(late_parts)
    ags = net.exchange_out(ags)

    wc = wt * gz_row
    wc = wc - jnp.mean(wc, axis=1, keepdims=True)
    wc = (wc[None, :, None, :] * eye[:, None, :, None]).reshape(8, HEADS * 8, -1)
    wc_hi = wc.astype(bf16)
    wc = jnp.concatenate([wc_hi, (wc - wc_hi.astype(f32)).astype(bf16)], axis=1)
    pair_grad, gw = pair_bwd(pair, gz_row, wc, db_a, db_b, deps=late_parts[:1])
    late_send, gw, s_one_grad, mid_sum, wq_sum, ags[1:3] = tie(
        late_send, gw, s_one_grad, mid_sum, wq_sum, ags[1:3]
    )

    s_grad = s_one_grad * gs1 + s_two_grad * gs2
    s_parts = [
        lax.dynamic_slice_in_dim(s_grad, ids[F + 2 + p] * R, R, 0) for p in range(F)
    ]
    flat = [grad_b_cond1, bq_grad, grad_b_cond2, jnp.sum(gw.reshape(HEADS, 8, -1), axis=1)]
    flat = jnp.concatenate([g.reshape(-1, 128) for g in flat], axis=0)
    shares = [packed_rows(mid_shapes[:3]) // net.Z, packed_rows(mid_shapes[3:]) // net.Z]
    mid_sum = jnp.concatenate(
        [mid_sum[:, : shares[0]].reshape(-1, 384), mid_sum[:, shares[0] :].reshape(-1, 384)], axis=0
    )
    (
        (total_wo, total_wab, total_wout, total_wc2, total_wq),
        late_sum,
        flat,
        s_parts,
        act_grad,
    ) = lockstep(
        (
            (mid_sum, wq_sum),
            [
                lambda x: [(y, net.core_swap(y)) for y in x],
                lambda x: unpack(net.c, [(*x[0], mid_shapes), (*x[1], [w_qkvg.shape])]),
            ],
        ),
        (total_of(late_send).astype(bf16), net.z_steps()),
        (flat, net.all_steps()),
        (s_parts, [net.chip_sum, net.to_owners]),
        (ags, [lambda x: x, lambda x: place(ids, x)]),
    )
    (total_wc1,) = unpack(net.c, [(*late_sum, [w_cond1.shape])])
    local_n, local_inv = norm_stats(single)
    single_grad = norm_back(local_n, local_inv, functools.reduce(jnp.add, s_parts))[None]
    grad_w_pair = flat[-HEADS:].T
    grad_gain_z = jnp.sum(wp * grad_w_pair, axis=1) / gz
    small, at = [], 0
    for n in (3 * D, D, 3 * D):
        small.append(flat[at // 128 : (at + n) // 128].reshape(-1))
        at += n
    small = [*small[:2], grad_gain_z, grad_w_pair, small[2]]
    total_bc1, total_bq, total_gz, total_wp, total_bc2 = (
        lax.dynamic_slice_in_dim(g, net.f * v_.shape[0], v_.shape[0], 0)
        for g, v_ in zip(small, [b_cond1, b_q, gain_z, w_pair, b_cond2])
    )
    total_gs1, total_gs2 = (
        jnp.sum(w.astype(f32) * g, axis=1) / gain.astype(f32)
        for w, g, gain in ((w_cond1, total_wc1, gain_s1), (w_cond2, total_wc2, gain_s2))
    )
    return (
        block_out[None],
        act_grad[None],
        single_grad,
        pair_grad[None],
        total_gs1,
        total_wc1,
        total_bc1,
        total_wq,
        total_bq,
        total_gz,
        total_wp,
        total_wo,
        total_gs2,
        total_wc2,
        total_bc2,
        total_wab,
        total_wout,
    )


def solution(mesh):
    dp, fsdp = mesh.shape["dp"], mesh.shape["fsdp"]
    split = Mesh(mesh.devices.reshape(dp // 2, 2, fsdp), ("z", "core", "fsdp"))
    return jax.shard_map(
        functools.partial(body, dp, fsdp),
        mesh=split,
        in_specs=(
            P(("z", "core"), None, "fsdp", None),
            P(("z", "core"), "fsdp", None),
            P(("z", "core"), "fsdp", None, None),
            P(("z", "core"), "fsdp"),
            P(("z", "core"), "fsdp"),
            P(("z", "core"), None, "fsdp", None),
            P("fsdp"),
            P("fsdp", None),
            P("fsdp"),
            P("fsdp", None),
            P("fsdp"),
            P("fsdp"),
            P("fsdp", None),
            P("fsdp", None),
            P("fsdp"),
            P("fsdp", None),
            P("fsdp"),
            P("fsdp", None),
            P("fsdp", None),
        ),
        out_specs=(
            P(("z", "core"), None, "fsdp", None),
            P(("z", "core"), None, "fsdp", None),
            P(("z", "core"), "fsdp", None),
            P(("z", "core"), "fsdp", None, None),
            P("fsdp"),
            P("fsdp", None),
            P("fsdp"),
            P("fsdp", None),
            P("fsdp"),
            P("fsdp"),
            P("fsdp", None),
            P("fsdp", None),
            P("fsdp"),
            P("fsdp", None),
            P("fsdp"),
            P("fsdp", None),
            P("fsdp", None),
        ),
        check_vma=False,
    )
```
